256 devices in a mesh: stn: 8 (over x, z_lo), tm: 32 (over z_hi, y, core).
Axes of the slice: x: 4, y: 4, z: 8 (z_hi: 4, z_lo: 2; z = z_hi * 2 + z_lo), core: 2. Of those that a mesh axis runs over, the one named last changes fastest.
Arguments:
- spectra: bfloat16 [16, 8, 128, 2, 4096], P('stn', None, 'tm'), may hold values from -6 to 6
- flags: int32 [16, 8, 128, 32], P('stn', None, 'tm'), may hold values from 0 to 1, as said below
- poly_index: int32 [16, 8, 128], P('stn', None, 'tm'), may hold values from 0 to 63
- delay_model: float32 [64, 3], replicated, may hold values from -48 to 48
- partner_order: int32 [16], replicated, may hold values from 0 to 15, each once
Outputs:
- fringe: float32 [2, 256, 8, 256], P(None, ('stn', 'tm'))
The draws below stay inside these ranges and needn't reach their ends.
Inputs may be any that keep to these rules, and one draw needn't show every extreme that they name: `flags`: 1 marks a flagged block; whole blocks of a station can be flagged for the full window. `partner_order`: each station appears once.
All inputs are finite; a program needn't handle non-finite values.
Results may differ from the reference program's by a relative error of at most 0.003.
Values may be sent and summed in bfloat16 or wider, within the bound.
No kernel may reach another device: no remote copies, remote signals or barrier semaphores. Data moves between devices by JAX's collectives and lax.ppermute only.
A program may use at most 128 MiB of HBM per device.

```python
import math
import jax
import jax.numpy as jnp
from jax import lax

S = 16
C = 4096
P_SIZE = 8
LAGS = 256
NPOLY = 64
SPP = 128
CB = 32


def model_rows(key):
    sign_key = jax.random.fold_in(key, 11)
    size_key = jax.random.fold_in(key, 12)
    mixed_key = jax.random.fold_in(key, 13)
    pick_key = jax.random.fold_in(key, 14)
    signs = jnp.where(jax.random.randint(sign_key, (NPOLY, 1), 0, 2) == 0, -1.0, 1.0).astype(jnp.float32)
    aligned = signs * jax.random.uniform(size_key, (NPOLY, 3), jnp.float32, 16.0, 48.0)
    mixed = jax.random.uniform(mixed_key, (NPOLY, 3), jnp.float32, -48.0, 48.0)
    picked = jax.random.randint(pick_key, (NPOLY, 1), 0, 4) == 0
    return jnp.where(picked, mixed, aligned)


def index_rows(key):
    return jax.random.randint(jax.random.fold_in(key, 21), (S, P_SIZE, SPP), 0, NPOLY).astype(jnp.int32)


def draw_delay_model(key, part):
    return model_rows(key)


def draw_poly_index(key, part):
    return index_rows(key)


def draw_spectra(key, part):
    model = model_rows(key)
    index = index_rows(key)
    coeffs = model[index]
    times = (jnp.arange(P_SIZE, dtype=jnp.int32)[:, None] * SPP + jnp.arange(SPP, dtype=jnp.int32)[None, :]).astype(jnp.float32)
    moment = times / float(P_SIZE * SPP)
    delay = coeffs[..., 0] + coeffs[..., 1] * moment + coeffs[..., 2] * moment * moment
    common = jnp.clip(jax.random.normal(jax.random.fold_in(key, 31), (2, P_SIZE, SPP, C), jnp.float32), -4.5, 4.5)
    offsets = jax.random.randint(jax.random.fold_in(key, 41), (S,), -(C // 6), C // 6 + 1).astype(jnp.int32)
    channel = jnp.arange(C, dtype=jnp.int32)
    freq = channel.astype(jnp.float32) * (math.pi / C)
    gains = jnp.ones((S,), jnp.float32)
    strength = 0.5
    noise_base = jax.random.fold_in(key, 51)

    def one_station(items):
        station, station_delay, offset, gain = items
        noise_key = jax.random.fold_in(noise_base, station)
        noise = jnp.clip(jax.random.normal(noise_key, (P_SIZE, SPP, 2, C), jnp.float32), -4.5, 4.5)
        turns = channel * offset % C
        angle = station_delay[..., None] * freq - turns.astype(jnp.float32) * (2.0 * math.pi / C)
        cosine = jnp.cos(angle)
        sine = jnp.sin(angle)
        real = strength * (common[0] * cosine - common[1] * sine)
        imag = strength * (common[0] * sine + common[1] * cosine)
        signal = jnp.stack([real, imag], axis=2)
        return jnp.clip(gain * noise + signal, -6.0, 6.0)
    stations = lax.map(one_station, (jnp.arange(S, dtype=jnp.int32), delay, offsets, gains))
    return stations.astype(jnp.bfloat16)


def draw_flags(key, part):
    sample_key = jax.random.fold_in(key, 101)
    whole_key = jax.random.fold_in(key, 202)
    shared_key = jax.random.fold_in(key, 303)
    sample = jax.random.randint(sample_key, (S, P_SIZE, SPP, CB), 0, 8) == 0
    whole = jax.random.randint(whole_key, (S, 1, 1, CB), 0, 16) == 0
    shared = jax.random.randint(shared_key, (1, P_SIZE, SPP, CB), 0, 3) == 0
    return jnp.logical_or(jnp.logical_or(sample, whole), shared).astype(jnp.int32)


def setup_inputs(seed: int = 0) -> dict:
    key_of = jax.random.split(jax.random.key(seed), 6)
    return {
        "spectra": draw_spectra(jax.random.fold_in(key_of[5], 71), 0),
        "flags": draw_flags(jax.random.fold_in(key_of[5], 71), 0),
        "poly_index": draw_poly_index(jax.random.fold_in(key_of[5], 71), 0),
        "delay_model": draw_delay_model(jax.random.fold_in(key_of[5], 71), 0),
        "partner_order": jax.random.permutation(key_of[4], S).astype(jnp.int32),
    }


def rotate(spectra, flags, coeffs, times, total_time):
    channels = spectra.shape[-1]
    blocks = flags.shape[-1]
    moment = times / total_time
    delay = coeffs[..., 0] + coeffs[..., 1] * moment + coeffs[..., 2] * moment * moment
    freq = jnp.arange(channels, dtype=jnp.int32).astype(jnp.float32) * (math.pi / channels)
    phase = delay[..., None] * freq
    cosine = jnp.cos(phase)
    sine = jnp.sin(phase)
    real = spectra[..., 0, :].astype(jnp.float32)
    imag = spectra[..., 1, :].astype(jnp.float32)
    weight = 1.0 - flags.astype(jnp.float32)
    weight = jnp.broadcast_to(weight[..., None], weight.shape + (channels // blocks,)).reshape(real.shape)
    new_real = weight * (real * cosine + imag * sine)
    new_imag = weight * (imag * cosine - real * sine)
    return jnp.stack([new_real, new_imag], axis=-2).astype(jnp.bfloat16)

def transform(vis, counts, lags):
    rows, periods, _, channels = vis.shape
    blocks = counts.shape[-1]
    scale = 1.0 / jnp.sqrt(jnp.maximum(counts, 1.0))
    normed = vis.reshape(rows, periods, 2, blocks, channels // blocks) * scale[:, :, None, :, None]
    normed = normed.reshape(rows, periods, 2, channels)
    index = jnp.arange(lags, dtype=jnp.int32)
    middle = lags // 2
    delays = jnp.where(index < middle, index - middle, index - middle + 1)
    turns = jnp.arange(channels, dtype=jnp.int32)[:, None] * delays[None, :] % channels
    angle = turns.astype(jnp.float32) * (2.0 * math.pi / channels)
    cosine = jnp.cos(angle)
    sine = jnp.sin(angle)
    highest = lax.Precision.HIGHEST
    real = normed[:, :, 0].reshape(rows * periods, channels)
    imag = normed[:, :, 1].reshape(rows * periods, channels)
    part_real = jnp.dot(real, cosine, precision=highest) + jnp.dot(imag, sine, precision=highest)
    part_imag = jnp.dot(imag, cosine, precision=highest) - jnp.dot(real, sine, precision=highest)
    part_real = part_real.reshape(rows, periods, lags)
    part_imag = part_imag.reshape(rows, periods, lags)
    pidx = jnp.arange(periods, dtype=jnp.int32)
    pturn = pidx[:, None] * pidx[None, :] % periods
    pangle = pturn.astype(jnp.float32) * (2.0 * math.pi / periods)
    pcos = jnp.cos(pangle)
    psin = jnp.sin(pangle)
    out_real = jnp.einsum('rp,npl->nrl', pcos, part_real, precision=highest) + jnp.einsum('rp,npl->nrl', psin, part_imag, precision=highest)
    out_imag = jnp.einsum('rp,npl->nrl', pcos, part_imag, precision=highest) - jnp.einsum('rp,npl->nrl', psin, part_real, precision=highest)
    factor = 1.0 / math.sqrt(periods * channels)
    return jnp.stack([out_real, out_imag]) * factor

def reference(spectra, flags, poly_index, delay_model, partner_order):
    stations, periods, depth, _, channels = spectra.shape
    times = (jnp.arange(periods, dtype=jnp.int32)[:, None] * depth + jnp.arange(depth, dtype=jnp.int32)[None, :]).astype(jnp.float32)
    total_time = float(periods * depth)

    def one_station(items):
        spectrum, flag, index = items
        coeffs = delay_model[index]
        return rotate(spectrum[None], flag[None], coeffs[None], times, total_time)[0]
    rotated = lax.map(one_station, (spectra, flags, poly_index))
    wide = rotated.astype(jnp.float32)

    def one_row(mine):
        product = jnp.einsum('pkxc,bpkyc->bpxyc', mine.astype(jnp.float32), wide)
        real = product[:, :, 0, 0] + product[:, :, 1, 1]
        imag = product[:, :, 1, 0] - product[:, :, 0, 1]
        return jnp.stack([real, imag], axis=2)
    vis = lax.map(one_row, rotated)
    weight = 1.0 - flags.astype(jnp.float32)
    counts = jnp.einsum('apkx,bpkx->abpx', weight, weight, precision=lax.Precision.HIGHEST)
    vis = jnp.take(vis, partner_order, axis=1).reshape(stations * stations, periods, 2, channels)
    counts = jnp.take(counts, partner_order, axis=1).reshape(stations * stations, periods, counts.shape[-1])
    return transform(vis, counts, LAGS)
```

```python
import math

import jax
import jax.numpy as jnp
import numpy as np
from jax import lax
from jax.experimental import pallas as pl
from jax.experimental.pallas import tpu as pltpu
from jax.sharding import PartitionSpec as P

S = 16
C = 4096
PERIODS = 8
LAGS = 256
SPP = 128
CB = 32
STN = 8
TM = 32
K = 4
ROWS = 24
LANES = 128
HALF = LAGS // 2
HIGHEST = lax.Precision.HIGHEST


def rows_of(shape):
    return lax.broadcasted_iota(jnp.int32, shape, len(shape) - 2)


def lanes_of(shape):
    return lax.broadcasted_iota(jnp.int32, shape, len(shape) - 1)


def rotate_kernel(first_ref, poly_ref, model_ref, flags_ref, x_ref, out_ref):
    p = pl.program_id(0)
    row = rows_of((8, LANES))
    even = row % 2 == 0
    which = row // 2
    lane = lanes_of((8, LANES)).astype(jnp.float32)
    sign = jnp.where(even, 1.0, -1.0)
    for s in range(2):
        delay = jnp.zeros((8, LANES), jnp.float32)
        weight = jnp.zeros((8, CB), jnp.float32)
        for k in range(K):
            index = poly_ref[s, p, k]
            time = p * SPP + first_ref[0] + k
            moment = time.astype(jnp.float32) * (1.0 / (PERIODS * SPP))
            value = (
                model_ref[index, 0]
                + model_ref[index, 1] * moment
                + model_ref[index, 2] * moment * moment
            )
            delay = jnp.where(which == k, value, delay)
            flag = flags_ref[s, 0, k : k + 1, :].astype(jnp.float32)
            weight = jnp.where(
                which[:, :CB] == k, jnp.broadcast_to(1.0 - flag, (8, CB)), weight
            )
        fine = delay * (lane * (math.pi / C))
        fine_cos = jnp.cos(fine)
        fine_sin = jnp.sin(fine)
        signed_cos = sign * fine_cos
        signed_sin = sign * fine_sin
        coarse = delay[:, :CB] * (lane[:, :CB] * (math.pi * LANES / C))
        coarse_cos = weight * jnp.cos(coarse)
        coarse_sin = weight * jnp.sin(coarse)
        for q in range(CB):
            x = x_ref[s, 0, :, q * LANES : (q + 1) * LANES].astype(jnp.float32)
            a_cos = jnp.broadcast_to(coarse_cos[:, q : q + 1], (8, LANES))
            a_sin = jnp.broadcast_to(coarse_sin[:, q : q + 1], (8, LANES))
            cosine = a_cos * fine_cos - a_sin * fine_sin
            sine = a_sin * signed_cos + a_cos * signed_sin
            other = jnp.where(even, pltpu.roll(x, 7, 0), pltpu.roll(x, 1, 0))
            turned = x * cosine + other * sine
            out_ref[q, s * 8 : s * 8 + 8, :] = turned.astype(jnp.bfloat16)
    for q in range(CB):
        tile = jnp.zeros((8, LANES), jnp.float32)
        for s in range(2):
            for k in range(K):
                flag = flags_ref[s, 0, k : k + 1, q : q + 1].astype(jnp.float32)
                tile = jnp.where(
                    row == s * K + k, jnp.broadcast_to(1.0 - flag, (8, LANES)), tile
                )
        out_ref[q, 16:24, :] = tile.astype(jnp.bfloat16)


def rotated_chunks(spectra, flags, poly_index, delay_model, first):
    tiles = spectra.reshape(2, PERIODS, 2 * K, C)
    return pl.pallas_call(
        rotate_kernel,
        grid=(PERIODS,),
        in_specs=[
            pl.BlockSpec(memory_space=pltpu.SMEM),
            pl.BlockSpec(memory_space=pltpu.SMEM),
            pl.BlockSpec(memory_space=pltpu.SMEM),
            pl.BlockSpec((2, 1, K, CB), lambda p: (0, p, 0, 0)),
            pl.BlockSpec((2, 1, 2 * K, C), lambda p: (0, p, 0, 0)),
        ],
        out_specs=pl.BlockSpec((CB, ROWS, LANES), lambda p: (p, 0, 0)),
        out_shape=jax.ShapeDtypeStruct((PERIODS * CB, ROWS, LANES), jnp.bfloat16),
        name="rotate",
    )(first, poly_index, delay_model, flags, tiles)


def row_sums(values):
    row = rows_of((8, LANES))
    upper = row < 4
    stage = [
        jnp.where(upper, values[i], values[i + 4])
        + pltpu.roll(jnp.where(upper, values[i + 4], values[i]), 4, 0)
        for i in range(4)
    ]
    for distance in (2, 1):
        first = row % (2 * distance) < distance
        stage = [
            jnp.where(first, stage[i], stage[i + distance])
            + jnp.where(
                first,
                pltpu.roll(stage[i], 8 - distance, 0),
                pltpu.roll(stage[i + distance], distance, 0),
            )
            for i in range(distance)
        ]
    return stage[0]


def correlate_kernel(order_ref, y_ref, out_ref, wide, turned, weights, scales, held):
    row = rows_of((8, LANES))
    even = row % 2 == 0
    lane = lanes_of((8, LANES))

    def unpack(t, carry):
        total = jnp.zeros((8, LANES), jnp.float32)
        for n in range(STN):
            for s in range(2):
                x = y_ref[n, t, s * 8 : s * 8 + 8, :].astype(jnp.float32)
                wide[2 * n + s, t] = x
                turned[2 * n + s, t] = jnp.where(
                    even, -pltpu.roll(x, 7, 0), pltpu.roll(x, 1, 0)
                )
            w = y_ref[n, t, 16:24, :].astype(jnp.float32)
            total = jnp.where(lane // 8 == 2 * n, w, total)
            total = jnp.where(lane // 8 == 2 * n + 1, pltpu.roll(w, 4, 0), total)
        weights[pl.ds(pl.multiple_of(t * 8, 8), 8), :] = jnp.where(row < K, total, 0.0)
        return carry

    lax.fori_loop(0, TM, unpack, 0)
    counts = lax.dot_general(
        weights[...].astype(jnp.bfloat16),
        weights[...].astype(jnp.bfloat16),
        (((0,), (0,)), ((), ())),
        preferred_element_type=jnp.float32,
    )
    scales[...] = 1.0 / jnp.sqrt(jnp.maximum(counts, 1.0))

    def place(b, block, tile):
        rows = jnp.concatenate(
            [scales[8 * (4 * block + i) : 8 * (4 * block + i) + 2, :] for i in range(4)]
        )
        held[b, block] = tile * jnp.broadcast_to(rows[:, 8 * b : 8 * b + 1], (8, LANES))

    for block_a in range(4):
        for block_b in range(block_a, 4):
            pairs = [
                (i, j)
                for i in range(4)
                for j in range(4)
                if block_a != block_b or i <= j
            ]

            def add(t, sums, block_a=block_a, block_b=block_b, pairs=pairs):
                mine = [wide[4 * block_a + i, t] for i in range(4)]
                theirs = [wide[4 * block_b + j, t] for j in range(4)]
                crossed = [turned[4 * block_b + j, t] for j in range(4)]
                return tuple(
                    (re + mine[i] * theirs[j], im + mine[i] * crossed[j])
                    for (re, im), (i, j) in zip(sums, pairs)
                )

            zero = jnp.zeros((8, LANES), jnp.float32)
            sums = lax.fori_loop(0, TM, add, tuple((zero, zero) for _ in pairs))
            vis = dict(zip(pairs, sums))
            if block_a == block_b:
                for i in range(4):
                    vis[i, i] = (vis[i, i][0], zero)
                    for j in range(i):
                        vis[i, j] = (vis[j, i][0], -vis[j, i][1])
            for j in range(4):
                place(
                    4 * block_b + j,
                    block_a,
                    row_sums([vis[i, j][part] for i in range(4) for part in range(2)]),
                )
            if block_a != block_b:
                for i in range(4):
                    place(
                        4 * block_a + i,
                        block_b,
                        row_sums(
                            [
                                vis[i, j][part] if part == 0 else -vis[i, j][part]
                                for j in range(4)
                                for part in range(2)
                            ]
                        ),
                    )
    for j in range(S):
        b = order_ref[j]
        for block in range(4):
            tile = held[b, block]
            for i in range(4):
                out_ref[(4 * block + i) * S + j] = tile[2 * i : 2 * i + 2, :]


def correlated(order, arrived):
    return pl.pallas_call(
        correlate_kernel,
        in_specs=[
            pl.BlockSpec(memory_space=pltpu.SMEM),
            pl.BlockSpec(memory_space=pltpu.VMEM),
        ],
        out_specs=pl.BlockSpec(memory_space=pltpu.VMEM),
        out_shape=jax.ShapeDtypeStruct((S * S, 2, LANES), jnp.float32),
        scratch_shapes=[
            pltpu.VMEM((S, TM, 8, LANES), jnp.float32),
            pltpu.VMEM((S, TM, 8, LANES), jnp.float32),
            pltpu.VMEM((TM * 8, LANES), jnp.float32),
            pltpu.VMEM((LANES, LANES), jnp.float32),
            pltpu.VMEM((S, 4, 8, LANES), jnp.float32),
        ],
        compiler_params=pltpu.CompilerParams(vmem_limit_bytes=32 * 2**20),
        name="correlate",
    )(order, arrived.reshape(STN, TM, ROWS, LANES))


def fringe_tables():
    lag = np.arange(1, HALF + 1)
    fine = 2.0 * np.pi * ((np.arange(LANES)[:, None] * lag) % C) / C
    coarse = 2.0 * np.pi * ((np.arange(CB)[:, None] * lag) % CB) / CB
    period = 2.0 * np.pi * ((np.arange(PERIODS)[:, None] * np.arange(PERIODS)) % PERIODS)
    period = period / PERIODS
    factor = 1.0 / math.sqrt(PERIODS * C)
    flip = np.eye(HALF)[::-1]
    return [
        np.ascontiguousarray(table, np.float32)
        for table in (
            np.concatenate([np.cos(fine), np.sin(fine)], axis=1),
            np.stack([np.cos(coarse), np.sin(coarse)]),
            np.stack([np.cos(period), np.sin(period)]) * factor,
            flip,
        )
    ]


def fringe_kernel(z_ref, fine_ref, coarse_ref, period_ref, flip_ref, out_ref):
    fine = fine_ref[...]
    re = jnp.dot(z_ref[0], fine, precision=HIGHEST, preferred_element_type=jnp.float32)
    im = jnp.dot(z_ref[1], fine, precision=HIGHEST, preferred_element_type=jnp.float32)
    parts = [[], [], [], []]
    for p in range(PERIODS):
        sums = [jnp.zeros((8, LANES), jnp.float32)] * 4
        for g in range(CB // 8):
            at = slice(p * CB + g * 8, p * CB + g * 8 + 8)
            re_cos, re_sin = re[at, :HALF], re[at, HALF:]
            im_cos, im_sin = im[at, :HALF], im[at, HALF:]
            cosine = coarse_ref[0, g * 8 : g * 8 + 8, :]
            sine = coarse_ref[1, g * 8 : g * 8 + 8, :]
            plus_re, plus_im = re_cos + im_sin, im_cos - re_sin
            minus_re, minus_im = re_cos - im_sin, im_cos + re_sin
            terms = (
                cosine * minus_re - sine * minus_im,
                cosine * minus_im + sine * minus_re,
                cosine * plus_re + sine * plus_im,
                cosine * plus_im - sine * plus_re,
            )
            sums = [total + term for total, term in zip(sums, terms)]
        for part, total in zip(parts, sums):
            part.append(total)
    minus_re, minus_im, plus_re, plus_im = (row_sums(part) for part in parts)
    reversed_ = jnp.dot(
        jnp.concatenate([minus_re, minus_im]),
        flip_ref[...],
        precision=HIGHEST,
        preferred_element_type=jnp.float32,
    )
    real = jnp.concatenate([reversed_[:8], plus_re], axis=1)
    imag = jnp.concatenate([reversed_[8:], plus_im], axis=1)
    cosine, sine = period_ref[0], period_ref[1]

    def turn(a, b):
        return jnp.dot(a, b, precision=HIGHEST, preferred_element_type=jnp.float32)

    out_ref[0, 0] = turn(cosine, real) + turn(sine, imag)
    out_ref[1, 0] = turn(cosine, imag) - turn(sine, real)


def fringed(normed):
    return pl.pallas_call(
        fringe_kernel,
        in_specs=[pl.BlockSpec(memory_space=pltpu.VMEM)] * 5,
        out_specs=pl.BlockSpec(memory_space=pltpu.VMEM),
        out_shape=jax.ShapeDtypeStruct((2, 1, PERIODS, LAGS), jnp.float32),
        compiler_params=pltpu.CompilerParams(vmem_limit_bytes=32 * 2**20),
        name="fringe",
    )(normed, *fringe_tables())


def per_device(spectra, flags, poly_index, delay_model, partner_order):
    axes = ("stn", "tm")
    first = (lax.axis_index("tm") * K).astype(jnp.int32).reshape(1)
    chunks = rotated_chunks(spectra, flags, poly_index, delay_model, first)
    arrived = lax.all_to_all(chunks, axes, split_axis=0, concat_axis=0, tiled=True)
    rows = correlated(partner_order, arrived)
    owned = lax.all_to_all(rows, axes, split_axis=0, concat_axis=0, tiled=True)
    return fringed(jnp.moveaxis(owned, 1, 0))


def solution(mesh):
    return jax.shard_map(
        per_device,
        mesh=mesh,
        in_specs=(
            P("stn", None, "tm", None, None),
            P("stn", None, "tm", None),
            P("stn", None, "tm"),
            P(),
            P(),
        ),
        out_specs=P(None, ("stn", "tm"), None, None),
        check_vma=False,
    )
```

```python
import math

import jax
import jax.numpy as jnp
import numpy as np
from jax import lax
from jax.experimental import pallas as pl
from jax.experimental.pallas import tpu as pltpu
from jax.sharding import PartitionSpec as P

S = 16
C = 4096
PERIODS = 8
LAGS = 256
SPP = 128
CB = 32
STN = 8
TM = 32
K = 4
SPECTRA = 2 * K
LANES = 128
HALF = LAGS // 2
HIGHEST = lax.Precision.HIGHEST


def rows_of(shape):
    return lax.broadcasted_iota(jnp.int32, shape, len(shape) - 2)


def lanes_of(shape):
    return lax.broadcasted_iota(jnp.int32, shape, len(shape) - 1)


def rotate_kernel(first_ref, poly_ref, model_ref, flags_ref, x_hbm, out_ref, x_ref, turned_re, turned_im, sems):
    def fetch(p):
        return pltpu.make_async_copy(x_hbm.at[:, p], x_ref.at[p], sems.at[p])

    for p in range(PERIODS):
        fetch(p).start()
    row = rows_of((8, LANES))
    lane = lanes_of((8, LANES))
    across = jnp.zeros((8, LANES), jnp.float32)
    down = []
    for p in range(PERIODS):
        column = jnp.zeros((8, LANES), jnp.float32)
        for s in range(2):
            for k in range(K):
                index = poly_ref[s, k, p]
                time = p * SPP + first_ref[0] + k
                moment = time.astype(jnp.float32) * (1.0 / (PERIODS * SPP))
                delay = (
                    model_ref[0, index]
                    + model_ref[1, index] * moment
                    + model_ref[2, index] * moment * moment
                )
                column = jnp.where(row == s * K + k, delay, column)
                across = jnp.where(lane == p * SPECTRA + s * K + k, delay, across)
        down.append(column)
    fine = [d * (lane.astype(jnp.float32) * (math.pi / C)) for d in down]
    fine_cos = [jnp.cos(f) for f in fine]
    fine_sin = [jnp.sin(f) for f in fine]
    weight = 1.0 - flags_ref[...].reshape(2 * PERIODS * K, CB).astype(jnp.float32)
    weight = weight.astype(jnp.bfloat16)
    source = rows_of((2 * PERIODS * K, LANES))
    source_s, source_p, source_k = source // (PERIODS * K), source // K % PERIODS, source % K
    target = lanes_of((2 * PERIODS * K, LANES))

    def spread(chosen):
        return lax.dot_general(
            weight,
            chosen.astype(jnp.bfloat16),
            (((0,), (0,)), ((), ())),
            preferred_element_type=jnp.float32,
        )

    spectrum = source_s * K + source_k
    coarse_weight = spread(
        jnp.where(target == source_p * SPECTRA + spectrum, 1.0, 0.0)
    )
    block = rows_of((CB, LANES)).astype(jnp.float32)
    coarse = jnp.tile(across, (CB // 8, 1)) * (block * (math.pi * LANES / C))
    coarse_cos = coarse_weight * jnp.cos(coarse)
    coarse_sin = coarse_weight * jnp.sin(coarse)
    for p in range(PERIODS):
        mark = jnp.where((source_p == p) & (target % SPECTRA == spectrum), 1.0, 0.0)
        sent = spread(mark).astype(jnp.bfloat16)
        fetch(p).wait()
        for s in range(2):
            for k in range(K):
                r = s * K + k
                x = x_ref[p, s, k].astype(jnp.float32)
                re = x[0:1].reshape(CB, LANES)
                im = x[1:2].reshape(CB, LANES)
                at = p * SPECTRA + r
                a_cos = jnp.broadcast_to(coarse_cos[:, at : at + 1], (CB, LANES))
                a_sin = jnp.broadcast_to(coarse_sin[:, at : at + 1], (CB, LANES))
                b_cos = jnp.broadcast_to(fine_cos[p][r : r + 1], (CB, LANES))
                b_sin = jnp.broadcast_to(fine_sin[p][r : r + 1], (CB, LANES))
                cosine = a_cos * b_cos - a_sin * b_sin
                sine = a_sin * b_cos + a_cos * b_sin
                turned_re[p % 2, pl.ds(r, CB, stride=SPECTRA), :] = re * cosine + im * sine
                turned_im[p % 2, pl.ds(r, CB, stride=SPECTRA), :] = im * cosine - re * sine
        for q in range(CB):
            at = slice(q * SPECTRA, (q + 1) * SPECTRA)
            both = jnp.concatenate([turned_re[p % 2, at], turned_im[p % 2, at]])
            out_ref[p * CB + q, 0:SPECTRA] = both.astype(jnp.bfloat16).reshape(SPECTRA, 2, LANES)
        out_ref[p * CB : (p + 1) * CB, SPECTRA] = jnp.broadcast_to(
            sent[:, None, :], (CB, 2, LANES)
        )


def rotated_chunks(spectra, flags, poly_index, delay_model, first):
    return pl.pallas_call(
        rotate_kernel,
        in_specs=[
            pl.BlockSpec(memory_space=pltpu.SMEM),
            pl.BlockSpec(memory_space=pltpu.SMEM),
            pl.BlockSpec(memory_space=pltpu.SMEM),
            pl.BlockSpec(memory_space=pltpu.VMEM),
            pl.BlockSpec(memory_space=pltpu.HBM),
        ],
        out_specs=pl.BlockSpec(memory_space=pltpu.VMEM),
        out_shape=jax.ShapeDtypeStruct((PERIODS * CB, SPECTRA + 1, 2, LANES), jnp.bfloat16),
        scratch_shapes=[
            pltpu.VMEM((PERIODS, 2, K, 2, C), jnp.bfloat16),
            pltpu.VMEM((2, CB * SPECTRA, LANES), jnp.float32),
            pltpu.VMEM((2, CB * SPECTRA, LANES), jnp.float32),
            pltpu.SemaphoreType.DMA((PERIODS,)),
        ],
        compiler_params=pltpu.CompilerParams(vmem_limit_bytes=32 * 2**20),
        name="rotate",
    )(first, poly_index.transpose(0, 2, 1), delay_model.T, flags, spectra)


def group_sums(values, group):
    row = rows_of((8, LANES))
    stage = list(values)
    distance = group // 2
    while distance:
        first = row % (2 * distance) < distance
        if 2 * distance == 8:
            stage = [
                jnp.where(first, stage[i], stage[i + distance])
                + pltpu.roll(jnp.where(first, stage[i + distance], stage[i]), 4, 0)
                for i in range(distance)
            ]
        else:
            stage = [
                jnp.where(first, stage[i], stage[i + distance])
                + jnp.where(
                    first,
                    pltpu.roll(stage[i], 8 - distance, 0),
                    pltpu.roll(stage[i + distance], distance, 0),
                )
                for i in range(distance)
            ]
        distance //= 2
    return stage[0]


def pair_scales(y_ref):
    lane = lanes_of((TM, LANES))
    seen = jnp.zeros((TM, LANES), jnp.float32)
    for n in range(STN):
        seen = jnp.where(
            lane // SPECTRA == n, y_ref[n, :, SPECTRA].astype(jnp.float32)[:, 0, :], seen
        )
    seen = seen.astype(jnp.bfloat16)
    together = lax.dot_general(
        seen, seen, (((0,), (0,)), ((), ())), preferred_element_type=jnp.float32
    )
    i, j = rows_of((LANES, LANES)), lanes_of((LANES, LANES))
    together = jnp.where(i % K == j % K, together, 0.0).astype(jnp.bfloat16)
    partner = jnp.where(i // K == j, 1.0, 0.0).astype(jnp.bfloat16)
    summed = jnp.dot(together, partner, preferred_element_type=jnp.float32)
    a, b = rows_of((STN * 8, LANES)), lanes_of((STN * 8, LANES))
    station = jnp.where(a // 4 == b // K, 1.0, 0.0).astype(jnp.bfloat16)
    counts = jnp.dot(
        station, summed.astype(jnp.bfloat16), preferred_element_type=jnp.float32
    )
    return 1.0 / jnp.sqrt(jnp.maximum(counts, 1.0))


def correlate_kernel(order_ref, y_ref, out_ref, mine_ref, theirs_ref, crossed_ref, scales, place_ref):
    for j in range(S):
        place_ref[order_ref[j]] = j
    row = rows_of((8, LANES))
    scales[...] = pair_scales(y_ref)

    def unpack(t, carry):
        for n in range(STN):
            x = y_ref[n, t, 0:SPECTRA].reshape(2 * SPECTRA, LANES).astype(jnp.float32)
            re, im = x[:SPECTRA], x[SPECTRA:]
            total, gap = re + im, im - re
            for part, value in enumerate((re, im, total)):
                mine_ref[n, part, t] = value
            for part, value in enumerate((total, gap)):
                theirs_ref[n, part, t] = value
            for part, value in enumerate((re, total, gap)):
                crossed_ref[n, part, t] = pltpu.roll(value, 4, 0)
        return carry

    lax.fori_loop(0, TM, unpack, 0)
    conjugate = jnp.where(row % 2 == 0, 1.0, -1.0)
    zero = jnp.zeros((8, LANES), jnp.float32)

    def finish(n, m, sums):
        values = []
        for number, (first, second, third) in enumerate((sums[:3], sums[3:])):
            real = first + third
            imag = zero if n == m and number == 0 else first - second
            values += [real, imag]
        tile = group_sums(values, 4)
        scale = scales[n * 8 : n * 8 + 8, :]
        even = jnp.broadcast_to(scale[:, 2 * m : 2 * m + 1], (8, LANES))
        odd = jnp.broadcast_to(scale[:, 2 * m + 1 : 2 * m + 2], (8, LANES))
        tile = tile * jnp.where((row < 2) | (row >= 6), even, odd)
        other = tile * conjugate
        for pair in range(4):
            h = pair // 2
            a = 2 * n + h
            b = 2 * m + (h if pair % 2 == 0 else 1 - h)
            at = slice(2 * pair, 2 * pair + 2)
            out_ref[a * S + place_ref[b]] = tile[at]
            if n != m:
                out_ref[b * S + place_ref[a]] = other[at]

    for block_n in range(0, STN, 2):
        for block_m in range(block_n, STN, 2):
            pairs = [
                (n, m)
                for n in range(block_n, block_n + 2)
                for m in range(block_m, block_m + 2)
                if n <= m
            ]

            def add(t, sums, pairs=pairs, block_n=block_n, block_m=block_m):
                mine = {
                    n: [mine_ref[n, part, t] for part in range(3)]
                    for n in range(block_n, block_n + 2)
                }
                theirs = {
                    m: [
                        mine_ref[m, 0, t],
                        theirs_ref[m, 0, t],
                        theirs_ref[m, 1, t],
                        *(crossed_ref[m, part, t] for part in range(3)),
                    ]
                    for m in range(block_m, block_m + 2)
                }
                result = []
                for (n, m), total in zip(pairs, sums):
                    re, im, both = mine[n]
                    factors = (both, re, im, both, re, im)
                    result.append(
                        tuple(
                            t0 + f * o for t0, f, o in zip(total, factors, theirs[m])
                        )
                    )
                return tuple(result)

            sums = lax.fori_loop(
                0, TM, add, tuple((zero,) * 6 for _ in pairs), unroll=4
            )
            for (n, m), total in zip(pairs, sums):
                finish(n, m, total)


def correlated(order, arrived):
    return pl.pallas_call(
        correlate_kernel,
        in_specs=[
            pl.BlockSpec(memory_space=pltpu.SMEM),
            pl.BlockSpec(memory_space=pltpu.VMEM),
        ],
        out_specs=pl.BlockSpec(memory_space=pltpu.VMEM),
        out_shape=jax.ShapeDtypeStruct((S * S, 2, LANES), jnp.float32),
        scratch_shapes=[
            pltpu.VMEM((STN, 3, TM, 8, LANES), jnp.float32),
            pltpu.VMEM((STN, 2, TM, 8, LANES), jnp.float32),
            pltpu.VMEM((STN, 3, TM, 8, LANES), jnp.float32),
            pltpu.VMEM((STN * 8, LANES), jnp.float32),
            pltpu.SMEM((S,), jnp.int32),
        ],
        compiler_params=pltpu.CompilerParams(vmem_limit_bytes=48 * 2**20),
        name="correlate",
    )(order, arrived.reshape(STN, TM, SPECTRA + 1, 2, LANES))


def fringe_tables():
    lag = np.arange(1, HALF + 1)
    fine = 2.0 * np.pi * ((np.arange(LANES)[:, None] * lag) % C) / C
    coarse = 2.0 * np.pi * ((np.arange(CB)[:, None] * lag) % CB) / CB
    period = 2.0 * np.pi * ((np.arange(PERIODS)[:, None] * np.arange(PERIODS)) % PERIODS)
    period = period / PERIODS
    factor = 1.0 / math.sqrt(PERIODS * C)
    flip = np.eye(HALF)[::-1]
    return [
        np.ascontiguousarray(table, np.float32)
        for table in (
            np.concatenate([np.cos(fine), np.sin(fine)], axis=1),
            np.stack([np.cos(coarse), np.sin(coarse)]),
            np.stack([np.cos(period), np.sin(period)]) * factor,
            flip,
        )
    ]


def fringe_kernel(z_ref, fine_ref, coarse_ref, period_ref, flip_ref, out_ref):
    fine = fine_ref[...]
    re = jnp.dot(z_ref[0], fine, precision=HIGHEST, preferred_element_type=jnp.float32)
    im = jnp.dot(z_ref[1], fine, precision=HIGHEST, preferred_element_type=jnp.float32)
    parts = [[], [], [], []]
    for p in range(PERIODS):
        sums = [jnp.zeros((8, LANES), jnp.float32)] * 4
        for g in range(CB // 8):
            at = slice(p * CB + g * 8, p * CB + g * 8 + 8)
            re_cos, re_sin = re[at, :HALF], re[at, HALF:]
            im_cos, im_sin = im[at, :HALF], im[at, HALF:]
            cosine = coarse_ref[0, g * 8 : g * 8 + 8, :]
            sine = coarse_ref[1, g * 8 : g * 8 + 8, :]
            plus_re, plus_im = re_cos + im_sin, im_cos - re_sin
            minus_re, minus_im = re_cos - im_sin, im_cos + re_sin
            terms = (
                cosine * minus_re - sine * minus_im,
                cosine * minus_im + sine * minus_re,
                cosine * plus_re + sine * plus_im,
                cosine * plus_im - sine * plus_re,
            )
            sums = [total + term for total, term in zip(sums, terms)]
        for part, total in zip(parts, sums):
            part.append(total)
    minus_re, minus_im, plus_re, plus_im = (group_sums(part, 8) for part in parts)
    reversed_ = jnp.dot(
        jnp.concatenate([minus_re, minus_im]),
        flip_ref[...],
        precision=HIGHEST,
        preferred_element_type=jnp.float32,
    )
    real = jnp.concatenate([reversed_[:8], plus_re], axis=1)
    imag = jnp.concatenate([reversed_[8:], plus_im], axis=1)
    cosine, sine = period_ref[0], period_ref[1]

    def turn(a, b):
        return jnp.dot(a, b, precision=HIGHEST, preferred_element_type=jnp.float32)

    out_ref[0, 0] = turn(cosine, real) + turn(sine, imag)
    out_ref[1, 0] = turn(cosine, imag) - turn(sine, real)


def fringed(normed):
    return pl.pallas_call(
        fringe_kernel,
        in_specs=[pl.BlockSpec(memory_space=pltpu.VMEM)] * 5,
        out_specs=pl.BlockSpec(memory_space=pltpu.VMEM),
        out_shape=jax.ShapeDtypeStruct((2, 1, PERIODS, LAGS), jnp.float32),
        compiler_params=pltpu.CompilerParams(vmem_limit_bytes=32 * 2**20),
        name="fringe",
    )(normed, *fringe_tables())


def per_device(spectra, flags, poly_index, delay_model, partner_order):
    axes = ("stn", "tm")
    first = (lax.axis_index("tm") * K).astype(jnp.int32).reshape(1)
    chunks = rotated_chunks(spectra, flags, poly_index, delay_model, first)
    arrived = lax.all_to_all(chunks, axes, split_axis=0, concat_axis=0, tiled=True)
    rows = correlated(partner_order, arrived)
    owned = lax.all_to_all(rows, axes, split_axis=0, concat_axis=0, tiled=True)
    return fringed(jnp.moveaxis(owned, 1, 0))


def solution(mesh):
    return jax.shard_map(
        per_device,
        mesh=mesh,
        in_specs=(
            P("stn", None, "tm", None, None),
            P("stn", None, "tm", None),
            P("stn", None, "tm"),
            P(),
            P(),
        ),
        out_specs=P(None, ("stn", "tm"), None, None),
        check_vma=False,
    )
```

```python
import math

import jax
import jax.numpy as jnp
import numpy as np
from jax import lax
from jax.experimental import pallas as pl
from jax.experimental.pallas import tpu as pltpu
from jax.sharding import Mesh
from jax.sharding import PartitionSpec as P

S = 16
C = 4096
PERIODS = 8
LAGS = 256
SPP = 128
CB = 32
STN = 8
QUARTERS = 4
UNITS = 8
ITEMS = 4
K = 4
SPECTRA = 2 * K
LANES = 128
HALF = LAGS // 2
HIGHEST = lax.Precision.HIGHEST


def rows_of(shape):
    return lax.broadcasted_iota(jnp.int32, shape, len(shape) - 2)


def lanes_of(shape):
    return lax.broadcasted_iota(jnp.int32, shape, len(shape) - 1)


def rotate_kernel(first_ref, poly_ref, model_ref, flags_ref, x_hbm, out_ref, x_ref, turned_re, turned_im, sems):
    def fetch(p):
        return pltpu.make_async_copy(x_hbm.at[:, p], x_ref.at[p], sems.at[p])

    for p in range(PERIODS):
        fetch(p).start()
    row = rows_of((8, LANES))
    lane = lanes_of((8, LANES))
    across = jnp.zeros((8, LANES), jnp.float32)
    down = []
    for p in range(PERIODS):
        column = jnp.zeros((8, LANES), jnp.float32)
        for s in range(2):
            for k in range(K):
                index = poly_ref[s, k, p]
                time = p * SPP + first_ref[0] + k
                moment = time.astype(jnp.float32) * (1.0 / (PERIODS * SPP))
                delay = (
                    model_ref[0, index]
                    + model_ref[1, index] * moment
                    + model_ref[2, index] * moment * moment
                )
                column = jnp.where(row == s * K + k, delay, column)
                across = jnp.where(lane == p * SPECTRA + s * K + k, delay, across)
        down.append(column)
    fine = [d * (lane.astype(jnp.float32) * (math.pi / C)) for d in down]
    fine_cos = [jnp.cos(f) for f in fine]
    fine_sin = [jnp.sin(f) for f in fine]
    weight = 1.0 - flags_ref[...].reshape(2 * PERIODS * K, CB).astype(jnp.float32)
    weight = weight.astype(jnp.bfloat16)
    source = rows_of((2 * PERIODS * K, LANES))
    source_s, source_p, source_k = source // (PERIODS * K), source // K % PERIODS, source % K
    target = lanes_of((2 * PERIODS * K, LANES))

    def spread(chosen):
        return lax.dot_general(
            weight,
            chosen.astype(jnp.bfloat16),
            (((0,), (0,)), ((), ())),
            preferred_element_type=jnp.float32,
        )

    spectrum = source_s * K + source_k
    coarse_weight = spread(
        jnp.where(target == source_p * SPECTRA + spectrum, 1.0, 0.0)
    )
    block = rows_of((CB, LANES)).astype(jnp.float32)
    coarse = jnp.tile(across, (CB // 8, 1)) * (block * (math.pi * LANES / C))
    coarse_cos = coarse_weight * jnp.cos(coarse)
    coarse_sin = coarse_weight * jnp.sin(coarse)
    for p in range(PERIODS):
        mark = jnp.where((source_p == p) & (target % SPECTRA == spectrum), 1.0, 0.0)
        sent = spread(mark).astype(jnp.bfloat16)
        fetch(p).wait()
        for s in range(2):
            for k in range(K):
                r = s * K + k
                x = x_ref[p, s, k].astype(jnp.float32)
                re = x[0:1].reshape(CB, LANES)
                im = x[1:2].reshape(CB, LANES)
                at = p * SPECTRA + r
                a_cos = jnp.broadcast_to(coarse_cos[:, at : at + 1], (CB, LANES))
                a_sin = jnp.broadcast_to(coarse_sin[:, at : at + 1], (CB, LANES))
                b_cos = jnp.broadcast_to(fine_cos[p][r : r + 1], (CB, LANES))
                b_sin = jnp.broadcast_to(fine_sin[p][r : r + 1], (CB, LANES))
                cosine = a_cos * b_cos - a_sin * b_sin
                sine = a_sin * b_cos + a_cos * b_sin
                turned_re[p % 2, pl.ds(r, CB, stride=SPECTRA), :] = re * cosine + im * sine
                turned_im[p % 2, pl.ds(r, CB, stride=SPECTRA), :] = im * cosine - re * sine
        for q in range(CB):
            at = slice(q * SPECTRA, (q + 1) * SPECTRA)
            both = jnp.concatenate([turned_re[p % 2, at], turned_im[p % 2, at]])
            out_ref[p * CB + q, 0:SPECTRA] = both.astype(jnp.bfloat16).reshape(SPECTRA, 2, LANES)
        out_ref[p * CB : (p + 1) * CB, SPECTRA] = jnp.broadcast_to(
            sent[:, None, :], (CB, 2, LANES)
        )


def rotated_chunks(spectra, flags, poly_index, delay_model, first):
    return pl.pallas_call(
        rotate_kernel,
        in_specs=[
            pl.BlockSpec(memory_space=pltpu.SMEM),
            pl.BlockSpec(memory_space=pltpu.SMEM),
            pl.BlockSpec(memory_space=pltpu.SMEM),
            pl.BlockSpec(memory_space=pltpu.VMEM),
            pl.BlockSpec(memory_space=pltpu.HBM),
        ],
        out_specs=pl.BlockSpec(memory_space=pltpu.VMEM),
        out_shape=jax.ShapeDtypeStruct((PERIODS * CB, SPECTRA + 1, 2, LANES), jnp.bfloat16),
        scratch_shapes=[
            pltpu.VMEM((PERIODS, 2, K, 2, C), jnp.bfloat16),
            pltpu.VMEM((2, CB * SPECTRA, LANES), jnp.float32),
            pltpu.VMEM((2, CB * SPECTRA, LANES), jnp.float32),
            pltpu.SemaphoreType.DMA((PERIODS,)),
        ],
        compiler_params=pltpu.CompilerParams(vmem_limit_bytes=32 * 2**20),
        name="rotate",
    )(first, poly_index.transpose(0, 2, 1), delay_model.T, flags, spectra)


def group_sums(values, group):
    row = rows_of((8, LANES))
    stage = list(values)
    distance = group // 2
    while distance:
        first = row % (2 * distance) < distance
        if 2 * distance == 8:
            stage = [
                jnp.where(first, stage[i], stage[i + distance])
                + pltpu.roll(jnp.where(first, stage[i + distance], stage[i]), 4, 0)
                for i in range(distance)
            ]
        else:
            stage = [
                jnp.where(first, stage[i], stage[i + distance])
                + jnp.where(
                    first,
                    pltpu.roll(stage[i], 8 - distance, 0),
                    pltpu.roll(stage[i + distance], distance, 0),
                )
                for i in range(distance)
            ]
        distance //= 2
    return stage[0]


def pair_counts(seen):
    seen = seen.astype(jnp.bfloat16)
    together = lax.dot_general(
        seen, seen, (((0,), (0,)), ((), ())), preferred_element_type=jnp.float32
    )
    i, j = rows_of((LANES, LANES)), lanes_of((LANES, LANES))
    together = jnp.where(i % K == j % K, together, 0.0).astype(jnp.bfloat16)
    partner = jnp.where(i // K == j, 1.0, 0.0).astype(jnp.bfloat16)
    summed = jnp.dot(together, partner, preferred_element_type=jnp.float32)
    station = jnp.where(rows_of((S, LANES)) == lanes_of((S, LANES)) // K, 1.0, 0.0)
    return jnp.dot(
        station.astype(jnp.bfloat16),
        summed.astype(jnp.bfloat16),
        preferred_element_type=jnp.float32,
    )


PAIRS = [(n, m) for n in range(STN) for m in range(n, STN)]


def correlate_kernel(order_ref, y_ref, out_ref, mine_ref, theirs_ref, crossed_ref, tiles, counts, place_ref):
    for j in range(S):
        place_ref[order_ref[j]] = j
    row = rows_of((8, LANES))
    lane = lanes_of((8, LANES))
    zero = jnp.zeros((8, LANES), jnp.float32)

    def finish(n, m, item, sums):
        values = []
        for number, (first, second, third) in enumerate((sums[:3], sums[3:])):
            real = first + third
            imag = zero if n == m and number == 0 else first - second
            values += [real, imag]
        tile = group_sums(values, 4)
        if n == m:
            left = tile - tile.astype(jnp.bfloat16).astype(jnp.float32)
            tile = jnp.where(row % 4 == 1, pltpu.roll(left, 1, 0), tile)
        tiles[PAIRS.index((n, m)), item] = tile

    def one_item(item, carry):
        seen = zero
        for n in range(STN):
            for u in range(UNITS):
                x = y_ref[n, u, item, 0:SPECTRA].reshape(2 * SPECTRA, LANES)
                x = x.astype(jnp.float32)
                re, im = x[:SPECTRA], x[SPECTRA:]
                total, gap = re + im, im - re
                for part, value in enumerate((re, im, total)):
                    mine_ref[n, part, u] = value
                theirs_ref[n, u] = gap
                for part, value in enumerate((re, total, gap)):
                    crossed_ref[n, part, u] = pltpu.roll(value, 4, 0)
            weight = y_ref[n, :, item, SPECTRA].astype(jnp.float32)[:, 0, :]
            seen = jnp.where(lane // SPECTRA == n, weight, seen)
        counts[item] = pair_counts(seen)
        for block_n in range(0, STN, 2):
            for block_m in range(block_n, STN, 2):
                pairs = [
                    (n, m)
                    for n in range(block_n, block_n + 2)
                    for m in range(block_m, block_m + 2)
                    if n <= m
                ]
                sums = {pair: None for pair in pairs}
                for u in range(UNITS):
                    mine = {
                        n: [mine_ref[n, part, u] for part in range(3)]
                        for n in range(block_n, block_n + 2)
                    }
                    theirs = {
                        m: [
                            mine_ref[m, 0, u],
                            mine_ref[m, 2, u],
                            theirs_ref[m, u],
                            *(crossed_ref[m, part, u] for part in range(3)),
                        ]
                        for m in range(block_m, block_m + 2)
                    }
                    for n, m in pairs:
                        re, im, both = mine[n]
                        terms = [
                            f * o
                            for f, o in zip((both, re, im, both, re, im), theirs[m])
                        ]
                        old = sums[n, m]
                        sums[n, m] = (
                            terms if old is None else [x + y for x, y in zip(old, terms)]
                        )
                for n, m in pairs:
                    finish(n, m, item, sums[n, m])
        return carry

    lax.fori_loop(0, ITEMS, one_item, 0)
    conjugate = jnp.where(row % 2 == 0, 1.0, -1.0)
    upper, inner = row < 4, row % 4 < 2
    for number, (n, m) in enumerate(PAIRS):
        t = [tiles[number, item] for item in range(ITEMS)]
        halves = (
            [jnp.where(upper, t[i], pltpu.roll(t[i + 2], 4, 0)) for i in range(2)],
            [jnp.where(upper, pltpu.roll(t[i], 4, 0), t[i + 2]) for i in range(2)],
        )
        for h, (x, y) in enumerate(halves):
            same = jnp.where(inner, x, pltpu.roll(y, 2, 0))
            crossed = jnp.where(inner, pltpu.roll(x, 6, 0), y)
            a = 2 * n + h
            for b, value in ((2 * m + h, same), (2 * m + 1 - h, crossed)):
                out_ref[a * S + place_ref[b], 0:ITEMS] = value.astype(
                    jnp.bfloat16
                ).reshape(ITEMS, 2, LANES)
                if n != m:
                    out_ref[b * S + place_ref[a], 0:ITEMS] = (
                        (value * conjugate).astype(jnp.bfloat16).reshape(ITEMS, 2, LANES)
                    )
    group = lanes_of((S, LANES)) // (LANES // ITEMS)
    for b in range(S):
        seen = jnp.zeros((S, LANES), jnp.float32)
        for item in range(ITEMS):
            column = jnp.broadcast_to(counts[item, :, b : b + 1], (S, LANES))
            seen = jnp.where(group == item, column, seen)
        at = place_ref[b]
        for a in range(S):
            out_ref[a * S + at, ITEMS] = jnp.broadcast_to(
                seen[a : a + 1], (2, LANES)
            ).astype(jnp.bfloat16)


def correlated(order, arrived):
    return pl.pallas_call(
        correlate_kernel,
        in_specs=[
            pl.BlockSpec(memory_space=pltpu.SMEM),
            pl.BlockSpec(memory_space=pltpu.VMEM),
        ],
        out_specs=pl.BlockSpec(memory_space=pltpu.VMEM),
        out_shape=jax.ShapeDtypeStruct((S * S, ITEMS + 1, 2, LANES), jnp.bfloat16),
        scratch_shapes=[
            pltpu.VMEM((STN, 3, UNITS, 8, LANES), jnp.float32),
            pltpu.VMEM((STN, UNITS, 8, LANES), jnp.float32),
            pltpu.VMEM((STN, 3, UNITS, 8, LANES), jnp.float32),
            pltpu.VMEM((len(PAIRS), ITEMS, 8, LANES), jnp.float32),
            pltpu.VMEM((ITEMS, S, LANES), jnp.float32),
            pltpu.SMEM((S,), jnp.int32),
        ],
        compiler_params=pltpu.CompilerParams(vmem_limit_bytes=32 * 2**20),
        name="correlate",
    )(order, arrived.reshape(STN, UNITS, ITEMS, SPECTRA + 1, 2, LANES))


def fringe_tables():
    lag = np.arange(1, HALF + 1)
    fine = 2.0 * np.pi * ((np.arange(LANES)[:, None] * lag) % C) / C
    coarse = 2.0 * np.pi * ((np.arange(CB)[:, None] * lag) % CB) / CB
    period = 2.0 * np.pi * ((np.arange(PERIODS)[:, None] * np.arange(PERIODS)) % PERIODS)
    period = period / PERIODS
    factor = 1.0 / math.sqrt(PERIODS * C)
    flip = np.eye(HALF)[::-1]
    return [
        np.ascontiguousarray(table, np.float32)
        for table in (
            np.concatenate([np.cos(fine), np.sin(fine)], axis=1),
            np.stack([np.cos(coarse), np.sin(coarse)]),
            np.stack([np.cos(period), np.sin(period)]) * factor,
            flip,
        )
    ]


def fringe_kernel(
    row_ref, order_ref, z_ref, fine_ref, coarse_ref, period_ref, flip_ref, out_ref, sums, scales
):
    for p in range(PERIODS):
        for u in range(UNITS):
            parts = [
                z_ref[p, quarter, u, 0:ITEMS].reshape(2 * ITEMS, LANES).astype(jnp.float32)
                for quarter in range(QUARTERS)
            ]
            at = (p * UNITS + u) * 2 * ITEMS
            sums[at : at + 2 * ITEMS] = (parts[0] + parts[1]) + (parts[2] + parts[3])
        counts = sum(
            z_ref[p, quarter, :, ITEMS].astype(jnp.float32)[:, 0, :]
            for quarter in range(QUARTERS)
        )
        scale = 1.0 / jnp.sqrt(jnp.maximum(counts, 1.0))
        for item in range(ITEMS):
            at = item * (LANES // ITEMS)
            scales[pl.ds(p * CB + item, UNITS, stride=ITEMS), :] = jnp.broadcast_to(
                scale[:, at : at + 1], (UNITS, LANES)
            )
    alone = order_ref[row_ref[0] % S] == row_ref[0] // S
    left = jnp.where(alone, 1.0, 0.0)
    first = sums[pl.ds(0, PERIODS * CB, stride=2), :]
    second = sums[pl.ds(1, PERIODS * CB, stride=2), :]
    fine = fine_ref[...]
    re = jnp.dot(
        (first + left * second) * scales[...],
        fine,
        precision=HIGHEST,
        preferred_element_type=jnp.float32,
    )
    im = jnp.dot(
        (second * (1.0 - left)) * scales[...],
        fine,
        precision=HIGHEST,
        preferred_element_type=jnp.float32,
    )
    parts = [[], [], [], []]
    for p in range(PERIODS):
        sums = [jnp.zeros((8, LANES), jnp.float32)] * 4
        for g in range(CB // 8):
            at = slice(p * CB + g * 8, p * CB + g * 8 + 8)
            re_cos, re_sin = re[at, :HALF], re[at, HALF:]
            im_cos, im_sin = im[at, :HALF], im[at, HALF:]
            cosine = coarse_ref[0, g * 8 : g * 8 + 8, :]
            sine = coarse_ref[1, g * 8 : g * 8 + 8, :]
            plus_re, plus_im = re_cos + im_sin, im_cos - re_sin
            minus_re, minus_im = re_cos - im_sin, im_cos + re_sin
            terms = (
                cosine * minus_re - sine * minus_im,
                cosine * minus_im + sine * minus_re,
                cosine * plus_re + sine * plus_im,
                cosine * plus_im - sine * plus_re,
            )
            sums = [total + term for total, term in zip(sums, terms)]
        for part, total in zip(parts, sums):
            part.append(total)
    minus_re, minus_im, plus_re, plus_im = (group_sums(part, 8) for part in parts)
    reversed_ = jnp.dot(
        jnp.concatenate([minus_re, minus_im]),
        flip_ref[...],
        precision=HIGHEST,
        preferred_element_type=jnp.float32,
    )
    real = jnp.concatenate([reversed_[:8], plus_re], axis=1)
    imag = jnp.concatenate([reversed_[8:], plus_im], axis=1)
    cosine, sine = period_ref[0], period_ref[1]

    def turn(a, b):
        return jnp.dot(a, b, precision=HIGHEST, preferred_element_type=jnp.float32)

    out_ref[0, 0] = turn(cosine, real) + turn(sine, imag)
    out_ref[1, 0] = turn(cosine, imag) - turn(sine, real)


def fringed(row, order, owned):
    return pl.pallas_call(
        fringe_kernel,
        in_specs=[pl.BlockSpec(memory_space=pltpu.SMEM)] * 2
        + [pl.BlockSpec(memory_space=pltpu.VMEM)] * 5,
        out_specs=pl.BlockSpec(memory_space=pltpu.VMEM),
        out_shape=jax.ShapeDtypeStruct((2, 1, PERIODS, LAGS), jnp.float32),
        scratch_shapes=[
            pltpu.VMEM((PERIODS * CB * 2, LANES), jnp.float32),
            pltpu.VMEM((PERIODS * CB, LANES), jnp.float32),
        ],
        compiler_params=pltpu.CompilerParams(vmem_limit_bytes=32 * 2**20),
        name="fringe",
    )(
        row,
        order,
        owned.reshape(PERIODS, QUARTERS, UNITS, ITEMS + 1, 2, LANES),
        *fringe_tables(),
    )


def per_device(spectra, flags, poly_index, delay_model, partner_order):
    plane = ("stn", "unit")
    everyone = ("stn", "quarter", "unit")
    shard = lax.axis_index(("quarter", "unit")).astype(jnp.int32)
    row = lax.axis_index(everyone).astype(jnp.int32)
    chunks = rotated_chunks(spectra, flags, poly_index, delay_model, (shard * K).reshape(1))
    chunks = chunks.reshape(STN * UNITS, ITEMS * (SPECTRA + 1), 2, LANES)
    arrived = lax.all_to_all(chunks, plane, split_axis=0, concat_axis=0, tiled=True)
    rows = correlated(partner_order, arrived)
    owned = lax.all_to_all(rows, everyone, split_axis=0, concat_axis=0, tiled=True)
    return fringed(row.reshape(1), partner_order, owned)


def solution(mesh):
    finer = Mesh(
        mesh.devices.reshape(STN, QUARTERS, UNITS), ("stn", "quarter", "unit")
    )
    time = ("quarter", "unit")
    return jax.shard_map(
        per_device,
        mesh=finer,
        in_specs=(
            P("stn", None, time, None, None),
            P("stn", None, time, None),
            P("stn", None, time),
            P(),
            P(),
        ),
        out_specs=P(None, ("stn", "quarter", "unit"), None, None),
        check_vma=False,
    )
```

```python
import math

import jax
import jax.numpy as jnp
import numpy as np
from jax import lax
from jax.experimental import pallas as pl
from jax.experimental.pallas import tpu as pltpu
from jax.sharding import Mesh
from jax.sharding import PartitionSpec as P

S = 16
C = 4096
PERIODS = 8
LAGS = 256
SPP = 128
CB = 32
STN = 8
QUARTERS = 4
UNITS = 8
ITEMS = 4
K = 4
NPOLY = 64
SPECTRA = 2 * K
LANES = 128
HALF = LAGS // 2
HIGHEST = lax.Precision.HIGHEST


def rows_of(shape):
    return lax.broadcasted_iota(jnp.int32, shape, len(shape) - 2)


def lanes_of(shape):
    return lax.broadcasted_iota(jnp.int32, shape, len(shape) - 1)


def in_hbm(array):
    return pltpu.with_memory_space_constraint(array, pltpu.HBM)


def rotate_kernel(
    first_ref,
    poly_hbm,
    model_hbm,
    flags_hbm,
    x_hbm,
    out_ref,
    poly_ref,
    model_ref,
    flags_ref,
    x_ref,
    turned_re,
    turned_im,
    sems,
    small_sems,
):
    def fetch(p):
        return pltpu.make_async_copy(x_hbm.at[:, p], x_ref.at[p], sems.at[p])

    small = [
        pltpu.make_async_copy(source, target, small_sems.at[number])
        for number, (source, target) in enumerate(
            ((poly_hbm, poly_ref), (model_hbm, model_ref), (flags_hbm, flags_ref))
        )
    ]
    for copy in small:
        copy.start()
    for p in range(PERIODS):
        fetch(p).start()
    for copy in small:
        copy.wait()
    row = rows_of((8, LANES))
    lane = lanes_of((8, LANES))
    across = jnp.zeros((8, LANES), jnp.float32)
    down = []
    for p in range(PERIODS):
        column = jnp.zeros((8, LANES), jnp.float32)
        for s in range(2):
            for k in range(K):
                index = poly_ref[s, k, p]
                time = p * SPP + first_ref[0] + k
                moment = time.astype(jnp.float32) * (1.0 / (PERIODS * SPP))
                delay = (
                    model_ref[0, index]
                    + model_ref[1, index] * moment
                    + model_ref[2, index] * moment * moment
                )
                column = jnp.where(row == s * K + k, delay, column)
                across = jnp.where(lane == p * SPECTRA + s * K + k, delay, across)
        down.append(column)
    fine = [d * (lane.astype(jnp.float32) * (math.pi / C)) for d in down]
    fine_cos = [jnp.cos(f) for f in fine]
    fine_sin = [jnp.sin(f) for f in fine]
    weight = 1.0 - flags_ref[...].reshape(2 * PERIODS * K, CB).astype(jnp.float32)
    weight = weight.astype(jnp.bfloat16)
    source = rows_of((2 * PERIODS * K, LANES))
    source_s, source_p, source_k = source // (PERIODS * K), source // K % PERIODS, source % K
    target = lanes_of((2 * PERIODS * K, LANES))

    def spread(chosen):
        return lax.dot_general(
            weight,
            chosen.astype(jnp.bfloat16),
            (((0,), (0,)), ((), ())),
            preferred_element_type=jnp.float32,
        )

    spectrum = source_s * K + source_k
    coarse_weight = spread(
        jnp.where(target == source_p * SPECTRA + spectrum, 1.0, 0.0)
    )
    block = rows_of((CB, LANES)).astype(jnp.float32)
    coarse = jnp.tile(across, (CB // 8, 1)) * (block * (math.pi * LANES / C))
    coarse_cos = coarse_weight * jnp.cos(coarse)
    coarse_sin = coarse_weight * jnp.sin(coarse)
    for p in range(PERIODS):
        mark = jnp.where((source_p == p) & (target % SPECTRA == spectrum), 1.0, 0.0)
        sent = spread(mark).astype(jnp.bfloat16)
        fetch(p).wait()
        for s in range(2):
            for k in range(K):
                r = s * K + k
                x = x_ref[p, s, k].astype(jnp.float32)
                re = x[0:1].reshape(CB, LANES)
                im = x[1:2].reshape(CB, LANES)
                at = p * SPECTRA + r
                a_cos = jnp.broadcast_to(coarse_cos[:, at : at + 1], (CB, LANES))
                a_sin = jnp.broadcast_to(coarse_sin[:, at : at + 1], (CB, LANES))
                b_cos = jnp.broadcast_to(fine_cos[p][r : r + 1], (CB, LANES))
                b_sin = jnp.broadcast_to(fine_sin[p][r : r + 1], (CB, LANES))
                cosine = a_cos * b_cos - a_sin * b_sin
                sine = a_sin * b_cos + a_cos * b_sin
                turned_re[p % 2, pl.ds(r, CB, stride=SPECTRA), :] = re * cosine + im * sine
                turned_im[p % 2, pl.ds(r, CB, stride=SPECTRA), :] = im * cosine - re * sine
        for q in range(CB):
            at = slice(q * SPECTRA, (q + 1) * SPECTRA)
            both = jnp.concatenate([turned_re[p % 2, at], turned_im[p % 2, at]])
            out_ref[p * CB + q, 0:SPECTRA] = both.astype(jnp.bfloat16).reshape(SPECTRA, 2, LANES)
        out_ref[p * CB : (p + 1) * CB, SPECTRA] = jnp.broadcast_to(
            sent[:, None, :], (CB, 2, LANES)
        )


def rotated_chunks(spectra, flags, poly_index, delay_model, first):
    return pl.pallas_call(
        rotate_kernel,
        in_specs=[pl.BlockSpec(memory_space=pltpu.SMEM)]
        + [pl.BlockSpec(memory_space=pltpu.HBM)] * 4,
        out_specs=pl.BlockSpec(memory_space=pltpu.VMEM),
        out_shape=jax.ShapeDtypeStruct((PERIODS * CB, SPECTRA + 1, 2, LANES), jnp.bfloat16),
        scratch_shapes=[
            pltpu.SMEM((2, K, PERIODS), jnp.int32),
            pltpu.SMEM((3, NPOLY), jnp.float32),
            pltpu.VMEM((2, PERIODS, K, CB), jnp.int32),
            pltpu.VMEM((PERIODS, 2, K, 2, C), jnp.bfloat16),
            pltpu.VMEM((2, CB * SPECTRA, LANES), jnp.float32),
            pltpu.VMEM((2, CB * SPECTRA, LANES), jnp.float32),
            pltpu.SemaphoreType.DMA((PERIODS,)),
            pltpu.SemaphoreType.DMA((3,)),
        ],
        compiler_params=pltpu.CompilerParams(vmem_limit_bytes=32 * 2**20),
        name="rotate",
    )(
        first,
        in_hbm(poly_index.transpose(0, 2, 1)),
        in_hbm(delay_model.T),
        in_hbm(flags),
        in_hbm(spectra),
    )


def group_sums(values, group):
    row = rows_of((8, LANES))
    stage = list(values)
    distance = group // 2
    while distance:
        first = row % (2 * distance) < distance
        if 2 * distance == 8:
            stage = [
                jnp.where(first, stage[i], stage[i + distance])
                + pltpu.roll(jnp.where(first, stage[i + distance], stage[i]), 4, 0)
                for i in range(distance)
            ]
        else:
            stage = [
                jnp.where(first, stage[i], stage[i + distance])
                + jnp.where(
                    first,
                    pltpu.roll(stage[i], 8 - distance, 0),
                    pltpu.roll(stage[i + distance], distance, 0),
                )
                for i in range(distance)
            ]
        distance //= 2
    return stage[0]


def pair_counts(seen):
    seen = seen.astype(jnp.bfloat16)
    together = lax.dot_general(
        seen, seen, (((0,), (0,)), ((), ())), preferred_element_type=jnp.float32
    )
    i, j = rows_of((LANES, LANES)), lanes_of((LANES, LANES))
    together = jnp.where(i % K == j % K, together, 0.0).astype(jnp.bfloat16)
    partner = jnp.where(i // K == j, 1.0, 0.0).astype(jnp.bfloat16)
    summed = jnp.dot(together, partner, preferred_element_type=jnp.float32)
    station = jnp.where(rows_of((S, LANES)) == lanes_of((S, LANES)) // K, 1.0, 0.0)
    return jnp.dot(
        station.astype(jnp.bfloat16),
        summed.astype(jnp.bfloat16),
        preferred_element_type=jnp.float32,
    )


PAIRS = [(n, m) for n in range(STN) for m in range(n, STN)]


def correlate_kernel(order_ref, y_ref, out_ref, mine_ref, theirs_ref, crossed_ref, tiles, counts, place_ref):
    for j in range(S):
        place_ref[order_ref[j]] = j
    row = rows_of((8, LANES))
    lane = lanes_of((8, LANES))
    zero = jnp.zeros((8, LANES), jnp.float32)

    def finish(n, m, item, sums):
        values = []
        for number, (first, second, third) in enumerate((sums[:3], sums[3:])):
            real = first + third
            imag = zero if n == m and number == 0 else first - second
            values += [real, imag]
        tile = group_sums(values, 4)
        if n == m:
            left = tile - tile.astype(jnp.bfloat16).astype(jnp.float32)
            tile = jnp.where(row % 4 == 1, pltpu.roll(left, 1, 0), tile)
        tiles[PAIRS.index((n, m)), item] = tile

    def one_item(item, carry):
        seen = zero
        for n in range(STN):
            for u in range(UNITS):
                x = y_ref[n, u, item, 0:SPECTRA].reshape(2 * SPECTRA, LANES)
                x = x.astype(jnp.float32)
                re, im = x[:SPECTRA], x[SPECTRA:]
                total, gap = re + im, im - re
                for part, value in enumerate((re, im, total)):
                    mine_ref[n, part, u] = value
                theirs_ref[n, u] = gap
                for part, value in enumerate((re, total, gap)):
                    crossed_ref[n, part, u] = pltpu.roll(value, 4, 0)
            weight = y_ref[n, :, item, SPECTRA].astype(jnp.float32)[:, 0, :]
            seen = jnp.where(lane // SPECTRA == n, weight, seen)
        counts[item] = pair_counts(seen)
        for block_n in range(0, STN, 2):
            for block_m in range(block_n, STN, 2):
                pairs = [
                    (n, m)
                    for n in range(block_n, block_n + 2)
                    for m in range(block_m, block_m + 2)
                    if n <= m
                ]
                sums = {pair: None for pair in pairs}
                for u in range(UNITS):
                    mine = {
                        n: [mine_ref[n, part, u] for part in range(3)]
                        for n in range(block_n, block_n + 2)
                    }
                    theirs = {
                        m: [
                            mine_ref[m, 0, u],
                            mine_ref[m, 2, u],
                            theirs_ref[m, u],
                            *(crossed_ref[m, part, u] for part in range(3)),
                        ]
                        for m in range(block_m, block_m + 2)
                    }
                    for n, m in pairs:
                        re, im, both = mine[n]
                        terms = [
                            f * o
                            for f, o in zip((both, re, im, both, re, im), theirs[m])
                        ]
                        old = sums[n, m]
                        sums[n, m] = (
                            terms if old is None else [x + y for x, y in zip(old, terms)]
                        )
                for n, m in pairs:
                    finish(n, m, item, sums[n, m])
        return carry

    lax.fori_loop(0, ITEMS, one_item, 0)
    conjugate = jnp.where(row % 2 == 0, 1.0, -1.0)
    upper, inner = row < 4, row % 4 < 2
    for number, (n, m) in enumerate(PAIRS):
        t = [tiles[number, item] for item in range(ITEMS)]
        halves = (
            [jnp.where(upper, t[i], pltpu.roll(t[i + 2], 4, 0)) for i in range(2)],
            [jnp.where(upper, pltpu.roll(t[i], 4, 0), t[i + 2]) for i in range(2)],
        )
        for h, (x, y) in enumerate(halves):
            same = jnp.where(inner, x, pltpu.roll(y, 2, 0))
            crossed = jnp.where(inner, pltpu.roll(x, 6, 0), y)
            a = 2 * n + h
            for b, value in ((2 * m + h, same), (2 * m + 1 - h, crossed)):
                out_ref[a * S + place_ref[b], 0:ITEMS] = value.astype(
                    jnp.bfloat16
                ).reshape(ITEMS, 2, LANES)
                if n != m:
                    out_ref[b * S + place_ref[a], 0:ITEMS] = (
                        (value * conjugate).astype(jnp.bfloat16).reshape(ITEMS, 2, LANES)
                    )
    group = lanes_of((S, LANES)) // (LANES // ITEMS)
    for b in range(S):
        seen = jnp.zeros((S, LANES), jnp.float32)
        for item in range(ITEMS):
            column = jnp.broadcast_to(counts[item, :, b : b + 1], (S, LANES))
            seen = jnp.where(group == item, column, seen)
        at = place_ref[b]
        for a in range(S):
            out_ref[a * S + at, ITEMS] = jnp.broadcast_to(
                seen[a : a + 1], (2, LANES)
            ).astype(jnp.bfloat16)


def correlated(order, arrived):
    return pl.pallas_call(
        correlate_kernel,
        in_specs=[
            pl.BlockSpec(memory_space=pltpu.SMEM),
            pl.BlockSpec(memory_space=pltpu.VMEM),
        ],
        out_specs=pl.BlockSpec(memory_space=pltpu.VMEM),
        out_shape=jax.ShapeDtypeStruct((S * S, ITEMS + 1, 2, LANES), jnp.bfloat16),
        scratch_shapes=[
            pltpu.VMEM((STN, 3, UNITS, 8, LANES), jnp.float32),
            pltpu.VMEM((STN, UNITS, 8, LANES), jnp.float32),
            pltpu.VMEM((STN, 3, UNITS, 8, LANES), jnp.float32),
            pltpu.VMEM((len(PAIRS), ITEMS, 8, LANES), jnp.float32),
            pltpu.VMEM((ITEMS, S, LANES), jnp.float32),
            pltpu.SMEM((S,), jnp.int32),
        ],
        compiler_params=pltpu.CompilerParams(vmem_limit_bytes=32 * 2**20),
        name="correlate",
    )(order, arrived.reshape(STN, UNITS, ITEMS, SPECTRA + 1, 2, LANES))


def fringe_tables():
    lag = np.arange(1, HALF + 1)
    fine = 2.0 * np.pi * ((np.arange(LANES)[:, None] * lag) % C) / C
    coarse = 2.0 * np.pi * ((np.arange(CB)[:, None] * lag) % CB) / CB
    period = 2.0 * np.pi * ((np.arange(PERIODS)[:, None] * np.arange(PERIODS)) % PERIODS)
    period = period / PERIODS
    factor = 1.0 / math.sqrt(PERIODS * C)
    flip = np.eye(HALF)[::-1]
    return [
        np.ascontiguousarray(table, np.float32)
        for table in (
            np.concatenate([np.cos(fine), np.sin(fine)], axis=1),
            np.stack([np.cos(coarse), np.sin(coarse)]),
            np.stack([np.cos(period), np.sin(period)]) * factor,
            flip,
        )
    ]


def fringe_kernel(
    row_ref, order_ref, z_ref, fine_ref, coarse_ref, period_ref, flip_ref, out_ref, sums, scales
):
    for p in range(PERIODS):
        for u in range(UNITS):
            parts = [
                z_ref[p, quarter, u, 0:ITEMS].reshape(2 * ITEMS, LANES).astype(jnp.float32)
                for quarter in range(QUARTERS)
            ]
            at = (p * UNITS + u) * 2 * ITEMS
            sums[at : at + 2 * ITEMS] = (parts[0] + parts[1]) + (parts[2] + parts[3])
        counts = sum(
            z_ref[p, quarter, :, ITEMS].astype(jnp.float32)[:, 0, :]
            for quarter in range(QUARTERS)
        )
        scale = 1.0 / jnp.sqrt(jnp.maximum(counts, 1.0))
        for item in range(ITEMS):
            at = item * (LANES // ITEMS)
            scales[pl.ds(p * CB + item, UNITS, stride=ITEMS), :] = jnp.broadcast_to(
                scale[:, at : at + 1], (UNITS, LANES)
            )
    alone = order_ref[row_ref[0] % S] == row_ref[0] // S
    left = jnp.where(alone, 1.0, 0.0)
    first = sums[pl.ds(0, PERIODS * CB, stride=2), :]
    second = sums[pl.ds(1, PERIODS * CB, stride=2), :]
    fine = fine_ref[...]
    re = jnp.dot(
        (first + left * second) * scales[...],
        fine,
        precision=HIGHEST,
        preferred_element_type=jnp.float32,
    )
    im = jnp.dot(
        (second * (1.0 - left)) * scales[...],
        fine,
        precision=HIGHEST,
        preferred_element_type=jnp.float32,
    )
    parts = [[], [], [], []]
    for p in range(PERIODS):
        sums = [jnp.zeros((8, LANES), jnp.float32)] * 4
        for g in range(CB // 8):
            at = slice(p * CB + g * 8, p * CB + g * 8 + 8)
            re_cos, re_sin = re[at, :HALF], re[at, HALF:]
            im_cos, im_sin = im[at, :HALF], im[at, HALF:]
            cosine = coarse_ref[0, g * 8 : g * 8 + 8, :]
            sine = coarse_ref[1, g * 8 : g * 8 + 8, :]
            plus_re, plus_im = re_cos + im_sin, im_cos - re_sin
            minus_re, minus_im = re_cos - im_sin, im_cos + re_sin
            terms = (
                cosine * minus_re - sine * minus_im,
                cosine * minus_im + sine * minus_re,
                cosine * plus_re + sine * plus_im,
                cosine * plus_im - sine * plus_re,
            )
            sums = [total + term for total, term in zip(sums, terms)]
        for part, total in zip(parts, sums):
            part.append(total)
    minus_re, minus_im, plus_re, plus_im = (group_sums(part, 8) for part in parts)
    reversed_ = jnp.dot(
        jnp.concatenate([minus_re, minus_im]),
        flip_ref[...],
        precision=HIGHEST,
        preferred_element_type=jnp.float32,
    )
    real = jnp.concatenate([reversed_[:8], plus_re], axis=1)
    imag = jnp.concatenate([reversed_[8:], plus_im], axis=1)
    cosine, sine = period_ref[0], period_ref[1]

    def turn(a, b):
        return jnp.dot(a, b, precision=HIGHEST, preferred_element_type=jnp.float32)

    out_ref[0, 0] = turn(cosine, real) + turn(sine, imag)
    out_ref[1, 0] = turn(cosine, imag) - turn(sine, real)


def fringed(row, order, owned):
    return pl.pallas_call(
        fringe_kernel,
        in_specs=[pl.BlockSpec(memory_space=pltpu.SMEM)] * 2
        + [pl.BlockSpec(memory_space=pltpu.VMEM)] * 5,
        out_specs=pl.BlockSpec(memory_space=pltpu.VMEM),
        out_shape=jax.ShapeDtypeStruct((2, 1, PERIODS, LAGS), jnp.float32),
        scratch_shapes=[
            pltpu.VMEM((PERIODS * CB * 2, LANES), jnp.float32),
            pltpu.VMEM((PERIODS * CB, LANES), jnp.float32),
        ],
        compiler_params=pltpu.CompilerParams(vmem_limit_bytes=32 * 2**20),
        name="fringe",
    )(
        row,
        order,
        owned.reshape(PERIODS, QUARTERS, UNITS, ITEMS + 1, 2, LANES),
        *fringe_tables(),
    )


def per_device(spectra, flags, poly_index, delay_model, partner_order):
    plane = ("stn", "unit")
    everyone = ("stn", "quarter", "unit")
    shard = lax.axis_index(("quarter", "unit")).astype(jnp.int32)
    row = lax.axis_index(everyone).astype(jnp.int32)
    chunks = rotated_chunks(spectra, flags, poly_index, delay_model, (shard * K).reshape(1))
    chunks = chunks.reshape(STN * UNITS, ITEMS * (SPECTRA + 1), 2, LANES)
    arrived = lax.all_to_all(chunks, plane, split_axis=0, concat_axis=0, tiled=True)
    rows = correlated(partner_order, arrived)
    owned = lax.all_to_all(rows, everyone, split_axis=0, concat_axis=0, tiled=True)
    return fringed(row.reshape(1), partner_order, owned)


def solution(mesh):
    finer = Mesh(
        mesh.devices.reshape(STN, QUARTERS, UNITS), ("stn", "quarter", "unit")
    )
    time = ("quarter", "unit")
    return jax.shard_map(
        per_device,
        mesh=finer,
        in_specs=(
            P("stn", None, time, None, None),
            P("stn", None, time, None),
            P("stn", None, time),
            P(),
            P(),
        ),
        out_specs=P(None, ("stn", "quarter", "unit"), None, None),
        check_vma=False,
    )
```

```python
import math

import jax
import jax.numpy as jnp
import ml_dtypes
import numpy as np
from jax import lax
from jax.experimental import pallas as pl
from jax.experimental.pallas import tpu as pltpu
from jax.sharding import Mesh
from jax.sharding import PartitionSpec as P

S = 16
C = 4096
PERIODS = 8
LAGS = 256
SPP = 128
CB = 32
STN = 8
QUARTERS = 4
UNITS = 8
ITEMS = 4
K = 4
NPOLY = 64
SPECTRA = 2 * K
TILES = ITEMS * SPECTRA + 1
LANES = 128
HALF = LAGS // 2
HIGHEST = lax.Precision.HIGHEST
COSINE = [(-1) ** n * (2 * math.pi) ** (2 * n) / math.factorial(2 * n) for n in range(10)]
SINE = [(-1) ** n * (2 * math.pi) ** (2 * n + 1) / math.factorial(2 * n + 1) for n in range(10)]


def rows_of(shape):
    return lax.broadcasted_iota(jnp.int32, shape, len(shape) - 2)


def lanes_of(shape):
    return lax.broadcasted_iota(jnp.int32, shape, len(shape) - 1)


def turn(delay, index, whole):
    turns = delay * index.astype(jnp.float32) * (1.0 / whole)
    turns = turns - jnp.round(turns)
    square = turns * turns
    cosine = jnp.full_like(square, COSINE[-1])
    for coefficient in COSINE[-2::-1]:
        cosine = cosine * square + coefficient
    sine = jnp.full_like(square, SINE[-1])
    for coefficient in SINE[-2::-1]:
        sine = sine * square + coefficient
    return cosine, sine * turns


def in_hbm(array):
    return pltpu.with_memory_space_constraint(array, pltpu.HBM)


def rotate_kernel(
    place_ref,
    poly_hbm,
    model_hbm,
    flags_hbm,
    x_hbm,
    out_ref,
    poly_ref,
    model_ref,
    flags_ref,
    x_ref,
    turned_re,
    turned_im,
    sems,
    small_sems,
):
    def fetch(p):
        return pltpu.make_async_copy(x_hbm.at[:, p], x_ref.at[p], sems.at[p])

    small = [
        pltpu.make_async_copy(source, target, small_sems.at[number])
        for number, (source, target) in enumerate(
            ((poly_hbm, poly_ref), (model_hbm, model_ref), (flags_hbm, flags_ref))
        )
    ]
    for copy in small:
        copy.start()
    for p in range(PERIODS):
        fetch(p).start()
    for copy in small:
        copy.wait()
    row = rows_of((8, LANES))
    lane = lanes_of((8, LANES))
    across = jnp.zeros((8, LANES), jnp.float32)
    down = []
    for p in range(PERIODS):
        column = jnp.zeros((8, LANES), jnp.float32)
        for s in range(2):
            for k in range(K):
                index = poly_ref[s, k, p]
                time = p * SPP + place_ref[0] % (QUARTERS * UNITS) * K + k
                moment = time.astype(jnp.float32) * (1.0 / (PERIODS * SPP))
                delay = (
                    model_ref[0, index]
                    + model_ref[1, index] * moment
                    + model_ref[2, index] * moment * moment
                )
                column = jnp.where(row == s * K + k, delay, column)
                across = jnp.where(lane == p * SPECTRA + s * K + k, delay, across)
        down.append(column)
    fine_cos, fine_sin = zip(*(turn(column, lane, 2 * C) for column in down))
    weight = 1.0 - flags_ref[...].reshape(2 * PERIODS * K, CB).astype(jnp.float32)
    weight = weight.astype(jnp.bfloat16)
    source = rows_of((2 * PERIODS * K, LANES))
    source_s, source_p, source_k = source // (PERIODS * K), source // K % PERIODS, source % K
    target = lanes_of((2 * PERIODS * K, LANES))

    def spread(chosen):
        return lax.dot_general(
            weight,
            chosen.astype(jnp.bfloat16),
            (((0,), (0,)), ((), ())),
            preferred_element_type=jnp.float32,
        )

    spectrum = source_s * K + source_k
    coarse_weight = spread(
        jnp.where(target == source_p * SPECTRA + spectrum, 1.0, 0.0)
    )
    block = rows_of((CB, LANES))
    cosine, sine = turn(jnp.tile(across, (CB // 8, 1)), block, 2 * CB)
    coarse_cos = coarse_weight * cosine
    coarse_sin = coarse_weight * sine
    held = block % ITEMS == lanes_of((CB, LANES)) // (LANES // ITEMS)
    merge = rows_of((UNITS, CB)) == lanes_of((UNITS, CB)) // ITEMS
    merge = jnp.where(merge, 1.0, 0.0).astype(jnp.bfloat16)
    for p in range(PERIODS):
        mark = jnp.where((source_p == p) & (target % SPECTRA == spectrum), 1.0, 0.0)
        sent = jnp.where(held, spread(mark), 0.0).astype(jnp.bfloat16)
        sent = jnp.dot(merge, sent, preferred_element_type=jnp.float32).astype(jnp.bfloat16)
        fetch(p).wait()
        for s in range(2):
            for k in range(K):
                r = s * K + k
                x = x_ref[p, s, k].astype(jnp.float32)
                re = x[0:1].reshape(CB, LANES)
                im = x[1:2].reshape(CB, LANES)
                at = p * SPECTRA + r
                a_cos = jnp.broadcast_to(coarse_cos[:, at : at + 1], (CB, LANES))
                a_sin = jnp.broadcast_to(coarse_sin[:, at : at + 1], (CB, LANES))
                b_cos = jnp.broadcast_to(fine_cos[p][r : r + 1], (CB, LANES))
                b_sin = jnp.broadcast_to(fine_sin[p][r : r + 1], (CB, LANES))
                cosine = a_cos * b_cos - a_sin * b_sin
                sine = a_sin * b_cos + a_cos * b_sin
                turned_re[p % 2, pl.ds(r, CB, stride=SPECTRA), :] = re * cosine + im * sine
                turned_im[p % 2, pl.ds(r, CB, stride=SPECTRA), :] = im * cosine - re * sine
        for q in range(CB):
            at = slice(q * SPECTRA, (q + 1) * SPECTRA)
            both = jnp.concatenate([turned_re[p % 2, at], turned_im[p % 2, at]])
            tile = q % ITEMS * SPECTRA
            out_ref[p * UNITS + q // ITEMS, tile : tile + SPECTRA] = both.astype(
                jnp.bfloat16
            ).reshape(SPECTRA, 2, LANES)
        out_ref[p * UNITS : (p + 1) * UNITS, TILES - 1] = jnp.broadcast_to(
            sent[:, None, :], (UNITS, 2, LANES)
        )


def rotated_chunks(spectra, flags, poly_index, delay_model, place):
    return pl.pallas_call(
        rotate_kernel,
        in_specs=[pl.BlockSpec(memory_space=pltpu.SMEM)]
        + [pl.BlockSpec(memory_space=pltpu.HBM)] * 4,
        out_specs=pl.BlockSpec(memory_space=pltpu.VMEM),
        out_shape=jax.ShapeDtypeStruct((PERIODS * UNITS, TILES, 2, LANES), jnp.bfloat16),
        scratch_shapes=[
            pltpu.SMEM((2, K, PERIODS), jnp.int32),
            pltpu.SMEM((3, NPOLY), jnp.float32),
            pltpu.VMEM((2, PERIODS, K, CB), jnp.int32),
            pltpu.VMEM((PERIODS, 2, K, 2, C), jnp.bfloat16),
            pltpu.VMEM((2, CB * SPECTRA, LANES), jnp.float32),
            pltpu.VMEM((2, CB * SPECTRA, LANES), jnp.float32),
            pltpu.SemaphoreType.DMA((PERIODS,)),
            pltpu.SemaphoreType.DMA((3,)),
        ],
        compiler_params=pltpu.CompilerParams(vmem_limit_bytes=32 * 2**20),
        name="rotate",
    )(
        place,
        in_hbm(poly_index.transpose(0, 2, 1)),
        in_hbm(delay_model.T),
        in_hbm(flags),
        in_hbm(spectra),
    )


def group_sums(values, group):
    row = rows_of((8, LANES))
    stage = list(values)
    distance = group // 2
    while distance:
        first = row % (2 * distance) < distance
        if 2 * distance == 8:
            stage = [
                jnp.where(first, stage[i], stage[i + distance])
                + pltpu.roll(jnp.where(first, stage[i + distance], stage[i]), 4, 0)
                for i in range(distance)
            ]
        else:
            stage = [
                jnp.where(first, stage[i], stage[i + distance])
                + jnp.where(
                    first,
                    pltpu.roll(stage[i], 8 - distance, 0),
                    pltpu.roll(stage[i + distance], distance, 0),
                )
                for i in range(distance)
            ]
        distance //= 2
    return stage[0]


PAIRS = [(n, m) for n in range(STN) for m in range(n, STN)]


def correlate_kernel(order_ref, y_ref, out_ref, mine_ref, theirs_ref, crossed_ref, tiles, place_ref):
    for j in range(S):
        place_ref[order_ref[j]] = j
    row = rows_of((8, LANES))
    lane = lanes_of((8, LANES))
    zero = jnp.zeros((8, LANES), jnp.float32)

    def finish(n, m, item, sums):
        values = []
        for number, (first, second, third) in enumerate((sums[:3], sums[3:])):
            real = first + third
            imag = zero if n == m and number == 0 else first - second
            values += [real, imag]
        tile = group_sums(values, 4)
        if n == m:
            left = tile - tile.astype(jnp.bfloat16).astype(jnp.float32)
            tile = jnp.where(row % 4 == 1, pltpu.roll(left, 1, 0), tile)
        tiles[PAIRS.index((n, m)), item] = tile

    weights = [
        y_ref[n, :, TILES - 1].astype(jnp.float32)[:, 0, :] for n in range(STN)
    ]
    swapped = [pltpu.roll(weight, K, 1) for weight in weights]
    products = [weights[n] * weights[m] for n, m in PAIRS]
    products += [weights[n] * swapped[m] for n, m in PAIRS]
    counts = [group_sums(products[i : i + 8], 8) for i in range(0, len(products), 8)]

    def count_row(number):
        return counts[number // 8][number % 8 : number % 8 + 1]

    def one_item(item, carry):
        for n in range(STN):
            for u in range(UNITS):
                x = y_ref[n, u, pl.ds(item * SPECTRA, SPECTRA)].reshape(2 * SPECTRA, LANES)
                x = x.astype(jnp.float32)
                re, im = x[:SPECTRA], x[SPECTRA:]
                total, gap = re + im, im - re
                for part, value in enumerate((re, im, total)):
                    mine_ref[n, part, u] = value
                theirs_ref[n, u] = gap
                for part, value in enumerate((re, total, gap)):
                    crossed_ref[n, part, u] = pltpu.roll(value, 4, 0)
        for block_n in range(0, STN, 2):
            for block_m in range(block_n, STN, 2):
                pairs = [
                    (n, m)
                    for n in range(block_n, block_n + 2)
                    for m in range(block_m, block_m + 2)
                    if n <= m
                ]
                sums = {pair: None for pair in pairs}
                for u in range(UNITS):
                    mine = {
                        n: [mine_ref[n, part, u] for part in range(3)]
                        for n in range(block_n, block_n + 2)
                    }
                    theirs = {
                        m: [
                            mine_ref[m, 0, u],
                            mine_ref[m, 2, u],
                            theirs_ref[m, u],
                            *(crossed_ref[m, part, u] for part in range(3)),
                        ]
                        for m in range(block_m, block_m + 2)
                    }
                    for n, m in pairs:
                        re, im, both = mine[n]
                        terms = [
                            f * o
                            for f, o in zip((both, re, im, both, re, im), theirs[m])
                        ]
                        old = sums[n, m]
                        sums[n, m] = (
                            terms if old is None else [x + y for x, y in zip(old, terms)]
                        )
                for n, m in pairs:
                    finish(n, m, item, sums[n, m])
        return carry

    lax.fori_loop(0, ITEMS, one_item, 0)
    conjugate = jnp.where(row % 2 == 0, 1.0, -1.0)
    upper, inner = row < 4, row % 4 < 2
    for number, (n, m) in enumerate(PAIRS):
        t = [tiles[number, item] for item in range(ITEMS)]
        halves = (
            [jnp.where(upper, t[i], pltpu.roll(t[i + 2], 4, 0)) for i in range(2)],
            [jnp.where(upper, pltpu.roll(t[i], 4, 0), t[i + 2]) for i in range(2)],
        )
        for h, (x, y) in enumerate(halves):
            same = jnp.where(inner, x, pltpu.roll(y, 2, 0))
            crossed = jnp.where(inner, pltpu.roll(x, 6, 0), y)
            a = 2 * n + h
            for b, value in ((2 * m + h, same), (2 * m + 1 - h, crossed)):
                out_ref[a * S + place_ref[b], 0:ITEMS] = value.astype(
                    jnp.bfloat16
                ).reshape(ITEMS, 2, LANES)
                if n != m:
                    out_ref[b * S + place_ref[a], 0:ITEMS] = (
                        (value * conjugate).astype(jnp.bfloat16).reshape(ITEMS, 2, LANES)
                    )
        def put(stations, row_of_counts):
            pair_of_rows = jnp.broadcast_to(row_of_counts, (2, LANES)).astype(jnp.bfloat16)
            for a, b in stations:
                out_ref[a * S + place_ref[b], ITEMS] = pair_of_rows

        same, crossed = count_row(number), count_row(len(PAIRS) + number)
        put([(2 * n + h, 2 * m + h) for h in range(2)], same)
        put([(2 * n + h, 2 * m + 1 - h) for h in range(2)], crossed)
        if n != m:
            put([(2 * m + h, 2 * n + h) for h in range(2)], same)
            put([(2 * m + 1 - h, 2 * n + h) for h in range(2)], pltpu.roll(crossed, K, 1))


def correlated(order, arrived):
    return pl.pallas_call(
        correlate_kernel,
        in_specs=[
            pl.BlockSpec(memory_space=pltpu.SMEM),
            pl.BlockSpec(memory_space=pltpu.VMEM),
        ],
        out_specs=pl.BlockSpec(memory_space=pltpu.VMEM),
        out_shape=jax.ShapeDtypeStruct((S * S, ITEMS + 1, 2, LANES), jnp.bfloat16),
        scratch_shapes=[
            pltpu.VMEM((STN, 3, UNITS, 8, LANES), jnp.float32),
            pltpu.VMEM((STN, UNITS, 8, LANES), jnp.float32),
            pltpu.VMEM((STN, 3, UNITS, 8, LANES), jnp.float32),
            pltpu.VMEM((len(PAIRS), ITEMS, 8, LANES), jnp.float32),
            pltpu.SMEM((S,), jnp.int32),
        ],
        compiler_params=pltpu.CompilerParams(vmem_limit_bytes=32 * 2**20),
        name="correlate",
    )(order, arrived.reshape(STN, UNITS, TILES, 2, LANES))


def fringe_tables():
    lag = np.arange(1, HALF + 1)
    fine = 2.0 * np.pi * ((np.arange(LANES)[:, None] * lag) % C) / C
    coarse = 2.0 * np.pi * ((np.arange(CB)[:, None] * lag) % CB) / CB
    period = 2.0 * np.pi * ((np.arange(PERIODS)[:, None] * np.arange(PERIODS)) % PERIODS)
    period = period / PERIODS
    factor = 1.0 / math.sqrt(PERIODS * C)
    flip = np.eye(HALF)[::-1]
    fine = np.concatenate([np.cos(fine), np.sin(fine)], axis=1).astype(np.float32)
    high = fine.astype(ml_dtypes.bfloat16)
    low = (fine - high.astype(np.float32)).astype(ml_dtypes.bfloat16)
    return [np.concatenate([high, high, low])] + [
        np.ascontiguousarray(table, np.float32)
        for table in (
            np.stack([np.cos(coarse), np.sin(coarse)]),
            np.stack([np.cos(period), np.sin(period)]) * factor,
            flip,
        )
    ]


def fringe_kernel(
    place_ref, order_ref, z_ref, fine_ref, coarse_ref, period_ref, flip_ref, out_ref, sums, scales, seen
):
    for p in range(PERIODS):
        for u in range(UNITS):
            parts = [
                z_ref[p, quarter, u, 0:ITEMS].reshape(2 * ITEMS, LANES).astype(jnp.float32)
                for quarter in range(QUARTERS)
            ]
            at = (p * UNITS + u) * 2 * ITEMS
            sums[at : at + 2 * ITEMS] = (parts[0] + parts[1]) + (parts[2] + parts[3])
        seen[p * UNITS : (p + 1) * UNITS] = sum(
            z_ref[p, quarter, :, ITEMS].astype(jnp.float32)[:, 0, :]
            for quarter in range(QUARTERS)
        )
    source, target = rows_of((LANES, LANES)), lanes_of((LANES, LANES))
    wide = LANES // ITEMS
    spectrum = place_ref[0] // S % 2
    added = (source // wide == target // wide) & (source % wide // K == 4 + spectrum)
    counts = jnp.dot(
        seen[...].astype(jnp.bfloat16),
        jnp.where(added, 1.0, 0.0).astype(jnp.bfloat16),
        preferred_element_type=jnp.float32,
    )
    scale = 1.0 / jnp.sqrt(jnp.maximum(counts, 1.0))
    for item in range(ITEMS):
        scales[pl.ds(item, PERIODS * UNITS, stride=ITEMS), :] = jnp.broadcast_to(
            scale[:, item * wide : item * wide + 1], (PERIODS * UNITS, LANES)
        )
    alone = order_ref[place_ref[0] % S] == place_ref[0] // S
    left = jnp.where(alone, 1.0, 0.0)
    first = sums[pl.ds(0, PERIODS * CB, stride=2), :]
    second = sums[pl.ds(1, PERIODS * CB, stride=2), :]
    values = jnp.concatenate(
        [(first + left * second) * scales[...], (second * (1.0 - left)) * scales[...]]
    )
    high = values.astype(jnp.bfloat16)
    low = (values - high.astype(jnp.float32)).astype(jnp.bfloat16)
    both = jnp.dot(
        jnp.concatenate([high, low, high], axis=1),
        fine_ref[...],
        preferred_element_type=jnp.float32,
    )
    re, im = both[: PERIODS * CB], both[PERIODS * CB :]
    parts = [[], [], [], []]
    for p in range(PERIODS):
        sums = [jnp.zeros((8, LANES), jnp.float32)] * 4
        for g in range(CB // 8):
            at = slice(p * CB + g * 8, p * CB + g * 8 + 8)
            re_cos, re_sin = re[at, :HALF], re[at, HALF:]
            im_cos, im_sin = im[at, :HALF], im[at, HALF:]
            cosine = coarse_ref[0, g * 8 : g * 8 + 8, :]
            sine = coarse_ref[1, g * 8 : g * 8 + 8, :]
            plus_re, plus_im = re_cos + im_sin, im_cos - re_sin
            minus_re, minus_im = re_cos - im_sin, im_cos + re_sin
            terms = (
                cosine * minus_re - sine * minus_im,
                cosine * minus_im + sine * minus_re,
                cosine * plus_re + sine * plus_im,
                cosine * plus_im - sine * plus_re,
            )
            sums = [total + term for total, term in zip(sums, terms)]
        for part, total in zip(parts, sums):
            part.append(total)
    minus_re, minus_im, plus_re, plus_im = (group_sums(part, 8) for part in parts)
    reversed_ = jnp.dot(
        jnp.concatenate([minus_re, minus_im]),
        flip_ref[...],
        precision=HIGHEST,
        preferred_element_type=jnp.float32,
    )
    real = jnp.concatenate([reversed_[:8], plus_re], axis=1)
    imag = jnp.concatenate([reversed_[8:], plus_im], axis=1)
    cosine, sine = period_ref[0], period_ref[1]

    def turn(a, b):
        return jnp.dot(a, b, precision=HIGHEST, preferred_element_type=jnp.float32)

    out_ref[0, 0] = turn(cosine, real) + turn(sine, imag)
    out_ref[1, 0] = turn(cosine, imag) - turn(sine, real)


def fringed(place, order, owned):
    return pl.pallas_call(
        fringe_kernel,
        in_specs=[pl.BlockSpec(memory_space=pltpu.SMEM)] * 2
        + [pl.BlockSpec(memory_space=pltpu.VMEM)] * 5,
        out_specs=pl.BlockSpec(memory_space=pltpu.VMEM),
        out_shape=jax.ShapeDtypeStruct((2, 1, PERIODS, LAGS), jnp.float32),
        scratch_shapes=[
            pltpu.VMEM((PERIODS * CB * 2, LANES), jnp.float32),
            pltpu.VMEM((PERIODS * CB, LANES), jnp.float32),
            pltpu.VMEM((PERIODS * UNITS, LANES), jnp.float32),
        ],
        compiler_params=pltpu.CompilerParams(vmem_limit_bytes=32 * 2**20),
        name="fringe",
    )(
        place,
        order,
        owned.reshape(PERIODS, QUARTERS, UNITS, ITEMS + 1, 2, LANES),
        *fringe_tables(),
    )


def per_device(spectra, flags, poly_index, delay_model, partner_order):
    plane = ("stn", "unit")
    everyone = ("stn", "quarter", "unit")
    row = lax.axis_index(everyone).astype(jnp.int32)
    place = row.reshape(1)
    chunks = rotated_chunks(spectra, flags, poly_index, delay_model, place)
    arrived = lax.all_to_all(chunks, plane, split_axis=0, concat_axis=0, tiled=True)
    rows = correlated(partner_order, arrived)
    owned = lax.all_to_all(rows, everyone, split_axis=0, concat_axis=0, tiled=True)
    return fringed(place, partner_order, owned)


def solution(mesh):
    finer = Mesh(
        mesh.devices.reshape(STN, QUARTERS, UNITS), ("stn", "quarter", "unit")
    )
    time = ("quarter", "unit")
    return jax.shard_map(
        per_device,
        mesh=finer,
        in_specs=(
            P("stn", None, time, None, None),
            P("stn", None, time, None),
            P("stn", None, time),
            P(),
            P(),
        ),
        out_specs=P(None, ("stn", "quarter", "unit"), None, None),
        check_vma=False,
    )
```

```python
import math

import jax
import jax.numpy as jnp
import ml_dtypes
import numpy as np
from jax import lax
from jax.experimental import pallas as pl
from jax.experimental.pallas import tpu as pltpu
from jax.sharding import Mesh
from jax.sharding import PartitionSpec as P

S = 16
C = 4096
PERIODS = 8
LAGS = 256
SPP = 128
CB = 32
STN = 8
QUARTERS = 4
UNITS = 8
ITEMS = 4
K = 4
NPOLY = 64
SPECTRA = 2 * K
TILES = ITEMS * SPECTRA + 1
LANES = 128
HALF = LAGS // 2
HIGHEST = lax.Precision.HIGHEST
COSINE = [(-1) ** n * (2 * math.pi) ** (2 * n) / math.factorial(2 * n) for n in range(10)]
SINE = [(-1) ** n * (2 * math.pi) ** (2 * n + 1) / math.factorial(2 * n + 1) for n in range(10)]


def rows_of(shape):
    return lax.broadcasted_iota(jnp.int32, shape, len(shape) - 2)


def lanes_of(shape):
    return lax.broadcasted_iota(jnp.int32, shape, len(shape) - 1)


def turn(delay, index, whole):
    turns = delay * index.astype(jnp.float32) * (1.0 / whole)
    turns = turns - jnp.round(turns)
    square = turns * turns
    cosine = jnp.full_like(square, COSINE[-1])
    for coefficient in COSINE[-2::-1]:
        cosine = cosine * square + coefficient
    sine = jnp.full_like(square, SINE[-1])
    for coefficient in SINE[-2::-1]:
        sine = sine * square + coefficient
    return cosine, sine * turns


def in_hbm(array):
    return pltpu.with_memory_space_constraint(array, pltpu.HBM)


def rotate_kernel(
    place_ref,
    poly_hbm,
    model_hbm,
    flags_hbm,
    x_hbm,
    out_ref,
    poly_ref,
    model_ref,
    flags_ref,
    x_ref,
    turned_re,
    turned_im,
    sems,
):
    small = [
        pltpu.make_async_copy(source, target, sems.at[number])
        for number, (source, target) in enumerate(
            ((poly_hbm, poly_ref), (model_hbm, model_ref), (flags_hbm, flags_ref))
        )
    ]
    for copy in small:
        copy.start()
    fetch = pltpu.make_async_copy(x_hbm, x_ref, sems.at[3])
    fetch.start()
    for copy in small:
        copy.wait()
    row = rows_of((8, LANES))
    lane = lanes_of((8, LANES))
    across = jnp.zeros((8, LANES), jnp.float32)
    down = []
    for p in range(PERIODS):
        column = jnp.zeros((8, LANES), jnp.float32)
        for s in range(2):
            for k in range(K):
                index = poly_ref[s, k, p]
                time = p * SPP + place_ref[0] % (QUARTERS * UNITS) * K + k
                moment = time.astype(jnp.float32) * (1.0 / (PERIODS * SPP))
                delay = (
                    model_ref[0, index]
                    + model_ref[1, index] * moment
                    + model_ref[2, index] * moment * moment
                )
                column = jnp.where(row == s * K + k, delay, column)
                across = jnp.where(lane == p * SPECTRA + s * K + k, delay, across)
        down.append(column)
    fine_cos, fine_sin = zip(*(turn(column, lane, 2 * C) for column in down))
    weight = 1.0 - flags_ref[...].reshape(2 * PERIODS * K, CB).astype(jnp.float32)
    weight = weight.astype(jnp.bfloat16)
    source = rows_of((2 * PERIODS * K, LANES))
    source_s, source_p, source_k = source // (PERIODS * K), source // K % PERIODS, source % K
    target = lanes_of((2 * PERIODS * K, LANES))

    def spread(chosen):
        return lax.dot_general(
            weight,
            chosen.astype(jnp.bfloat16),
            (((0,), (0,)), ((), ())),
            preferred_element_type=jnp.float32,
        )

    spectrum = source_s * K + source_k
    coarse_weight = spread(
        jnp.where(target == source_p * SPECTRA + spectrum, 1.0, 0.0)
    )
    block = rows_of((CB, LANES))
    cosine, sine = turn(jnp.tile(across, (CB // 8, 1)), block, 2 * CB)
    coarse_cos = coarse_weight * cosine
    coarse_sin = coarse_weight * sine
    held = block % ITEMS == lanes_of((CB, LANES)) // (LANES // ITEMS)
    merge = rows_of((UNITS, CB)) == lanes_of((UNITS, CB)) // ITEMS
    merge = jnp.where(merge, 1.0, 0.0).astype(jnp.bfloat16)
    for p in range(PERIODS):
        mark = jnp.where((source_p == p) & (target % SPECTRA == spectrum), 1.0, 0.0)
        sent = jnp.where(held, spread(mark), 0.0).astype(jnp.bfloat16)
        sent = jnp.dot(merge, sent, preferred_element_type=jnp.float32).astype(jnp.bfloat16)
        if p == 0:
            fetch.wait()
        for s in range(2):
            for k in range(K):
                r = s * K + k
                x = x_ref[s, p, k].astype(jnp.float32)
                re = x[0:1].reshape(CB, LANES)
                im = x[1:2].reshape(CB, LANES)
                at = p * SPECTRA + r
                a_cos = jnp.broadcast_to(coarse_cos[:, at : at + 1], (CB, LANES))
                a_sin = jnp.broadcast_to(coarse_sin[:, at : at + 1], (CB, LANES))
                b_cos = jnp.broadcast_to(fine_cos[p][r : r + 1], (CB, LANES))
                b_sin = jnp.broadcast_to(fine_sin[p][r : r + 1], (CB, LANES))
                cosine = a_cos * b_cos - a_sin * b_sin
                sine = a_sin * b_cos + a_cos * b_sin
                turned_re[p % 2, pl.ds(r, CB, stride=SPECTRA), :] = re * cosine + im * sine
                turned_im[p % 2, pl.ds(r, CB, stride=SPECTRA), :] = im * cosine - re * sine
        for q in range(CB):
            at = slice(q * SPECTRA, (q + 1) * SPECTRA)
            both = jnp.concatenate([turned_re[p % 2, at], turned_im[p % 2, at]])
            tile = q % ITEMS * SPECTRA
            out_ref[p * UNITS + q // ITEMS, tile : tile + SPECTRA] = both.astype(
                jnp.bfloat16
            ).reshape(SPECTRA, 2, LANES)
        out_ref[p * UNITS : (p + 1) * UNITS, TILES - 1] = jnp.broadcast_to(
            sent[:, None, :], (UNITS, 2, LANES)
        )


def rotated_chunks(spectra, flags, poly_index, delay_model, place):
    return pl.pallas_call(
        rotate_kernel,
        in_specs=[pl.BlockSpec(memory_space=pltpu.SMEM)]
        + [pl.BlockSpec(memory_space=pltpu.HBM)] * 4,
        out_specs=pl.BlockSpec(memory_space=pltpu.VMEM),
        out_shape=jax.ShapeDtypeStruct((PERIODS * UNITS, TILES, 2, LANES), jnp.bfloat16),
        scratch_shapes=[
            pltpu.SMEM((2, K, PERIODS), jnp.int32),
            pltpu.SMEM((3, NPOLY), jnp.float32),
            pltpu.VMEM((2, PERIODS, K, CB), jnp.int32),
            pltpu.VMEM((2, PERIODS, K, 2, C), jnp.bfloat16),
            pltpu.VMEM((2, CB * SPECTRA, LANES), jnp.float32),
            pltpu.VMEM((2, CB * SPECTRA, LANES), jnp.float32),
            pltpu.SemaphoreType.DMA((4,)),
        ],
        compiler_params=pltpu.CompilerParams(vmem_limit_bytes=32 * 2**20),
        name="rotate",
    )(
        place,
        in_hbm(poly_index.transpose(0, 2, 1)),
        in_hbm(delay_model.T),
        in_hbm(flags),
        in_hbm(spectra),
    )


def group_sums(values, group):
    row = rows_of((8, LANES))
    stage = list(values)
    distance = group // 2
    while distance:
        first = row % (2 * distance) < distance
        if 2 * distance == 8:
            stage = [
                jnp.where(first, stage[i], stage[i + distance])
                + pltpu.roll(jnp.where(first, stage[i + distance], stage[i]), 4, 0)
                for i in range(distance)
            ]
        else:
            stage = [
                jnp.where(first, stage[i], stage[i + distance])
                + jnp.where(
                    first,
                    pltpu.roll(stage[i], 8 - distance, 0),
                    pltpu.roll(stage[i + distance], distance, 0),
                )
                for i in range(distance)
            ]
        distance //= 2
    return stage[0]


PAIRS = [(n, m) for n in range(STN) for m in range(n, STN)]


def correlate_kernel(order_ref, y_ref, out_ref, mine_ref, theirs_ref, crossed_ref, tiles, place_ref):
    for j in range(S):
        place_ref[order_ref[j]] = j
    row = rows_of((8, LANES))
    lane = lanes_of((8, LANES))
    zero = jnp.zeros((8, LANES), jnp.float32)

    def finish(n, m, item, sums):
        values = []
        for number, (first, second, third) in enumerate((sums[:3], sums[3:])):
            real = first + third
            imag = zero if n == m and number == 0 else first - second
            values += [real, imag]
        tile = group_sums(values, 4)
        if n == m:
            left = tile - tile.astype(jnp.bfloat16).astype(jnp.float32)
            tile = jnp.where(row % 4 == 1, pltpu.roll(left, 1, 0), tile)
        tiles[PAIRS.index((n, m)), item] = tile

    weights = [
        y_ref[n, :, TILES - 1].astype(jnp.float32)[:, 0, :] for n in range(STN)
    ]
    swapped = [pltpu.roll(weight, K, 1) for weight in weights]
    products = [weights[n] * weights[m] for n, m in PAIRS]
    products += [weights[n] * swapped[m] for n, m in PAIRS]
    counts = [group_sums(products[i : i + 8], 8) for i in range(0, len(products), 8)]

    def count_row(number):
        return counts[number // 8][number % 8 : number % 8 + 1]

    def one_item(item, carry):
        for n in range(STN):
            for u in range(UNITS):
                x = y_ref[n, u, pl.ds(item * SPECTRA, SPECTRA)].reshape(2 * SPECTRA, LANES)
                x = x.astype(jnp.float32)
                re, im = x[:SPECTRA], x[SPECTRA:]
                total, gap = re + im, im - re
                for part, value in enumerate((re, im, total)):
                    mine_ref[n, part, u] = value
                theirs_ref[n, u] = gap
                re, im = pltpu.roll(re, 4, 0), pltpu.roll(im, 4, 0)
                for part, value in enumerate((re, re + im, im - re)):
                    crossed_ref[n, part, u] = value
        for block_n in range(0, STN, 2):
            for block_m in range(block_n, STN, 2):
                pairs = [
                    (n, m)
                    for n in range(block_n, block_n + 2)
                    for m in range(block_m, block_m + 2)
                    if n <= m
                ]
                sums = {pair: None for pair in pairs}
                for u in range(UNITS):
                    mine = {
                        n: [mine_ref[n, part, u] for part in range(3)]
                        for n in range(block_n, block_n + 2)
                    }
                    theirs = {
                        m: [
                            mine_ref[m, 0, u],
                            mine_ref[m, 2, u],
                            theirs_ref[m, u],
                            *(crossed_ref[m, part, u] for part in range(3)),
                        ]
                        for m in range(block_m, block_m + 2)
                    }
                    for n, m in pairs:
                        re, im, both = mine[n]
                        terms = [
                            f * o
                            for f, o in zip((both, re, im, both, re, im), theirs[m])
                        ]
                        old = sums[n, m]
                        sums[n, m] = (
                            terms if old is None else [x + y for x, y in zip(old, terms)]
                        )
                for n, m in pairs:
                    finish(n, m, item, sums[n, m])
        return carry

    lax.fori_loop(0, ITEMS, one_item, 0)
    conjugate = jnp.where(row % 2 == 0, 1.0, -1.0)
    upper, inner = row < 4, row % 4 < 2
    for number, (n, m) in enumerate(PAIRS):
        t = [tiles[number, item] for item in range(ITEMS)]
        halves = (
            [jnp.where(upper, t[i], pltpu.roll(t[i + 2], 4, 0)) for i in range(2)],
            [jnp.where(upper, pltpu.roll(t[i], 4, 0), t[i + 2]) for i in range(2)],
        )
        for h, (x, y) in enumerate(halves):
            same = jnp.where(inner, x, pltpu.roll(y, 2, 0))
            crossed = jnp.where(inner, pltpu.roll(x, 6, 0), y)
            a = 2 * n + h
            for b, value in ((2 * m + h, same), (2 * m + 1 - h, crossed)):
                out_ref[a * S + place_ref[b], 0:ITEMS] = value.astype(
                    jnp.bfloat16
                ).reshape(ITEMS, 2, LANES)
                if n != m:
                    out_ref[b * S + place_ref[a], 0:ITEMS] = (
                        (value * conjugate).astype(jnp.bfloat16).reshape(ITEMS, 2, LANES)
                    )
        def put(stations, row_of_counts):
            pair_of_rows = jnp.broadcast_to(row_of_counts, (2, LANES)).astype(jnp.bfloat16)
            for a, b in stations:
                out_ref[a * S + place_ref[b], ITEMS] = pair_of_rows

        same, crossed = count_row(number), count_row(len(PAIRS) + number)
        put([(2 * n + h, 2 * m + h) for h in range(2)], same)
        put([(2 * n + h, 2 * m + 1 - h) for h in range(2)], crossed)
        if n != m:
            put([(2 * m + h, 2 * n + h) for h in range(2)], same)
            put([(2 * m + 1 - h, 2 * n + h) for h in range(2)], pltpu.roll(crossed, K, 1))


def correlated(order, arrived):
    return pl.pallas_call(
        correlate_kernel,
        in_specs=[
            pl.BlockSpec(memory_space=pltpu.SMEM),
            pl.BlockSpec(memory_space=pltpu.VMEM),
        ],
        out_specs=pl.BlockSpec(memory_space=pltpu.VMEM),
        out_shape=jax.ShapeDtypeStruct((S * S, ITEMS + 1, 2, LANES), jnp.bfloat16),
        scratch_shapes=[
            pltpu.VMEM((STN, 3, UNITS, 8, LANES), jnp.float32),
            pltpu.VMEM((STN, UNITS, 8, LANES), jnp.float32),
            pltpu.VMEM((STN, 3, UNITS, 8, LANES), jnp.float32),
            pltpu.VMEM((len(PAIRS), ITEMS, 8, LANES), jnp.float32),
            pltpu.SMEM((S,), jnp.int32),
        ],
        compiler_params=pltpu.CompilerParams(vmem_limit_bytes=32 * 2**20),
        name="correlate",
    )(order, arrived.reshape(STN, UNITS, TILES, 2, LANES))


def fringe_tables():
    lag = np.arange(1, HALF + 1)
    fine = 2.0 * np.pi * ((np.arange(LANES)[:, None] * lag) % C) / C
    coarse = 2.0 * np.pi * ((np.arange(CB)[:, None] * lag) % CB) / CB
    period = 2.0 * np.pi * ((np.arange(PERIODS)[:, None] * np.arange(PERIODS)) % PERIODS)
    period = period / PERIODS
    factor = 1.0 / math.sqrt(PERIODS * C)
    flip = np.eye(HALF)[::-1]
    fine = np.concatenate([np.cos(fine), np.sin(fine)], axis=1).astype(np.float32)
    high = fine.astype(ml_dtypes.bfloat16)
    low = (fine - high.astype(np.float32)).astype(ml_dtypes.bfloat16)
    return [np.concatenate([high, high, low])] + [
        np.ascontiguousarray(table, np.float32)
        for table in (
            np.stack([np.cos(coarse), np.sin(coarse)]),
            np.stack([np.cos(period), np.sin(period)]) * factor,
            flip,
        )
    ]


def fringe_kernel(
    place_ref, order_ref, z_ref, fine_ref, coarse_ref, period_ref, flip_ref, out_ref, sums, scales, seen
):
    for p in range(PERIODS):
        for u in range(UNITS):
            parts = [
                z_ref[p, quarter, u, 0:ITEMS].reshape(2 * ITEMS, LANES).astype(jnp.float32)
                for quarter in range(QUARTERS)
            ]
            at = (p * UNITS + u) * 2 * ITEMS
            sums[at : at + 2 * ITEMS] = (parts[0] + parts[1]) + (parts[2] + parts[3])
        seen[p * UNITS : (p + 1) * UNITS] = sum(
            z_ref[p, quarter, :, ITEMS].astype(jnp.float32)[:, 0, :]
            for quarter in range(QUARTERS)
        )
    source, target = rows_of((LANES, LANES)), lanes_of((LANES, LANES))
    wide = LANES // ITEMS
    spectrum = place_ref[0] // S % 2
    added = (source // wide == target // wide) & (source % wide // K == 4 + spectrum)
    counts = jnp.dot(
        seen[...].astype(jnp.bfloat16),
        jnp.where(added, 1.0, 0.0).astype(jnp.bfloat16),
        preferred_element_type=jnp.float32,
    )
    scale = 1.0 / jnp.sqrt(jnp.maximum(counts, 1.0))
    for item in range(ITEMS):
        scales[pl.ds(item, PERIODS * UNITS, stride=ITEMS), :] = jnp.broadcast_to(
            scale[:, item * wide : item * wide + 1], (PERIODS * UNITS, LANES)
        )
    alone = order_ref[place_ref[0] % S] == place_ref[0] // S
    left = jnp.where(alone, 1.0, 0.0)
    first = sums[pl.ds(0, PERIODS * CB, stride=2), :]
    second = sums[pl.ds(1, PERIODS * CB, stride=2), :]
    values = jnp.concatenate(
        [(first + left * second) * scales[...], (second * (1.0 - left)) * scales[...]]
    )
    high = values.astype(jnp.bfloat16)
    low = (values - high.astype(jnp.float32)).astype(jnp.bfloat16)
    both = jnp.dot(
        jnp.concatenate([high, low, high], axis=1),
        fine_ref[...],
        preferred_element_type=jnp.float32,
    )
    re, im = both[: PERIODS * CB], both[PERIODS * CB :]
    parts = [[], [], [], []]
    for p in range(PERIODS):
        sums = [jnp.zeros((8, LANES), jnp.float32)] * 4
        for g in range(CB // 8):
            at = slice(p * CB + g * 8, p * CB + g * 8 + 8)
            re_cos, re_sin = re[at, :HALF], re[at, HALF:]
            im_cos, im_sin = im[at, :HALF], im[at, HALF:]
            cosine = coarse_ref[0, g * 8 : g * 8 + 8, :]
            sine = coarse_ref[1, g * 8 : g * 8 + 8, :]
            plus_re, plus_im = re_cos + im_sin, im_cos - re_sin
            minus_re, minus_im = re_cos - im_sin, im_cos + re_sin
            terms = (
                cosine * minus_re - sine * minus_im,
                cosine * minus_im + sine * minus_re,
                cosine * plus_re + sine * plus_im,
                cosine * plus_im - sine * plus_re,
            )
            sums = [total + term for total, term in zip(sums, terms)]
        for part, total in zip(parts, sums):
            part.append(total)
    minus_re, minus_im, plus_re, plus_im = (group_sums(part, 8) for part in parts)
    reversed_ = jnp.dot(
        jnp.concatenate([minus_re, minus_im]),
        flip_ref[...],
        precision=HIGHEST,
        preferred_element_type=jnp.float32,
    )
    real = jnp.concatenate([reversed_[:8], plus_re], axis=1)
    imag = jnp.concatenate([reversed_[8:], plus_im], axis=1)
    cosine, sine = period_ref[0], period_ref[1]

    def turn(a, b):
        return jnp.dot(a, b, precision=HIGHEST, preferred_element_type=jnp.float32)

    out_ref[0, 0] = turn(cosine, real) + turn(sine, imag)
    out_ref[1, 0] = turn(cosine, imag) - turn(sine, real)


def fringed(place, order, owned):
    return pl.pallas_call(
        fringe_kernel,
        in_specs=[pl.BlockSpec(memory_space=pltpu.SMEM)] * 2
        + [pl.BlockSpec(memory_space=pltpu.VMEM)] * 5,
        out_specs=pl.BlockSpec(memory_space=pltpu.VMEM),
        out_shape=jax.ShapeDtypeStruct((2, 1, PERIODS, LAGS), jnp.float32),
        scratch_shapes=[
            pltpu.VMEM((PERIODS * CB * 2, LANES), jnp.float32),
            pltpu.VMEM((PERIODS * CB, LANES), jnp.float32),
            pltpu.VMEM((PERIODS * UNITS, LANES), jnp.float32),
        ],
        compiler_params=pltpu.CompilerParams(vmem_limit_bytes=32 * 2**20),
        name="fringe",
    )(
        place,
        order,
        owned.reshape(PERIODS, QUARTERS, UNITS, ITEMS + 1, 2, LANES),
        *fringe_tables(),
    )


def per_device(spectra, flags, poly_index, delay_model, partner_order):
    plane = ("stn", "unit")
    everyone = ("stn", "quarter", "unit")
    row = lax.axis_index(everyone).astype(jnp.int32)
    place = row.reshape(1)
    chunks = rotated_chunks(spectra, flags, poly_index, delay_model, place)
    arrived = lax.all_to_all(chunks, plane, split_axis=0, concat_axis=0, tiled=True)
    rows = correlated(partner_order, arrived)
    owned = lax.all_to_all(rows, everyone, split_axis=0, concat_axis=0, tiled=True)
    return fringed(place, partner_order, owned)


def solution(mesh):
    finer = Mesh(
        mesh.devices.reshape(STN, QUARTERS, UNITS), ("stn", "quarter", "unit")
    )
    time = ("quarter", "unit")
    return jax.shard_map(
        per_device,
        mesh=finer,
        in_specs=(
            P("stn", None, time, None, None),
            P("stn", None, time, None),
            P("stn", None, time),
            P(),
            P(),
        ),
        out_specs=P(None, ("stn", "quarter", "unit"), None, None),
        check_vma=False,
    )
```

```python
import math

import jax
import jax.numpy as jnp
import ml_dtypes
import numpy as np
from jax import lax
from jax.experimental import pallas as pl
from jax.experimental.pallas import tpu as pltpu
from jax.sharding import Mesh
from jax.sharding import PartitionSpec as P

S = 16
C = 4096
PERIODS = 8
LAGS = 256
SPP = 128
CB = 32
STN = 8
QUARTERS = 4
UNITS = 8
ITEMS = 4
K = 4
NPOLY = 64
SPECTRA = 2 * K
TILES = ITEMS * SPECTRA + 1
LANES = 128
HALF = LAGS // 2
HIGHEST = lax.Precision.HIGHEST
COSINE = [(-1) ** n * (2 * math.pi) ** (2 * n) / math.factorial(2 * n) for n in range(10)]
SINE = [(-1) ** n * (2 * math.pi) ** (2 * n + 1) / math.factorial(2 * n + 1) for n in range(10)]


def rows_of(shape):
    return lax.broadcasted_iota(jnp.int32, shape, len(shape) - 2)


def lanes_of(shape):
    return lax.broadcasted_iota(jnp.int32, shape, len(shape) - 1)


def turn(delay, index, whole):
    turns = delay * index.astype(jnp.float32) * (1.0 / whole)
    turns = turns - jnp.round(turns)
    square = turns * turns
    cosine = jnp.full_like(square, COSINE[-1])
    for coefficient in COSINE[-2::-1]:
        cosine = cosine * square + coefficient
    sine = jnp.full_like(square, SINE[-1])
    for coefficient in SINE[-2::-1]:
        sine = sine * square + coefficient
    return cosine, sine * turns


def in_hbm(array):
    return pltpu.with_memory_space_constraint(array, pltpu.HBM)


def rotate_kernel(
    place_ref,
    poly_hbm,
    model_hbm,
    flags_hbm,
    x_hbm,
    out_ref,
    poly_ref,
    model_ref,
    flags_ref,
    x_ref,
    turned_re,
    turned_im,
    sems,
):
    small = [
        pltpu.make_async_copy(source, target, sems.at[number])
        for number, (source, target) in enumerate(
            ((poly_hbm, poly_ref), (model_hbm, model_ref), (flags_hbm, flags_ref))
        )
    ]
    for copy in small:
        copy.start()
    fetch = pltpu.make_async_copy(x_hbm, x_ref, sems.at[3])
    fetch.start()
    for copy in small:
        copy.wait()
    row = rows_of((8, LANES))
    lane = lanes_of((8, LANES))
    across = jnp.zeros((8, LANES), jnp.float32)
    down = []
    for p in range(PERIODS):
        column = jnp.zeros((8, LANES), jnp.float32)
        for s in range(2):
            for k in range(K):
                index = poly_ref[s, k, p]
                time = p * SPP + place_ref[0] % (QUARTERS * UNITS) * K + k
                moment = time.astype(jnp.float32) * (1.0 / (PERIODS * SPP))
                delay = (
                    model_ref[0, index]
                    + model_ref[1, index] * moment
                    + model_ref[2, index] * moment * moment
                )
                column = jnp.where(row == s * K + k, delay, column)
                across = jnp.where(lane == p * SPECTRA + s * K + k, delay, across)
        down.append(column)
    fine_cos, fine_sin = zip(*(turn(column, lane, 2 * C) for column in down))
    weight = 1.0 - flags_ref[...].reshape(2 * PERIODS * K, CB).astype(jnp.float32)
    weight = weight.astype(jnp.bfloat16)
    source = rows_of((2 * PERIODS * K, LANES))
    source_s, source_p, source_k = source // (PERIODS * K), source // K % PERIODS, source % K
    target = lanes_of((2 * PERIODS * K, LANES))

    def spread(chosen):
        return lax.dot_general(
            weight,
            chosen.astype(jnp.bfloat16),
            (((0,), (0,)), ((), ())),
            preferred_element_type=jnp.float32,
        )

    spectrum = source_s * K + source_k
    coarse_weight = spread(
        jnp.where(target == source_p * SPECTRA + spectrum, 1.0, 0.0)
    )
    block = rows_of((CB, LANES))
    cosine, sine = turn(jnp.tile(across, (CB // 8, 1)), block, 2 * CB)
    coarse_cos = coarse_weight * cosine
    coarse_sin = coarse_weight * sine
    held = block % ITEMS == lanes_of((CB, LANES)) // (LANES // ITEMS)
    merge = rows_of((UNITS, CB)) == lanes_of((UNITS, CB)) // ITEMS
    merge = jnp.where(merge, 1.0, 0.0).astype(jnp.bfloat16)
    for p in range(PERIODS):
        mark = jnp.where((source_p == p) & (target % SPECTRA == spectrum), 1.0, 0.0)
        sent = jnp.where(held, spread(mark), 0.0).astype(jnp.bfloat16)
        sent = jnp.dot(merge, sent, preferred_element_type=jnp.float32).astype(jnp.bfloat16)
        if p == 0:
            fetch.wait()
        for s in range(2):
            for k in range(K):
                r = s * K + k
                x = x_ref[s, p, k].astype(jnp.float32)
                re = x[0:1].reshape(CB, LANES)
                im = x[1:2].reshape(CB, LANES)
                at = p * SPECTRA + r
                a_cos = jnp.broadcast_to(coarse_cos[:, at : at + 1], (CB, LANES))
                a_sin = jnp.broadcast_to(coarse_sin[:, at : at + 1], (CB, LANES))
                b_cos = jnp.broadcast_to(fine_cos[p][r : r + 1], (CB, LANES))
                b_sin = jnp.broadcast_to(fine_sin[p][r : r + 1], (CB, LANES))
                cosine = a_cos * b_cos - a_sin * b_sin
                sine = a_sin * b_cos + a_cos * b_sin
                turned_re[p % 2, pl.ds(r, CB, stride=SPECTRA), :] = re * cosine + im * sine
                turned_im[p % 2, pl.ds(r, CB, stride=SPECTRA), :] = im * cosine - re * sine
        for q in range(CB):
            at = slice(q * SPECTRA, (q + 1) * SPECTRA)
            both = jnp.concatenate([turned_re[p % 2, at], turned_im[p % 2, at]])
            tile = q % ITEMS * SPECTRA
            out_ref[p * UNITS + q // ITEMS, tile : tile + SPECTRA] = both.astype(
                jnp.bfloat16
            ).reshape(SPECTRA, 2, LANES)
        out_ref[p * UNITS : (p + 1) * UNITS, TILES - 1] = jnp.broadcast_to(
            sent[:, None, :], (UNITS, 2, LANES)
        )


def rotated_chunks(spectra, flags, poly_index, delay_model, place):
    return pl.pallas_call(
        rotate_kernel,
        in_specs=[pl.BlockSpec(memory_space=pltpu.SMEM)]
        + [pl.BlockSpec(memory_space=pltpu.HBM)] * 4,
        out_specs=pl.BlockSpec(memory_space=pltpu.VMEM),
        out_shape=jax.ShapeDtypeStruct((PERIODS * UNITS, TILES, 2, LANES), jnp.bfloat16),
        scratch_shapes=[
            pltpu.SMEM((2, K, PERIODS), jnp.int32),
            pltpu.SMEM((3, NPOLY), jnp.float32),
            pltpu.VMEM((2, PERIODS, K, CB), jnp.int32),
            pltpu.VMEM((2, PERIODS, K, 2, C), jnp.bfloat16),
            pltpu.VMEM((2, CB * SPECTRA, LANES), jnp.float32),
            pltpu.VMEM((2, CB * SPECTRA, LANES), jnp.float32),
            pltpu.SemaphoreType.DMA((4,)),
        ],
        compiler_params=pltpu.CompilerParams(vmem_limit_bytes=32 * 2**20),
        name="rotate",
    )(
        place,
        in_hbm(poly_index.transpose(0, 2, 1)),
        in_hbm(delay_model.T),
        in_hbm(flags),
        in_hbm(spectra),
    )


def group_sums(values, group):
    row = rows_of((8, LANES))
    stage = list(values)
    distance = group // 2
    while distance:
        first = row % (2 * distance) < distance
        if 2 * distance == 8:
            stage = [
                jnp.where(first, stage[i], stage[i + distance])
                + pltpu.roll(jnp.where(first, stage[i + distance], stage[i]), 4, 0)
                for i in range(distance)
            ]
        else:
            stage = [
                jnp.where(first, stage[i], stage[i + distance])
                + jnp.where(
                    first,
                    pltpu.roll(stage[i], 8 - distance, 0),
                    pltpu.roll(stage[i + distance], distance, 0),
                )
                for i in range(distance)
            ]
        distance //= 2
    return stage[0]


PAIRS = [(n, m) for n in range(STN) for m in range(n, STN)]


def correlate_kernel(order_ref, y_ref, out_ref, mine_ref, crossed_ref, tiles, place_ref):
    for j in range(S):
        place_ref[order_ref[j]] = j
    row = rows_of((8, LANES))
    lane = lanes_of((8, LANES))
    zero = jnp.zeros((8, LANES), jnp.float32)

    def finish(n, m, item, sums):
        if n == m:
            values = [sums[0] + sums[1], zero]
        else:
            values = [sums[0] + sums[2], sums[0] - sums[1]]
        values += [sums[-3] + sums[-1], sums[-3] - sums[-2]]
        tile = group_sums(values, 4)
        if n == m:
            left = tile - tile.astype(jnp.bfloat16).astype(jnp.float32)
            tile = jnp.where(row % 4 == 1, pltpu.roll(left, 1, 0), tile)
        tiles[PAIRS.index((n, m)), item] = tile

    weights = [
        y_ref[n, :, TILES - 1].astype(jnp.float32)[:, 0, :] for n in range(STN)
    ]
    swapped = [pltpu.roll(weight, K, 1) for weight in weights]
    products = []
    for n, m in PAIRS:
        products += [weights[n] * weights[m], weights[n] * swapped[m]]
    counts = [
        group_sums(products[i : i + 8], 8).astype(jnp.bfloat16)
        for i in range(0, len(products), 8)
    ]

    def one_item(item, carry):
        for n in range(STN):
            for u in range(UNITS):
                x = y_ref[n, u, pl.ds(item * SPECTRA, SPECTRA)].reshape(2 * SPECTRA, LANES)
                x = x.astype(jnp.float32)
                re, im = x[:SPECTRA], x[SPECTRA:]
                for part, value in enumerate((re, im)):
                    mine_ref[n, part, u] = value
                    crossed_ref[n, part, u] = pltpu.roll(value, 4, 0)
        for block_n in range(0, STN, 2):
            for block_m in range(block_n - block_n % 2, STN, 2):
                pairs = [
                    (n, m)
                    for n in range(block_n, block_n + 2)
                    for m in range(block_m, block_m + 2)
                    if n <= m
                ]
                sums = {}
                for u in range(UNITS):
                    mine, theirs = {}, {}
                    for n in range(block_n, block_n + 2):
                        re, im = mine_ref[n, 0, u], mine_ref[n, 1, u]
                        mine[n] = re, im, re + im
                    for m in range(block_m, block_m + 2):
                        for number, ref in enumerate((mine_ref, crossed_ref)):
                            re, im = ref[m, 0, u], ref[m, 1, u]
                            theirs[m, number] = re, re + im, im - re
                    for n, m in pairs:
                        re, im, both = mine[n]
                        terms = []
                        for number in range(2):
                            their_re, their_both, their_gap = theirs[m, number]
                            if n == m and not number:
                                terms += [re * re, im * im]
                            else:
                                terms += [both * their_re, re * their_both, im * their_gap]
                        old = sums.get((n, m))
                        sums[n, m] = (
                            terms if old is None else [x + y for x, y in zip(old, terms)]
                        )
                for n, m in pairs:
                    finish(n, m, item, sums[n, m])
        return carry

    lax.fori_loop(0, ITEMS, one_item, 0)
    conjugate = jnp.where(row % 2 == 0, 1.0, -1.0)
    upper, inner = row < 4, row % 4 < 2
    for number, (n, m) in enumerate(PAIRS):
        t = [tiles[number, item] for item in range(ITEMS)]
        halves = (
            [jnp.where(upper, t[i], pltpu.roll(t[i + 2], 4, 0)) for i in range(2)],
            [jnp.where(upper, pltpu.roll(t[i], 4, 0), t[i + 2]) for i in range(2)],
        )
        for h, (x, y) in enumerate(halves):
            same = jnp.where(inner, x, pltpu.roll(y, 2, 0))
            crossed = jnp.where(inner, pltpu.roll(x, 6, 0), y)
            a = 2 * n + h
            for b, value in ((2 * m + h, same), (2 * m + 1 - h, crossed)):
                out_ref[a * S + place_ref[b], 0:ITEMS] = value.astype(
                    jnp.bfloat16
                ).reshape(ITEMS, 2, LANES)
                if n != m:
                    out_ref[b * S + place_ref[a], 0:ITEMS] = (
                        (value * conjugate).astype(jnp.bfloat16).reshape(ITEMS, 2, LANES)
                    )
        pair_of_rows = counts[number // 4][number % 4 * 2 : number % 4 * 2 + 2]
        for h in range(2):
            for other in range(2):
                a, b = 2 * n + h, 2 * m + other
                out_ref[a * S + place_ref[b], ITEMS] = pair_of_rows
                if n != m:
                    out_ref[b * S + place_ref[a], ITEMS] = pair_of_rows


def correlated(order, arrived):
    return pl.pallas_call(
        correlate_kernel,
        in_specs=[
            pl.BlockSpec(memory_space=pltpu.SMEM),
            pl.BlockSpec(memory_space=pltpu.VMEM),
        ],
        out_specs=pl.BlockSpec(memory_space=pltpu.VMEM),
        out_shape=jax.ShapeDtypeStruct((S * S, ITEMS + 1, 2, LANES), jnp.bfloat16),
        scratch_shapes=[
            pltpu.VMEM((STN, 2, UNITS, 8, LANES), jnp.float32),
            pltpu.VMEM((STN, 2, UNITS, 8, LANES), jnp.float32),
            pltpu.VMEM((len(PAIRS), ITEMS, 8, LANES), jnp.float32),
            pltpu.SMEM((S,), jnp.int32),
        ],
        compiler_params=pltpu.CompilerParams(vmem_limit_bytes=32 * 2**20),
        name="correlate",
    )(order, arrived.reshape(STN, UNITS, TILES, 2, LANES))


def fringe_tables():
    lag = np.arange(1, HALF + 1)
    fine = 2.0 * np.pi * ((np.arange(LANES)[:, None] * lag) % C) / C
    coarse = 2.0 * np.pi * ((np.arange(CB)[:, None] * lag) % CB) / CB
    period = 2.0 * np.pi * ((np.arange(PERIODS)[:, None] * np.arange(PERIODS)) % PERIODS)
    period = period / PERIODS
    factor = 1.0 / math.sqrt(PERIODS * C)
    flip = np.eye(HALF)[::-1]
    fine = np.concatenate([np.cos(fine), np.sin(fine)], axis=1).astype(np.float32)
    high = fine.astype(ml_dtypes.bfloat16)
    low = (fine - high.astype(np.float32)).astype(ml_dtypes.bfloat16)
    return [np.concatenate([high, high, low])] + [
        np.ascontiguousarray(table, np.float32)
        for table in (
            np.stack([np.cos(coarse), np.sin(coarse)]),
            np.stack([np.cos(period), np.sin(period)]) * factor,
            flip,
        )
    ]


def fringe_kernel(
    place_ref, order_ref, z_ref, fine_ref, coarse_ref, period_ref, flip_ref, out_ref, sums, scales, seen
):
    mine, partner = place_ref[0] // S, order_ref[place_ref[0] % S]
    crossed = mine % 2 != partner % 2
    spectrum = jnp.where(mine // 2 <= partner // 2, mine % 2, partner % 2)
    for p in range(PERIODS):
        for u in range(UNITS):
            parts = [
                z_ref[p, quarter, u, 0:ITEMS].reshape(2 * ITEMS, LANES).astype(jnp.float32)
                for quarter in range(QUARTERS)
            ]
            at = (p * UNITS + u) * 2 * ITEMS
            sums[at : at + 2 * ITEMS] = (parts[0] + parts[1]) + (parts[2] + parts[3])
        counts = sum(
            z_ref[p, quarter, :, ITEMS].astype(jnp.float32) for quarter in range(QUARTERS)
        )
        seen[p * UNITS : (p + 1) * UNITS] = jnp.where(
            crossed, counts[:, 1, :], counts[:, 0, :]
        )
    source, target = rows_of((LANES, LANES)), lanes_of((LANES, LANES))
    wide = LANES // ITEMS
    added = (source // wide == target // wide) & (source % wide // K == 4 + spectrum)
    counts = jnp.dot(
        seen[...].astype(jnp.bfloat16),
        jnp.where(added, 1.0, 0.0).astype(jnp.bfloat16),
        preferred_element_type=jnp.float32,
    )
    scale = 1.0 / jnp.sqrt(jnp.maximum(counts, 1.0))
    for item in range(ITEMS):
        scales[pl.ds(item, PERIODS * UNITS, stride=ITEMS), :] = jnp.broadcast_to(
            scale[:, item * wide : item * wide + 1], (PERIODS * UNITS, LANES)
        )
    left = jnp.where(mine == partner, 1.0, 0.0)
    first = sums[pl.ds(0, PERIODS * CB, stride=2), :]
    second = sums[pl.ds(1, PERIODS * CB, stride=2), :]
    values = jnp.concatenate(
        [(first + left * second) * scales[...], (second * (1.0 - left)) * scales[...]]
    )
    high = values.astype(jnp.bfloat16)
    low = (values - high.astype(jnp.float32)).astype(jnp.bfloat16)
    both = jnp.dot(
        jnp.concatenate([high, low, high], axis=1),
        fine_ref[...],
        preferred_element_type=jnp.float32,
    )
    re, im = both[: PERIODS * CB], both[PERIODS * CB :]
    parts = [[], [], [], []]
    for p in range(PERIODS):
        sums = [jnp.zeros((8, LANES), jnp.float32)] * 4
        for g in range(CB // 8):
            at = slice(p * CB + g * 8, p * CB + g * 8 + 8)
            re_cos, re_sin = re[at, :HALF], re[at, HALF:]
            im_cos, im_sin = im[at, :HALF], im[at, HALF:]
            cosine = coarse_ref[0, g * 8 : g * 8 + 8, :]
            sine = coarse_ref[1, g * 8 : g * 8 + 8, :]
            plus_re, plus_im = re_cos + im_sin, im_cos - re_sin
            minus_re, minus_im = re_cos - im_sin, im_cos + re_sin
            terms = (
                cosine * minus_re - sine * minus_im,
                cosine * minus_im + sine * minus_re,
                cosine * plus_re + sine * plus_im,
                cosine * plus_im - sine * plus_re,
            )
            sums = [total + term for total, term in zip(sums, terms)]
        for part, total in zip(parts, sums):
            part.append(total)
    minus_re, minus_im, plus_re, plus_im = (group_sums(part, 8) for part in parts)
    reversed_ = jnp.dot(
        jnp.concatenate([minus_re, minus_im]),
        flip_ref[...],
        precision=HIGHEST,
        preferred_element_type=jnp.float32,
    )
    real = jnp.concatenate([reversed_[:8], plus_re], axis=1)
    imag = jnp.concatenate([reversed_[8:], plus_im], axis=1)
    cosine, sine = period_ref[0], period_ref[1]

    def turn(a, b):
        return jnp.dot(a, b, precision=HIGHEST, preferred_element_type=jnp.float32)

    out_ref[0, 0] = turn(cosine, real) + turn(sine, imag)
    out_ref[1, 0] = turn(cosine, imag) - turn(sine, real)


def fringed(place, order, owned):
    return pl.pallas_call(
        fringe_kernel,
        in_specs=[pl.BlockSpec(memory_space=pltpu.SMEM)] * 2
        + [pl.BlockSpec(memory_space=pltpu.VMEM)] * 5,
        out_specs=pl.BlockSpec(memory_space=pltpu.VMEM),
        out_shape=jax.ShapeDtypeStruct((2, 1, PERIODS, LAGS), jnp.float32),
        scratch_shapes=[
            pltpu.VMEM((PERIODS * CB * 2, LANES), jnp.float32),
            pltpu.VMEM((PERIODS * CB, LANES), jnp.float32),
            pltpu.VMEM((PERIODS * UNITS, LANES), jnp.float32),
        ],
        compiler_params=pltpu.CompilerParams(vmem_limit_bytes=32 * 2**20),
        name="fringe",
    )(
        place,
        order,
        owned.reshape(PERIODS, QUARTERS, UNITS, ITEMS + 1, 2, LANES),
        *fringe_tables(),
    )


def per_device(spectra, flags, poly_index, delay_model, partner_order):
    plane = ("stn", "unit")
    everyone = ("stn", "quarter", "unit")
    row = lax.axis_index(everyone).astype(jnp.int32)
    place = row.reshape(1)
    chunks = rotated_chunks(spectra, flags, poly_index, delay_model, place)
    arrived = lax.all_to_all(chunks, plane, split_axis=0, concat_axis=0, tiled=True)
    rows = correlated(partner_order, arrived)
    owned = lax.all_to_all(rows, everyone, split_axis=0, concat_axis=0, tiled=True)
    return fringed(place, partner_order, owned)


def solution(mesh):
    finer = Mesh(
        mesh.devices.reshape(STN, QUARTERS, UNITS), ("stn", "quarter", "unit")
    )
    time = ("quarter", "unit")
    return jax.shard_map(
        per_device,
        mesh=finer,
        in_specs=(
            P("stn", None, time, None, None),
            P("stn", None, time, None),
            P("stn", None, time),
            P(),
            P(),
        ),
        out_specs=P(None, ("stn", "quarter", "unit"), None, None),
        check_vma=False,
    )
```

```python
import math

import jax
import jax.numpy as jnp
import ml_dtypes
import numpy as np
from jax import lax
from jax.experimental import pallas as pl
from jax.experimental.pallas import tpu as pltpu
from jax.sharding import Mesh
from jax.sharding import PartitionSpec as P

S = 16
C = 4096
PERIODS = 8
LAGS = 256
SPP = 128
CB = 32
STN = 8
QUARTERS = 4
UNITS = 8
ITEMS = 4
K = 4
NPOLY = 64
SPECTRA = 2 * K
TILES = ITEMS * SPECTRA + 1
LANES = 128
HALF = LAGS // 2
HIGHEST = lax.Precision.HIGHEST
WIDE = LANES // ITEMS
TERMS = WIDE - 1
COSINE = [(-1) ** n * (2 * math.pi) ** (2 * n) / math.factorial(2 * n) for n in range(10)]
SINE = [(-1) ** n * (2 * math.pi) ** (2 * n + 1) / math.factorial(2 * n + 1) for n in range(10)]


def rows_of(shape):
    return lax.broadcasted_iota(jnp.int32, shape, len(shape) - 2)


def lanes_of(shape):
    return lax.broadcasted_iota(jnp.int32, shape, len(shape) - 1)


def turn(delay, index, whole):
    turns = delay * index.astype(jnp.float32) * (1.0 / whole)
    turns = turns - jnp.round(turns)
    square = turns * turns
    cosine = jnp.full_like(square, COSINE[-1])
    for coefficient in COSINE[-2::-1]:
        cosine = cosine * square + coefficient
    sine = jnp.full_like(square, SINE[-1])
    for coefficient in SINE[-2::-1]:
        sine = sine * square + coefficient
    return cosine, sine * turns


def in_hbm(array):
    return pltpu.with_memory_space_constraint(array, pltpu.HBM)


def rotate_kernel(
    place_ref,
    poly_hbm,
    model_hbm,
    flags_hbm,
    x_hbm,
    out_ref,
    poly_ref,
    model_ref,
    flags_ref,
    x_ref,
    turned_re,
    turned_im,
    sems,
):
    small = [
        pltpu.make_async_copy(source, target, sems.at[number])
        for number, (source, target) in enumerate(
            ((poly_hbm, poly_ref), (model_hbm, model_ref), (flags_hbm, flags_ref))
        )
    ]
    for copy in small:
        copy.start()
    fetch = pltpu.make_async_copy(x_hbm, x_ref, sems.at[3])
    fetch.start()
    for copy in small:
        copy.wait()
    row = rows_of((8, LANES))
    lane = lanes_of((8, LANES))
    across = jnp.zeros((8, LANES), jnp.float32)
    down = []
    for p in range(PERIODS):
        column = jnp.zeros((8, LANES), jnp.float32)
        for s in range(2):
            for k in range(K):
                index = poly_ref[s, k, p]
                time = p * SPP + place_ref[0] % (QUARTERS * UNITS) * K + k
                moment = time.astype(jnp.float32) * (1.0 / (PERIODS * SPP))
                delay = (
                    model_ref[0, index]
                    + model_ref[1, index] * moment
                    + model_ref[2, index] * moment * moment
                )
                column = jnp.where(row == s * K + k, delay, column)
                across = jnp.where(lane == p * SPECTRA + s * K + k, delay, across)
        down.append(column)
    fine_cos, fine_sin = zip(*(turn(column, lane, 2 * C) for column in down))
    weight = 1.0 - flags_ref[...].reshape(2 * PERIODS * K, CB).astype(jnp.float32)
    weight = weight.astype(jnp.bfloat16)
    source = rows_of((2 * PERIODS * K, LANES))
    source_s, source_p, source_k = source // (PERIODS * K), source // K % PERIODS, source % K
    target = lanes_of((2 * PERIODS * K, LANES))

    def spread(chosen):
        return lax.dot_general(
            weight,
            chosen.astype(jnp.bfloat16),
            (((0,), (0,)), ((), ())),
            preferred_element_type=jnp.float32,
        )

    spectrum = source_s * K + source_k
    coarse_weight = spread(
        jnp.where(target == source_p * SPECTRA + spectrum, 1.0, 0.0)
    )
    block = rows_of((CB, LANES))
    cosine, sine = turn(jnp.tile(across, (CB // 8, 1)), block, 2 * CB)
    coarse_cos = coarse_weight * cosine
    coarse_sin = coarse_weight * sine
    held = block % ITEMS == lanes_of((CB, LANES)) // (LANES // ITEMS)
    merge = rows_of((UNITS, CB)) == lanes_of((UNITS, CB)) // ITEMS
    merge = jnp.where(merge, 1.0, 0.0).astype(jnp.bfloat16)
    for p in range(PERIODS):
        mark = jnp.where((source_p == p) & (target % SPECTRA == spectrum), 1.0, 0.0)
        sent = jnp.where(held, spread(mark), 0.0).astype(jnp.bfloat16)
        sent = jnp.dot(merge, sent, preferred_element_type=jnp.float32).astype(jnp.bfloat16)
        if p == 0:
            fetch.wait()
        for s in range(2):
            for k in range(K):
                r = s * K + k
                x = x_ref[s, p, k].astype(jnp.float32)
                re = x[0:1].reshape(CB, LANES)
                im = x[1:2].reshape(CB, LANES)
                at = p * SPECTRA + r
                a_cos = jnp.broadcast_to(coarse_cos[:, at : at + 1], (CB, LANES))
                a_sin = jnp.broadcast_to(coarse_sin[:, at : at + 1], (CB, LANES))
                b_cos = jnp.broadcast_to(fine_cos[p][r : r + 1], (CB, LANES))
                b_sin = jnp.broadcast_to(fine_sin[p][r : r + 1], (CB, LANES))
                cosine = a_cos * b_cos - a_sin * b_sin
                sine = a_sin * b_cos + a_cos * b_sin
                turned_re[p % 2, pl.ds(r, CB, stride=SPECTRA), :] = re * cosine + im * sine
                turned_im[p % 2, pl.ds(r, CB, stride=SPECTRA), :] = im * cosine - re * sine
        for q in range(CB):
            at = slice(q * SPECTRA, (q + 1) * SPECTRA)
            both = jnp.concatenate([turned_re[p % 2, at], turned_im[p % 2, at]])
            tile = q % ITEMS * SPECTRA
            out_ref[p * UNITS + q // ITEMS, tile : tile + SPECTRA] = both.astype(
                jnp.bfloat16
            ).reshape(SPECTRA, 2, LANES)
        out_ref[p * UNITS : (p + 1) * UNITS, TILES - 1] = jnp.broadcast_to(
            sent[:, None, :], (UNITS, 2, LANES)
        )


def rotated_chunks(spectra, flags, poly_index, delay_model, place):
    return pl.pallas_call(
        rotate_kernel,
        in_specs=[pl.BlockSpec(memory_space=pltpu.SMEM)]
        + [pl.BlockSpec(memory_space=pltpu.HBM)] * 4,
        out_specs=pl.BlockSpec(memory_space=pltpu.VMEM),
        out_shape=jax.ShapeDtypeStruct((PERIODS * UNITS, TILES, 2, LANES), jnp.bfloat16),
        scratch_shapes=[
            pltpu.SMEM((2, K, PERIODS), jnp.int32),
            pltpu.SMEM((3, NPOLY), jnp.float32),
            pltpu.VMEM((2, PERIODS, K, CB), jnp.int32),
            pltpu.VMEM((2, PERIODS, K, 2, C), jnp.bfloat16),
            pltpu.VMEM((2, CB * SPECTRA, LANES), jnp.float32),
            pltpu.VMEM((2, CB * SPECTRA, LANES), jnp.float32),
            pltpu.SemaphoreType.DMA((4,)),
        ],
        compiler_params=pltpu.CompilerParams(vmem_limit_bytes=32 * 2**20),
        name="rotate",
    )(
        place,
        in_hbm(poly_index.transpose(0, 2, 1)),
        in_hbm(delay_model.T),
        in_hbm(flags),
        in_hbm(spectra),
    )


def group_sums(values, group):
    row = rows_of((8, LANES))
    stage = list(values)
    distance = group // 2
    while distance:
        first = row % (2 * distance) < distance
        if 2 * distance == 8:
            stage = [
                jnp.where(first, stage[i], stage[i + distance])
                + pltpu.roll(jnp.where(first, stage[i + distance], stage[i]), 4, 0)
                for i in range(distance)
            ]
        else:
            stage = [
                jnp.where(first, stage[i], stage[i + distance])
                + jnp.where(
                    first,
                    pltpu.roll(stage[i], 8 - distance, 0),
                    pltpu.roll(stage[i + distance], distance, 0),
                )
                for i in range(distance)
            ]
        distance //= 2
    return stage[0]


PAIRS = [(n, m) for n in range(STN) for m in range(n, STN)]


def three_passes(values, table):
    high = values.astype(jnp.bfloat16)
    low = (values - high.astype(jnp.float32)).astype(jnp.bfloat16)
    return jnp.dot(
        jnp.concatenate([high, low, high], axis=1),
        table,
        preferred_element_type=jnp.float32,
    )


def correlate_kernel(order_ref, y_ref, terms_ref, out_ref, mine_ref, crossed_ref, tiles, place_ref):
    for j in range(S):
        place_ref[order_ref[j]] = j
    row = rows_of((8, LANES))
    lane = lanes_of((8, LANES))
    zero = jnp.zeros((8, LANES), jnp.float32)

    def finish(n, m, item, sums):
        if n == m:
            values = [sums[0] + sums[1], zero]
        else:
            values = [sums[0] + sums[2], sums[0] - sums[1]]
        values += [sums[-3] + sums[-1], sums[-3] - sums[-2]]
        tile = group_sums(values, 4)
        tiles[item, pl.ds(PAIRS.index((n, m)) * 8, 8)] = tile

    weights = [
        y_ref[n, :, TILES - 1].astype(jnp.float32)[:, 0, :] for n in range(STN)
    ]
    swapped = [pltpu.roll(weight, K, 1) for weight in weights]
    counts = []
    for n, m in PAIRS:
        same, other = weights[n] * weights[m], weights[n] * swapped[m]
        counts.append(group_sums([same, zero, other, zero] * 2, 8))
    counts = jnp.concatenate(counts)
    at = rows_of(counts.shape) % 8 // 4
    counts = jnp.where(lanes_of(counts.shape) % WIDE // K == 4 + at, counts, 0.0)
    i, j = rows_of((LANES, LANES)), lanes_of((LANES, LANES))
    last = jnp.where(j == i // WIDE * WIDE + TERMS, 1.0, 0.0)
    counts = jnp.dot(
        counts.astype(jnp.bfloat16),
        last.astype(jnp.bfloat16),
        preferred_element_type=jnp.float32,
    )

    def one_item(item, carry):
        for n in range(STN):
            for u in range(UNITS):
                x = y_ref[n, u, pl.ds(item * SPECTRA, SPECTRA)].reshape(2 * SPECTRA, LANES)
                x = x.astype(jnp.float32)
                re, im = x[:SPECTRA], x[SPECTRA:]
                for part, value in enumerate((re, im)):
                    mine_ref[n, part, u] = value
                    crossed_ref[n, part, u] = pltpu.roll(value, 4, 0)
        for block_n in range(0, STN, 2):
            for block_m in range(block_n - block_n % 2, STN, 2):
                pairs = [
                    (n, m)
                    for n in range(block_n, block_n + 2)
                    for m in range(block_m, block_m + 2)
                    if n <= m
                ]
                sums = {}
                for u in range(UNITS):
                    mine, theirs = {}, {}
                    for n in range(block_n, block_n + 2):
                        re, im = mine_ref[n, 0, u], mine_ref[n, 1, u]
                        mine[n] = re, im, re + im
                    for m in range(block_m, block_m + 2):
                        for number, ref in enumerate((mine_ref, crossed_ref)):
                            re, im = ref[m, 0, u], ref[m, 1, u]
                            theirs[m, number] = re, re + im, im - re
                    for n, m in pairs:
                        re, im, both = mine[n]
                        terms = []
                        for number in range(2):
                            their_re, their_both, their_gap = theirs[m, number]
                            if n == m and not number:
                                terms += [re * re, im * im]
                            else:
                                terms += [both * their_re, re * their_both, im * their_gap]
                        old = sums.get((n, m))
                        sums[n, m] = (
                            terms if old is None else [x + y for x, y in zip(old, terms)]
                        )
                for n, m in pairs:
                    finish(n, m, item, sums[n, m])
        return carry

    lax.fori_loop(0, ITEMS, one_item, 0)
    conjugate = jnp.where(row % 2 == 0, 1.0, -1.0)
    total = counts
    for item in range(ITEMS):
        total = total + three_passes(tiles[item], terms_ref[item])
    for number, (n, m) in enumerate(PAIRS):
        value = total[number * 8 : number * 8 + 8]
        other = value * conjugate
        for pair in range(4):
            h = pair // 2
            a, b = 2 * n + h, 2 * m + (h if pair % 2 == 0 else 1 - h)
            at = slice(2 * pair, 2 * pair + 2)
            out_ref[a * S + place_ref[b]] = value[at]
            if n != m:
                out_ref[b * S + place_ref[a]] = other[at]


def correlated(order, arrived):
    return pl.pallas_call(
        correlate_kernel,
        in_specs=[
            pl.BlockSpec(memory_space=pltpu.SMEM),
            pl.BlockSpec(memory_space=pltpu.VMEM),
            pl.BlockSpec(memory_space=pltpu.VMEM),
        ],
        out_specs=pl.BlockSpec(memory_space=pltpu.VMEM),
        out_shape=jax.ShapeDtypeStruct((S * S, 2, LANES), jnp.float32),
        scratch_shapes=[
            pltpu.VMEM((STN, 2, UNITS, 8, LANES), jnp.float32),
            pltpu.VMEM((STN, 2, UNITS, 8, LANES), jnp.float32),
            pltpu.VMEM((ITEMS, len(PAIRS) * 8, LANES), jnp.float32),
            pltpu.SMEM((S,), jnp.int32),
        ],
        compiler_params=pltpu.CompilerParams(vmem_limit_bytes=32 * 2**20),
        name="correlate",
    )(order, arrived.reshape(STN, UNITS, TILES, 2, LANES), term_tables())


def split_table(table):
    high = table.astype(np.float32).astype(ml_dtypes.bfloat16)
    low = (table - high.astype(np.float64)).astype(np.float32).astype(ml_dtypes.bfloat16)
    return np.concatenate([high, high, low])


CENTRE = (LANES - 1) / 2


def term_tables():
    x = (np.arange(LANES) - CENTRE) / CENTRE
    table = np.cos(np.arccos(x)[:, None] * np.arange(TERMS))
    placed = np.zeros((ITEMS, LANES, LANES))
    for item in range(ITEMS):
        placed[item, :, item * WIDE : item * WIDE + TERMS] = table
    return np.stack([split_table(each) for each in placed])


def fringe_tables():
    lag = np.arange(1, HALF + 1)
    z = 2.0 * np.pi * CENTRE * lag / C
    points = 2.0 * np.pi * np.arange(256) / 256
    order = np.arange(TERMS)
    bessel = np.cos(
        order[:, None, None] * points - z[:, None] * np.sin(points)
    ).mean(axis=2)
    series = np.where(order == 0, 1, 2)[:, None] * np.array([1, -1j, -1, 1j])[order % 4][:, None] * bessel
    fine = np.zeros((LANES, HALF), np.complex128)
    for item in range(ITEMS):
        turned = np.exp(-2j * np.pi * ((CENTRE + item * LANES) * lag % C) / C)
        fine[item * WIDE : item * WIDE + TERMS] = series * turned
    unit = 2.0 * np.pi * ((np.arange(UNITS)[:, None] * lag) % UNITS) / UNITS
    period = 2.0 * np.pi * ((np.arange(PERIODS)[:, None] * np.arange(PERIODS)) % PERIODS)
    period = period / PERIODS
    factor = 1.0 / math.sqrt(PERIODS * C)
    return [split_table(np.concatenate([fine.real, -fine.imag], axis=1))] + [
        np.ascontiguousarray(table, np.float32)
        for table in (
            np.stack([np.cos(unit), np.sin(unit)]),
            np.stack([np.cos(period), np.sin(period)]) * factor,
            np.eye(HALF)[::-1],
        )
    ]


def fringe_kernel(z_ref, fine_ref, coarse_ref, period_ref, flip_ref, out_ref):
    sums = [
        sum(z_ref[p, quarter] for quarter in range(QUARTERS)) for p in range(PERIODS)
    ]
    real = jnp.concatenate([each[:, 0, :] for each in sums])
    imag = jnp.concatenate([each[:, 1, :] for each in sums])
    i, j = rows_of((LANES, LANES)), lanes_of((LANES, LANES))
    spread = jnp.where(i == j // WIDE * WIDE + TERMS, 1.0, 0.0).astype(jnp.bfloat16)
    counts = jnp.dot(
        jnp.where(lanes_of(real.shape) % WIDE == TERMS, real, 0.0).astype(jnp.bfloat16),
        spread,
        preferred_element_type=jnp.float32,
    )
    scale = 1.0 / jnp.sqrt(jnp.maximum(counts, 1.0))
    both = three_passes(
        jnp.concatenate([real * scale, imag * scale]), fine_ref[...]
    )
    re, im = both[: PERIODS * UNITS], both[PERIODS * UNITS :]
    parts = [[], [], [], []]
    for p in range(PERIODS):
        sums = [jnp.zeros((8, LANES), jnp.float32)] * 4
        for g in range(1):
            at = slice(p * UNITS, p * UNITS + UNITS)
            re_cos, re_sin = re[at, :HALF], re[at, HALF:]
            im_cos, im_sin = im[at, :HALF], im[at, HALF:]
            cosine = coarse_ref[0, g * 8 : g * 8 + 8, :]
            sine = coarse_ref[1, g * 8 : g * 8 + 8, :]
            plus_re, plus_im = re_cos + im_sin, im_cos - re_sin
            minus_re, minus_im = re_cos - im_sin, im_cos + re_sin
            terms = (
                cosine * minus_re - sine * minus_im,
                cosine * minus_im + sine * minus_re,
                cosine * plus_re + sine * plus_im,
                cosine * plus_im - sine * plus_re,
            )
            sums = [total + term for total, term in zip(sums, terms)]
        for part, total in zip(parts, sums):
            part.append(total)
    minus_re, minus_im, plus_re, plus_im = (group_sums(part, 8) for part in parts)
    reversed_ = jnp.dot(
        jnp.concatenate([minus_re, minus_im]),
        flip_ref[...],
        precision=HIGHEST,
        preferred_element_type=jnp.float32,
    )
    real = jnp.concatenate([reversed_[:8], plus_re], axis=1)
    imag = jnp.concatenate([reversed_[8:], plus_im], axis=1)
    cosine, sine = period_ref[0], period_ref[1]

    def turn(a, b):
        return jnp.dot(a, b, precision=HIGHEST, preferred_element_type=jnp.float32)

    out_ref[0, 0] = turn(cosine, real) + turn(sine, imag)
    out_ref[1, 0] = turn(cosine, imag) - turn(sine, real)


def fringed(owned):
    return pl.pallas_call(
        fringe_kernel,
        in_specs=[pl.BlockSpec(memory_space=pltpu.VMEM)] * 5,
        out_specs=pl.BlockSpec(memory_space=pltpu.VMEM),
        out_shape=jax.ShapeDtypeStruct((2, 1, PERIODS, LAGS), jnp.float32),
        compiler_params=pltpu.CompilerParams(vmem_limit_bytes=32 * 2**20),
        name="fringe",
    )(owned.reshape(PERIODS, QUARTERS, UNITS, 2, LANES), *fringe_tables())


def per_device(spectra, flags, poly_index, delay_model, partner_order):
    plane = ("stn", "unit")
    everyone = ("stn", "quarter", "unit")
    row = lax.axis_index(everyone).astype(jnp.int32)
    place = row.reshape(1)
    chunks = rotated_chunks(spectra, flags, poly_index, delay_model, place)
    arrived = lax.all_to_all(chunks, plane, split_axis=0, concat_axis=0, tiled=True)
    rows = correlated(partner_order, arrived)
    owned = lax.all_to_all(rows, everyone, split_axis=0, concat_axis=0, tiled=True)
    return fringed(owned)


def solution(mesh):
    finer = Mesh(
        mesh.devices.reshape(STN, QUARTERS, UNITS), ("stn", "quarter", "unit")
    )
    time = ("quarter", "unit")
    return jax.shard_map(
        per_device,
        mesh=finer,
        in_specs=(
            P("stn", None, time, None, None),
            P("stn", None, time, None),
            P("stn", None, time),
            P(),
            P(),
        ),
        out_specs=P(None, ("stn", "quarter", "unit"), None, None),
        check_vma=False,
    )
```

```python
import math

import jax
import jax.numpy as jnp
import ml_dtypes
import numpy as np
from jax import lax
from jax.experimental import pallas as pl
from jax.experimental.pallas import tpu as pltpu
from jax.sharding import Mesh
from jax.sharding import PartitionSpec as P

S = 16
C = 4096
PERIODS = 8
LAGS = 256
SPP = 128
CB = 32
STN = 8
QUARTERS = 4
UNITS = 8
ITEMS = 4
K = 4
NPOLY = 64
SPECTRA = 2 * K
TILES = ITEMS * SPECTRA + 1
LANES = 128
HALF = LAGS // 2
HIGHEST = lax.Precision.HIGHEST
WIDE = LANES // ITEMS
TERMS = WIDE - 1
COSINE = [(-1) ** n * (2 * math.pi) ** (2 * n) / math.factorial(2 * n) for n in range(10)]
SINE = [(-1) ** n * (2 * math.pi) ** (2 * n + 1) / math.factorial(2 * n + 1) for n in range(10)]


def rows_of(shape):
    return lax.broadcasted_iota(jnp.int32, shape, len(shape) - 2)


def lanes_of(shape):
    return lax.broadcasted_iota(jnp.int32, shape, len(shape) - 1)


def turn(delay, index, whole):
    turns = delay * index.astype(jnp.float32) * (1.0 / whole)
    turns = turns - jnp.round(turns)
    square = turns * turns
    cosine = jnp.full_like(square, COSINE[-1])
    for coefficient in COSINE[-2::-1]:
        cosine = cosine * square + coefficient
    sine = jnp.full_like(square, SINE[-1])
    for coefficient in SINE[-2::-1]:
        sine = sine * square + coefficient
    return cosine, sine * turns


def in_hbm(array):
    return pltpu.with_memory_space_constraint(array, pltpu.HBM)


def rotate_kernel(
    place_ref,
    poly_hbm,
    model_hbm,
    flags_hbm,
    x_hbm,
    out_ref,
    poly_ref,
    model_ref,
    flags_ref,
    x_ref,
    turned_re,
    turned_im,
    sems,
):
    small = [
        pltpu.make_async_copy(source, target, sems.at[number])
        for number, (source, target) in enumerate(
            ((poly_hbm, poly_ref), (model_hbm, model_ref), (flags_hbm, flags_ref))
        )
    ]
    for copy in small:
        copy.start()
    fetch = pltpu.make_async_copy(x_hbm, x_ref, sems.at[3])
    fetch.start()
    for copy in small:
        copy.wait()
    row = rows_of((8, LANES))
    lane = lanes_of((8, LANES))
    across = jnp.zeros((8, LANES), jnp.float32)
    down = []
    for p in range(PERIODS):
        column = jnp.zeros((8, LANES), jnp.float32)
        for s in range(2):
            for k in range(K):
                index = poly_ref[s, k, p]
                time = p * SPP + place_ref[0] % (QUARTERS * UNITS) * K + k
                moment = time.astype(jnp.float32) * (1.0 / (PERIODS * SPP))
                delay = (
                    model_ref[0, index]
                    + model_ref[1, index] * moment
                    + model_ref[2, index] * moment * moment
                )
                column = jnp.where(row == s * K + k, delay, column)
                across = jnp.where(lane == p * SPECTRA + s * K + k, delay, across)
        down.append(column)
    fine_cos, fine_sin = zip(*(turn(column, lane, 2 * C) for column in down))
    weight = 1.0 - flags_ref[...].reshape(2 * PERIODS * K, CB).astype(jnp.float32)
    weight = weight.astype(jnp.bfloat16)
    source = rows_of((2 * PERIODS * K, LANES))
    source_s, source_p, source_k = source // (PERIODS * K), source // K % PERIODS, source % K
    target = lanes_of((2 * PERIODS * K, LANES))

    def spread(chosen):
        return lax.dot_general(
            weight,
            chosen.astype(jnp.bfloat16),
            (((0,), (0,)), ((), ())),
            preferred_element_type=jnp.float32,
        )

    spectrum = source_s * K + source_k
    coarse_weight = spread(
        jnp.where(target == source_p * SPECTRA + spectrum, 1.0, 0.0)
    )
    block = rows_of((CB, LANES))
    cosine, sine = turn(jnp.tile(across, (CB // 8, 1)), block, 2 * CB)
    coarse_cos = coarse_weight * cosine
    coarse_sin = coarse_weight * sine
    held = block % ITEMS == lanes_of((CB, LANES)) // (LANES // ITEMS)
    merge = rows_of((UNITS, CB)) == lanes_of((UNITS, CB)) // ITEMS
    merge = jnp.where(merge, 1.0, 0.0).astype(jnp.bfloat16)
    for p in range(PERIODS):
        mark = jnp.where((source_p == p) & (target % SPECTRA == spectrum), 1.0, 0.0)
        sent = jnp.where(held, spread(mark), 0.0).astype(jnp.bfloat16)
        sent = jnp.dot(merge, sent, preferred_element_type=jnp.float32).astype(jnp.bfloat16)
        if p == 0:
            fetch.wait()
        for s in range(2):
            for k in range(K):
                r = s * K + k
                x = x_ref[s, p, k].astype(jnp.float32)
                re = x[0:1].reshape(CB, LANES)
                im = x[1:2].reshape(CB, LANES)
                at = p * SPECTRA + r
                a_cos = jnp.broadcast_to(coarse_cos[:, at : at + 1], (CB, LANES))
                a_sin = jnp.broadcast_to(coarse_sin[:, at : at + 1], (CB, LANES))
                b_cos = jnp.broadcast_to(fine_cos[p][r : r + 1], (CB, LANES))
                b_sin = jnp.broadcast_to(fine_sin[p][r : r + 1], (CB, LANES))
                cosine = a_cos * b_cos - a_sin * b_sin
                sine = a_sin * b_cos + a_cos * b_sin
                turned_re[p % 2, pl.ds(r, CB, stride=SPECTRA), :] = re * cosine + im * sine
                turned_im[p % 2, pl.ds(r, CB, stride=SPECTRA), :] = im * cosine - re * sine
        for q in range(CB):
            at = slice(q * SPECTRA, (q + 1) * SPECTRA)
            both = jnp.concatenate([turned_re[p % 2, at], turned_im[p % 2, at]])
            tile = q % ITEMS * SPECTRA
            out_ref[p * UNITS + q // ITEMS, tile : tile + SPECTRA] = both.astype(
                jnp.bfloat16
            ).reshape(SPECTRA, 2, LANES)
        out_ref[p * UNITS : (p + 1) * UNITS, TILES - 1] = jnp.broadcast_to(
            sent[:, None, :], (UNITS, 2, LANES)
        )


def rotated_chunks(spectra, flags, poly_index, delay_model, place):
    return pl.pallas_call(
        rotate_kernel,
        in_specs=[pl.BlockSpec(memory_space=pltpu.SMEM)]
        + [pl.BlockSpec(memory_space=pltpu.HBM)] * 4,
        out_specs=pl.BlockSpec(memory_space=pltpu.VMEM),
        out_shape=jax.ShapeDtypeStruct((PERIODS * UNITS, TILES, 2, LANES), jnp.bfloat16),
        scratch_shapes=[
            pltpu.SMEM((2, K, PERIODS), jnp.int32),
            pltpu.SMEM((3, NPOLY), jnp.float32),
            pltpu.VMEM((2, PERIODS, K, CB), jnp.int32),
            pltpu.VMEM((2, PERIODS, K, 2, C), jnp.bfloat16),
            pltpu.VMEM((2, CB * SPECTRA, LANES), jnp.float32),
            pltpu.VMEM((2, CB * SPECTRA, LANES), jnp.float32),
            pltpu.SemaphoreType.DMA((4,)),
        ],
        compiler_params=pltpu.CompilerParams(vmem_limit_bytes=32 * 2**20),
        name="rotate",
    )(
        place,
        in_hbm(poly_index.transpose(0, 2, 1)),
        in_hbm(delay_model.T),
        in_hbm(flags),
        in_hbm(spectra),
    )


def group_sums(values, group):
    row = rows_of((8, LANES))
    stage = list(values)
    distance = group // 2
    while distance:
        first = row % (2 * distance) < distance
        if 2 * distance == 8:
            stage = [
                jnp.where(first, stage[i], stage[i + distance])
                + pltpu.roll(jnp.where(first, stage[i + distance], stage[i]), 4, 0)
                for i in range(distance)
            ]
        else:
            stage = [
                jnp.where(first, stage[i], stage[i + distance])
                + jnp.where(
                    first,
                    pltpu.roll(stage[i], 8 - distance, 0),
                    pltpu.roll(stage[i + distance], distance, 0),
                )
                for i in range(distance)
            ]
        distance //= 2
    return stage[0]


PAIRS = [(n, m) for n in range(STN) for m in range(n, STN)]


def three_passes(values, table):
    high = values.astype(jnp.bfloat16)
    low = (values - high.astype(jnp.float32)).astype(jnp.bfloat16)
    return jnp.dot(
        jnp.concatenate([high, low, high], axis=1),
        table,
        preferred_element_type=jnp.float32,
    )


def correlate_kernel(order_ref, y_ref, terms_ref, out_ref, mine_ref, crossed_ref, tiles, place_ref):
    for j in range(S):
        place_ref[order_ref[j]] = j
    row = rows_of((8, LANES))
    lane = lanes_of((8, LANES))
    zero = jnp.zeros((8, LANES), jnp.float32)

    def finish(n, m, item, sums):
        if n == m:
            values = [sums[0] + sums[1], zero]
        else:
            values = [sums[0] + sums[2], sums[0] - sums[1]]
        values += [sums[-3] + sums[-1], sums[-3] - sums[-2]]
        tile = group_sums(values, 4)
        tiles[item, pl.ds(PAIRS.index((n, m)) * 8, 8)] = tile

    weights = [
        y_ref[n, :, TILES - 1].astype(jnp.float32)[:, 0, :] for n in range(STN)
    ]
    swapped = [pltpu.roll(weight, K, 1) for weight in weights]
    counts = []
    for n, m in PAIRS:
        same, other = weights[n] * weights[m], weights[n] * swapped[m]
        counts.append(group_sums([same, zero, other, zero] * 2, 8))
    counts = jnp.concatenate(counts)
    at = rows_of(counts.shape) % 8 // 4
    counts = jnp.where(lanes_of(counts.shape) % WIDE // K == 4 + at, counts, 0.0)
    i, j = rows_of((LANES, LANES)), lanes_of((LANES, LANES))
    last = jnp.where(j == i // WIDE * WIDE + TERMS, 1.0, 0.0)
    counts = jnp.dot(
        counts.astype(jnp.bfloat16),
        last.astype(jnp.bfloat16),
        preferred_element_type=jnp.float32,
    )

    def one_item(item, carry):
        for n in range(STN):
            for u in range(UNITS):
                x = y_ref[n, u, pl.ds(item * SPECTRA, SPECTRA)].reshape(2 * SPECTRA, LANES)
                x = x.astype(jnp.float32)
                re, im = x[:SPECTRA], x[SPECTRA:]
                for part, value in enumerate((re, im)):
                    mine_ref[n, part, u] = value
                    crossed_ref[n, part, u] = pltpu.roll(value, 4, 0)
        for block_n in range(0, STN, 2):
            for block_m in range(block_n - block_n % 2, STN, 2):
                pairs = [
                    (n, m)
                    for n in range(block_n, block_n + 2)
                    for m in range(block_m, block_m + 2)
                    if n <= m
                ]
                sums = {}
                for u in range(UNITS):
                    mine, theirs = {}, {}
                    for n in range(block_n, block_n + 2):
                        re, im = mine_ref[n, 0, u], mine_ref[n, 1, u]
                        mine[n] = re, im, re + im
                    for m in range(block_m, block_m + 2):
                        for number, ref in enumerate((mine_ref, crossed_ref)):
                            re, im = ref[m, 0, u], ref[m, 1, u]
                            theirs[m, number] = re, re + im, im - re
                    for n, m in pairs:
                        re, im, both = mine[n]
                        terms = []
                        for number in range(2):
                            their_re, their_both, their_gap = theirs[m, number]
                            if n == m and not number:
                                terms += [re * re, im * im]
                            else:
                                terms += [both * their_re, re * their_both, im * their_gap]
                        old = sums.get((n, m))
                        sums[n, m] = (
                            terms if old is None else [x + y for x, y in zip(old, terms)]
                        )
                for n, m in pairs:
                    finish(n, m, item, sums[n, m])
        return carry

    lax.fori_loop(0, ITEMS, one_item, 0)
    conjugate = jnp.where(row % 2 == 0, 1.0, -1.0)
    total = counts
    for item in range(ITEMS):
        total = total + three_passes(tiles[item], terms_ref[item])
    for number, (n, m) in enumerate(PAIRS):
        value = total[number * 8 : number * 8 + 8]
        if n == m:
            left = value - value.astype(jnp.bfloat16).astype(jnp.float32)
            value = jnp.where(row % 4 == 1, pltpu.roll(left, 1, 0), value)
        other = (value * conjugate).astype(jnp.bfloat16)
        value = value.astype(jnp.bfloat16)
        for pair in range(4):
            h = pair // 2
            a, b = 2 * n + h, 2 * m + (h if pair % 2 == 0 else 1 - h)
            at = slice(2 * pair, 2 * pair + 2)
            out_ref[a * S + place_ref[b]] = value[at]
            if n != m:
                out_ref[b * S + place_ref[a]] = other[at]


def correlated(order, arrived):
    return pl.pallas_call(
        correlate_kernel,
        in_specs=[
            pl.BlockSpec(memory_space=pltpu.SMEM),
            pl.BlockSpec(memory_space=pltpu.VMEM),
            pl.BlockSpec(memory_space=pltpu.VMEM),
        ],
        out_specs=pl.BlockSpec(memory_space=pltpu.VMEM),
        out_shape=jax.ShapeDtypeStruct((S * S, 2, LANES), jnp.bfloat16),
        scratch_shapes=[
            pltpu.VMEM((STN, 2, UNITS, 8, LANES), jnp.float32),
            pltpu.VMEM((STN, 2, UNITS, 8, LANES), jnp.float32),
            pltpu.VMEM((ITEMS, len(PAIRS) * 8, LANES), jnp.float32),
            pltpu.SMEM((S,), jnp.int32),
        ],
        compiler_params=pltpu.CompilerParams(vmem_limit_bytes=32 * 2**20),
        name="correlate",
    )(order, arrived.reshape(STN, UNITS, TILES, 2, LANES), term_tables())


def split_table(table):
    high = table.astype(np.float32).astype(ml_dtypes.bfloat16)
    low = (table - high.astype(np.float64)).astype(np.float32).astype(ml_dtypes.bfloat16)
    return np.concatenate([high, high, low])


CENTRE = (LANES - 1) / 2


def term_tables():
    x = (np.arange(LANES) - CENTRE) / CENTRE
    table = np.cos(np.arccos(x)[:, None] * np.arange(TERMS))
    placed = np.zeros((ITEMS, LANES, LANES))
    for item in range(ITEMS):
        placed[item, :, item * WIDE : item * WIDE + TERMS] = table
    return np.stack([split_table(each) for each in placed])


def fringe_tables():
    lag = np.arange(1, HALF + 1)
    z = 2.0 * np.pi * CENTRE * lag / C
    points = 2.0 * np.pi * np.arange(256) / 256
    order = np.arange(TERMS)
    bessel = np.cos(
        order[:, None, None] * points - z[:, None] * np.sin(points)
    ).mean(axis=2)
    series = np.where(order == 0, 1, 2)[:, None] * np.array([1, -1j, -1, 1j])[order % 4][:, None] * bessel
    fine = np.zeros((LANES, HALF), np.complex128)
    for item in range(ITEMS):
        turned = np.exp(-2j * np.pi * ((CENTRE + item * LANES) * lag % C) / C)
        fine[item * WIDE : item * WIDE + TERMS] = series * turned
    unit = 2.0 * np.pi * ((np.arange(UNITS)[:, None] * lag) % UNITS) / UNITS
    period = 2.0 * np.pi * ((np.arange(PERIODS)[:, None] * np.arange(PERIODS)) % PERIODS)
    period = period / PERIODS
    factor = 1.0 / math.sqrt(PERIODS * C)
    return [split_table(np.concatenate([fine.real, -fine.imag], axis=1))] + [
        np.ascontiguousarray(table, np.float32)
        for table in (
            np.stack([np.cos(unit), np.sin(unit)]),
            np.stack([np.cos(period), np.sin(period)]) * factor,
            np.eye(HALF)[::-1],
        )
    ]


def fringe_kernel(place_ref, order_ref, z_ref, fine_ref, coarse_ref, period_ref, flip_ref, out_ref):
    sums = [
        sum(z_ref[p, quarter].astype(jnp.float32) for quarter in range(QUARTERS))
        for p in range(PERIODS)
    ]
    real = jnp.concatenate([each[:, 0, :] for each in sums])
    imag = jnp.concatenate([each[:, 1, :] for each in sums])
    alone = order_ref[place_ref[0] % S] == place_ref[0] // S
    left = jnp.where(alone, 1.0, 0.0)
    real, imag = real + left * imag, (1.0 - left) * imag
    i, j = rows_of((LANES, LANES)), lanes_of((LANES, LANES))
    spread = jnp.where(i == j // WIDE * WIDE + TERMS, 1.0, 0.0).astype(jnp.bfloat16)
    counts = jnp.dot(
        jnp.where(lanes_of(real.shape) % WIDE == TERMS, real, 0.0).astype(jnp.bfloat16),
        spread,
        preferred_element_type=jnp.float32,
    )
    scale = 1.0 / jnp.sqrt(jnp.maximum(counts, 1.0))
    both = three_passes(
        jnp.concatenate([real * scale, imag * scale]), fine_ref[...]
    )
    re, im = both[: PERIODS * UNITS], both[PERIODS * UNITS :]
    parts = [[], [], [], []]
    for p in range(PERIODS):
        sums = [jnp.zeros((8, LANES), jnp.float32)] * 4
        for g in range(1):
            at = slice(p * UNITS, p * UNITS + UNITS)
            re_cos, re_sin = re[at, :HALF], re[at, HALF:]
            im_cos, im_sin = im[at, :HALF], im[at, HALF:]
            cosine = coarse_ref[0, g * 8 : g * 8 + 8, :]
            sine = coarse_ref[1, g * 8 : g * 8 + 8, :]
            plus_re, plus_im = re_cos + im_sin, im_cos - re_sin
            minus_re, minus_im = re_cos - im_sin, im_cos + re_sin
            terms = (
                cosine * minus_re - sine * minus_im,
                cosine * minus_im + sine * minus_re,
                cosine * plus_re + sine * plus_im,
                cosine * plus_im - sine * plus_re,
            )
            sums = [total + term for total, term in zip(sums, terms)]
        for part, total in zip(parts, sums):
            part.append(total)
    minus_re, minus_im, plus_re, plus_im = (group_sums(part, 8) for part in parts)
    reversed_ = jnp.dot(
        jnp.concatenate([minus_re, minus_im]),
        flip_ref[...],
        precision=HIGHEST,
        preferred_element_type=jnp.float32,
    )
    real = jnp.concatenate([reversed_[:8], plus_re], axis=1)
    imag = jnp.concatenate([reversed_[8:], plus_im], axis=1)
    cosine, sine = period_ref[0], period_ref[1]

    def turn(a, b):
        return jnp.dot(a, b, precision=HIGHEST, preferred_element_type=jnp.float32)

    out_ref[0, 0] = turn(cosine, real) + turn(sine, imag)
    out_ref[1, 0] = turn(cosine, imag) - turn(sine, real)


def fringed(place, order, owned):
    return pl.pallas_call(
        fringe_kernel,
        in_specs=[pl.BlockSpec(memory_space=pltpu.SMEM)] * 2
        + [pl.BlockSpec(memory_space=pltpu.VMEM)] * 5,
        out_specs=pl.BlockSpec(memory_space=pltpu.VMEM),
        out_shape=jax.ShapeDtypeStruct((2, 1, PERIODS, LAGS), jnp.float32),
        compiler_params=pltpu.CompilerParams(vmem_limit_bytes=32 * 2**20),
        name="fringe",
    )(
        place,
        order,
        owned.reshape(PERIODS, QUARTERS, UNITS, 2, LANES),
        *fringe_tables(),
    )


def per_device(spectra, flags, poly_index, delay_model, partner_order):
    plane = ("stn", "unit")
    everyone = ("stn", "quarter", "unit")
    row = lax.axis_index(everyone).astype(jnp.int32)
    place = row.reshape(1)
    chunks = rotated_chunks(spectra, flags, poly_index, delay_model, place)
    arrived = lax.all_to_all(chunks, plane, split_axis=0, concat_axis=0, tiled=True)
    rows = correlated(partner_order, arrived)
    owned = lax.all_to_all(rows, everyone, split_axis=0, concat_axis=0, tiled=True)
    return fringed(place, partner_order, owned)


def solution(mesh):
    finer = Mesh(
        mesh.devices.reshape(STN, QUARTERS, UNITS), ("stn", "quarter", "unit")
    )
    time = ("quarter", "unit")
    return jax.shard_map(
        per_device,
        mesh=finer,
        in_specs=(
            P("stn", None, time, None, None),
            P("stn", None, time, None),
            P("stn", None, time),
            P(),
            P(),
        ),
        out_specs=P(None, ("stn", "quarter", "unit"), None, None),
        check_vma=False,
    )
```

```python
import math

import jax
import jax.numpy as jnp
import ml_dtypes
import numpy as np
from jax import lax
from jax.experimental import pallas as pl
from jax.experimental.pallas import tpu as pltpu
from jax.sharding import Mesh
from jax.sharding import PartitionSpec as P

S = 16
C = 4096
PERIODS = 8
LAGS = 256
SPP = 128
CB = 32
STN = 8
QUARTERS = 4
UNITS = 8
ITEMS = 4
K = 4
NPOLY = 64
SPECTRA = 2 * K
TILES = ITEMS * SPECTRA + 1
LANES = 128
HALF = LAGS // 2
HIGHEST = lax.Precision.HIGHEST
WIDE = LANES // ITEMS
TERMS = WIDE - 1
COSINE = [(-1) ** n * (2 * math.pi) ** (2 * n) / math.factorial(2 * n) for n in range(10)]
SINE = [(-1) ** n * (2 * math.pi) ** (2 * n + 1) / math.factorial(2 * n + 1) for n in range(10)]


def rows_of(shape):
    return lax.broadcasted_iota(jnp.int32, shape, len(shape) - 2)


def lanes_of(shape):
    return lax.broadcasted_iota(jnp.int32, shape, len(shape) - 1)


def turn(delay, index, whole):
    turns = delay * index.astype(jnp.float32) * (1.0 / whole)
    turns = turns - jnp.round(turns)
    square = turns * turns
    cosine = jnp.full_like(square, COSINE[-1])
    for coefficient in COSINE[-2::-1]:
        cosine = cosine * square + coefficient
    sine = jnp.full_like(square, SINE[-1])
    for coefficient in SINE[-2::-1]:
        sine = sine * square + coefficient
    return cosine, sine * turns


def in_hbm(array):
    return pltpu.with_memory_space_constraint(array, pltpu.HBM)


def rotate_kernel(
    place_ref,
    poly_hbm,
    model_hbm,
    flags_hbm,
    x_hbm,
    out_ref,
    poly_ref,
    model_ref,
    flags_ref,
    x_ref,
    turned_re,
    turned_im,
    sems,
):
    small = [
        pltpu.make_async_copy(source, target, sems.at[number])
        for number, (source, target) in enumerate(
            ((poly_hbm, poly_ref), (model_hbm, model_ref), (flags_hbm, flags_ref))
        )
    ]
    for copy in small:
        copy.start()
    fetch = pltpu.make_async_copy(x_hbm, x_ref, sems.at[3])
    fetch.start()
    for copy in small:
        copy.wait()
    row = rows_of((8, LANES))
    lane = lanes_of((8, LANES))
    across = jnp.zeros((8, LANES), jnp.float32)
    down = []
    for p in range(PERIODS):
        column = jnp.zeros((8, LANES), jnp.float32)
        for s in range(2):
            for k in range(K):
                index = poly_ref[s, k, p]
                time = p * SPP + place_ref[0] % (QUARTERS * UNITS) * K + k
                moment = time.astype(jnp.float32) * (1.0 / (PERIODS * SPP))
                delay = (
                    model_ref[0, index]
                    + model_ref[1, index] * moment
                    + model_ref[2, index] * moment * moment
                )
                column = jnp.where(row == s * K + k, delay, column)
                across = jnp.where(lane == p * SPECTRA + s * K + k, delay, across)
        down.append(column)
    fine_cos, fine_sin = zip(*(turn(column, lane, 2 * C) for column in down))
    weight = 1.0 - flags_ref[...].reshape(2 * PERIODS * K, CB).astype(jnp.float32)
    weight = weight.astype(jnp.bfloat16)
    source = rows_of((2 * PERIODS * K, LANES))
    source_s, source_p, source_k = source // (PERIODS * K), source // K % PERIODS, source % K
    target = lanes_of((2 * PERIODS * K, LANES))

    def spread(chosen):
        return lax.dot_general(
            weight,
            chosen.astype(jnp.bfloat16),
            (((0,), (0,)), ((), ())),
            preferred_element_type=jnp.float32,
        )

    spectrum = source_s * K + source_k
    coarse_weight = spread(
        jnp.where(target == source_p * SPECTRA + spectrum, 1.0, 0.0)
    )
    block = rows_of((CB, LANES))
    cosine, sine = turn(jnp.tile(across, (CB // 8, 1)), block, 2 * CB)
    coarse_cos = coarse_weight * cosine
    coarse_sin = coarse_weight * sine
    held = block % ITEMS == lanes_of((CB, LANES)) // (LANES // ITEMS)
    merge = rows_of((UNITS, CB)) == lanes_of((UNITS, CB)) // ITEMS
    merge = jnp.where(merge, 1.0, 0.0).astype(jnp.bfloat16)
    for p in range(PERIODS):
        mark = jnp.where((source_p == p) & (target % SPECTRA == spectrum), 1.0, 0.0)
        sent = jnp.where(held, spread(mark), 0.0).astype(jnp.bfloat16)
        sent = jnp.dot(merge, sent, preferred_element_type=jnp.float32).astype(jnp.bfloat16)
        if p == 0:
            fetch.wait()
        for s in range(2):
            for k in range(K):
                r = s * K + k
                x = x_ref[s, p, k].astype(jnp.float32)
                re = x[0:1].reshape(CB, LANES)
                im = x[1:2].reshape(CB, LANES)
                at = p * SPECTRA + r
                a_cos = jnp.broadcast_to(coarse_cos[:, at : at + 1], (CB, LANES))
                a_sin = jnp.broadcast_to(coarse_sin[:, at : at + 1], (CB, LANES))
                b_cos = jnp.broadcast_to(fine_cos[p][r : r + 1], (CB, LANES))
                b_sin = jnp.broadcast_to(fine_sin[p][r : r + 1], (CB, LANES))
                cosine = a_cos * b_cos - a_sin * b_sin
                sine = a_sin * b_cos + a_cos * b_sin
                turned_re[p % 2, pl.ds(r, CB, stride=SPECTRA), :] = re * cosine + im * sine
                turned_im[p % 2, pl.ds(r, CB, stride=SPECTRA), :] = im * cosine - re * sine
        for q in range(CB):
            at = slice(q * SPECTRA, (q + 1) * SPECTRA)
            both = jnp.concatenate([turned_re[p % 2, at], turned_im[p % 2, at]])
            tile = q % ITEMS * SPECTRA
            out_ref[p * UNITS + q // ITEMS, tile : tile + SPECTRA] = both.astype(
                jnp.bfloat16
            ).reshape(SPECTRA, 2, LANES)
        out_ref[p * UNITS : (p + 1) * UNITS, TILES - 1] = jnp.broadcast_to(
            sent[:, None, :], (UNITS, 2, LANES)
        )


def rotated_chunks(spectra, flags, poly_index, delay_model, place):
    return pl.pallas_call(
        rotate_kernel,
        in_specs=[pl.BlockSpec(memory_space=pltpu.SMEM)]
        + [pl.BlockSpec(memory_space=pltpu.HBM)] * 4,
        out_specs=pl.BlockSpec(memory_space=pltpu.VMEM),
        out_shape=jax.ShapeDtypeStruct((PERIODS * UNITS, TILES, 2, LANES), jnp.bfloat16),
        scratch_shapes=[
            pltpu.SMEM((2, K, PERIODS), jnp.int32),
            pltpu.SMEM((3, NPOLY), jnp.float32),
            pltpu.VMEM((2, PERIODS, K, CB), jnp.int32),
            pltpu.VMEM((2, PERIODS, K, 2, C), jnp.bfloat16),
            pltpu.VMEM((2, CB * SPECTRA, LANES), jnp.float32),
            pltpu.VMEM((2, CB * SPECTRA, LANES), jnp.float32),
            pltpu.SemaphoreType.DMA((4,)),
        ],
        compiler_params=pltpu.CompilerParams(vmem_limit_bytes=32 * 2**20),
        name="rotate",
    )(
        place,
        in_hbm(poly_index.transpose(0, 2, 1)),
        in_hbm(delay_model.T),
        in_hbm(flags),
        in_hbm(spectra),
    )


def group_sums(values, group):
    row = rows_of((8, LANES))
    stage = list(values)
    distance = group // 2
    while distance:
        first = row % (2 * distance) < distance
        if 2 * distance == 8:
            stage = [
                jnp.where(first, stage[i], stage[i + distance])
                + pltpu.roll(jnp.where(first, stage[i + distance], stage[i]), 4, 0)
                for i in range(distance)
            ]
        else:
            stage = [
                jnp.where(first, stage[i], stage[i + distance])
                + jnp.where(
                    first,
                    pltpu.roll(stage[i], 8 - distance, 0),
                    pltpu.roll(stage[i + distance], distance, 0),
                )
                for i in range(distance)
            ]
        distance //= 2
    return stage[0]


PAIRS = [(n, m) for n in range(STN) for m in range(n, STN)]


def three_passes(values, table):
    high = values.astype(jnp.bfloat16)
    low = (values - high.astype(jnp.float32)).astype(jnp.bfloat16)
    return jnp.dot(
        jnp.concatenate([high, low, high], axis=1),
        table,
        preferred_element_type=jnp.float32,
    )


def correlate_kernel(order_ref, y_ref, terms_ref, out_ref, mine_ref, crossed_ref, tiles, place_ref):
    for j in range(S):
        place_ref[order_ref[j]] = j
    row = rows_of((8, LANES))
    lane = lanes_of((8, LANES))
    zero = jnp.zeros((8, LANES), jnp.float32)

    def finish(n, m, item, sums):
        if n == m:
            values = [sums[0] + sums[1], zero]
        else:
            values = [sums[0] + sums[2], sums[0] - sums[1]]
        values += [sums[-3] + sums[-1], sums[-3] - sums[-2]]
        tile = group_sums(values, 4)
        tiles[item, pl.ds(PAIRS.index((n, m)) * 8, 8)] = tile

    weights = [
        y_ref[n, :, TILES - 1].astype(jnp.float32)[:, 0, :] for n in range(STN)
    ]
    swapped = [pltpu.roll(weight, K, 1) for weight in weights]
    counts = []
    for n, m in PAIRS:
        same, other = weights[n] * weights[m], weights[n] * swapped[m]
        counts.append(group_sums([same, zero, other, zero] * 2, 8))
    counts = jnp.concatenate(counts)
    at = rows_of(counts.shape) % 8 // 4
    counts = jnp.where(lanes_of(counts.shape) % WIDE // K == 4 + at, counts, 0.0)
    i, j = rows_of((LANES, LANES)), lanes_of((LANES, LANES))
    last = jnp.where(j == i // WIDE * WIDE + TERMS, 1.0, 0.0)
    counts = jnp.dot(
        counts.astype(jnp.bfloat16),
        last.astype(jnp.bfloat16),
        preferred_element_type=jnp.float32,
    )

    def one_item(item, carry):
        for n in range(STN):
            for u in range(UNITS):
                x = y_ref[n, u, pl.ds(item * SPECTRA, SPECTRA)].reshape(2 * SPECTRA, LANES)
                x = x.astype(jnp.float32)
                re, im = x[:SPECTRA], x[SPECTRA:]
                for part, value in enumerate((re, im)):
                    mine_ref[n, part, u] = value
                    crossed_ref[n, part, u] = pltpu.roll(value, 4, 0)
        for block_n in range(0, STN, 2):
            for block_m in range(block_n - block_n % 2, STN, 2):
                pairs = [
                    (n, m)
                    for n in range(block_n, block_n + 2)
                    for m in range(block_m, block_m + 2)
                    if n <= m
                ]
                sums = {}
                for u in range(UNITS):
                    mine, theirs = {}, {}
                    for n in range(block_n, block_n + 2):
                        re, im = mine_ref[n, 0, u], mine_ref[n, 1, u]
                        mine[n] = re, im, re + im
                    for m in range(block_m, block_m + 2):
                        for number, ref in enumerate((mine_ref, crossed_ref)):
                            re, im = ref[m, 0, u], ref[m, 1, u]
                            theirs[m, number] = re, re + im, im - re
                    for n, m in pairs:
                        re, im, both = mine[n]
                        terms = []
                        for number in range(2):
                            their_re, their_both, their_gap = theirs[m, number]
                            if n == m and not number:
                                terms += [re * re, im * im]
                            else:
                                terms += [both * their_re, re * their_both, im * their_gap]
                        old = sums.get((n, m))
                        sums[n, m] = (
                            terms if old is None else [x + y for x, y in zip(old, terms)]
                        )
                for n, m in pairs:
                    finish(n, m, item, sums[n, m])
        return carry

    lax.fori_loop(0, ITEMS, one_item, 0)
    conjugate = jnp.where(row % 2 == 0, 1.0, -1.0)
    total = counts
    for item in range(ITEMS):
        total = total + three_passes(tiles[item], terms_ref[item])
    for number, (n, m) in enumerate(PAIRS):
        value = total[number * 8 : number * 8 + 8]
        if n == m:
            left = value - value.astype(jnp.bfloat16).astype(jnp.float32)
            left = jnp.where(lane % WIDE == TERMS, 1.0, pltpu.roll(left, 1, 0))
            value = jnp.where(row % 4 == 1, left, value)
        other = (value * conjugate).astype(jnp.bfloat16)
        value = value.astype(jnp.bfloat16)
        for pair in range(4):
            h = pair // 2
            a, b = 2 * n + h, 2 * m + (h if pair % 2 == 0 else 1 - h)
            at = slice(2 * pair, 2 * pair + 2)
            out_ref[a * S + place_ref[b]] = value[at]
            if n != m:
                out_ref[b * S + place_ref[a]] = other[at]


def correlated(order, arrived):
    return pl.pallas_call(
        correlate_kernel,
        in_specs=[
            pl.BlockSpec(memory_space=pltpu.SMEM),
            pl.BlockSpec(memory_space=pltpu.VMEM),
            pl.BlockSpec(memory_space=pltpu.VMEM),
        ],
        out_specs=pl.BlockSpec(memory_space=pltpu.VMEM),
        out_shape=jax.ShapeDtypeStruct((S * S, 2, LANES), jnp.bfloat16),
        scratch_shapes=[
            pltpu.VMEM((STN, 2, UNITS, 8, LANES), jnp.float32),
            pltpu.VMEM((STN, 2, UNITS, 8, LANES), jnp.float32),
            pltpu.VMEM((ITEMS, len(PAIRS) * 8, LANES), jnp.float32),
            pltpu.SMEM((S,), jnp.int32),
        ],
        compiler_params=pltpu.CompilerParams(vmem_limit_bytes=32 * 2**20),
        name="correlate",
    )(order, arrived.reshape(STN, UNITS, TILES, 2, LANES), term_tables())


def split_table(table):
    high = table.astype(np.float32).astype(ml_dtypes.bfloat16)
    low = (table - high.astype(np.float64)).astype(np.float32).astype(ml_dtypes.bfloat16)
    return np.concatenate([high, high, low])


CENTRE = (LANES - 1) / 2


def term_tables():
    x = (np.arange(LANES) - CENTRE) / CENTRE
    table = np.cos(np.arccos(x)[:, None] * np.arange(TERMS))
    placed = np.zeros((ITEMS, LANES, LANES))
    for item in range(ITEMS):
        placed[item, :, item * WIDE : item * WIDE + TERMS] = table
    return np.stack([split_table(each) for each in placed])


def fringe_tables():
    lag = np.arange(1, HALF + 1)
    z = 2.0 * np.pi * CENTRE * lag / C
    points = 2.0 * np.pi * np.arange(256) / 256
    order = np.arange(TERMS)
    bessel = np.cos(
        order[:, None, None] * points - z[:, None] * np.sin(points)
    ).mean(axis=2)
    series = np.where(order == 0, 1, 2)[:, None] * np.array([1, -1j, -1, 1j])[order % 4][:, None] * bessel
    fine = np.zeros((LANES, HALF), np.complex128)
    for item in range(ITEMS):
        turned = np.exp(-2j * np.pi * ((CENTRE + item * LANES) * lag % C) / C)
        fine[item * WIDE : item * WIDE + TERMS] = series * turned
    unit = 2.0 * np.pi * ((np.arange(UNITS)[:, None] * lag) % UNITS) / UNITS
    period = 2.0 * np.pi * ((np.arange(PERIODS)[:, None] * np.arange(PERIODS)) % PERIODS)
    period = period / PERIODS
    factor = 1.0 / math.sqrt(PERIODS * C)
    return [split_table(np.concatenate([fine.real, -fine.imag], axis=1))] + [
        np.ascontiguousarray(table, np.float32)
        for table in (
            np.stack([np.cos(unit), np.sin(unit)]),
            np.stack([np.cos(period), np.sin(period)]) * factor,
            np.eye(HALF)[::-1],
        )
    ]


def fringe_kernel(z_ref, fine_ref, coarse_ref, period_ref, flip_ref, out_ref):
    sums = [
        sum(z_ref[p, quarter].astype(jnp.float32) for quarter in range(QUARTERS))
        for p in range(PERIODS)
    ]
    real = jnp.concatenate([each[:, 0, :] for each in sums])
    imag = jnp.concatenate([each[:, 1, :] for each in sums])
    i, j = rows_of((LANES, LANES)), lanes_of((LANES, LANES))
    spread = jnp.where(i == j // WIDE * WIDE + TERMS, 1.0, 0.0).astype(jnp.bfloat16)
    marks = jnp.concatenate([real, imag])
    marks = jnp.dot(
        jnp.where(lanes_of(marks.shape) % WIDE == TERMS, marks, 0.0).astype(jnp.bfloat16),
        spread,
        preferred_element_type=jnp.float32,
    )
    counts, alone = marks[: PERIODS * UNITS], marks[PERIODS * UNITS :] > 0.5
    real, imag = jnp.where(alone, real + imag, real), jnp.where(alone, 0.0, imag)
    scale = 1.0 / jnp.sqrt(jnp.maximum(counts, 1.0))
    both = three_passes(
        jnp.concatenate([real * scale, imag * scale]), fine_ref[...]
    )
    re, im = both[: PERIODS * UNITS], both[PERIODS * UNITS :]
    parts = [[], [], [], []]
    for p in range(PERIODS):
        sums = [jnp.zeros((8, LANES), jnp.float32)] * 4
        for g in range(1):
            at = slice(p * UNITS, p * UNITS + UNITS)
            re_cos, re_sin = re[at, :HALF], re[at, HALF:]
            im_cos, im_sin = im[at, :HALF], im[at, HALF:]
            cosine = coarse_ref[0, g * 8 : g * 8 + 8, :]
            sine = coarse_ref[1, g * 8 : g * 8 + 8, :]
            plus_re, plus_im = re_cos + im_sin, im_cos - re_sin
            minus_re, minus_im = re_cos - im_sin, im_cos + re_sin
            terms = (
                cosine * minus_re - sine * minus_im,
                cosine * minus_im + sine * minus_re,
                cosine * plus_re + sine * plus_im,
                cosine * plus_im - sine * plus_re,
            )
            sums = [total + term for total, term in zip(sums, terms)]
        for part, total in zip(parts, sums):
            part.append(total)
    minus_re, minus_im, plus_re, plus_im = (group_sums(part, 8) for part in parts)
    reversed_ = jnp.dot(
        jnp.concatenate([minus_re, minus_im]),
        flip_ref[...],
        precision=HIGHEST,
        preferred_element_type=jnp.float32,
    )
    real = jnp.concatenate([reversed_[:8], plus_re], axis=1)
    imag = jnp.concatenate([reversed_[8:], plus_im], axis=1)
    cosine, sine = period_ref[0], period_ref[1]

    def turn(a, b):
        return jnp.dot(a, b, precision=HIGHEST, preferred_element_type=jnp.float32)

    out_ref[0, 0] = turn(cosine, real) + turn(sine, imag)
    out_ref[1, 0] = turn(cosine, imag) - turn(sine, real)


def fringed(owned):
    return pl.pallas_call(
        fringe_kernel,
        in_specs=[pl.BlockSpec(memory_space=pltpu.VMEM)] * 5,
        out_specs=pl.BlockSpec(memory_space=pltpu.VMEM),
        out_shape=jax.ShapeDtypeStruct((2, 1, PERIODS, LAGS), jnp.float32),
        compiler_params=pltpu.CompilerParams(vmem_limit_bytes=32 * 2**20),
        name="fringe",
    )(
        owned.reshape(PERIODS, QUARTERS, UNITS, 2, LANES),
        *fringe_tables(),
    )


def per_device(spectra, flags, poly_index, delay_model, partner_order):
    plane = ("stn", "unit")
    everyone = ("stn", "quarter", "unit")
    row = lax.axis_index(everyone).astype(jnp.int32)
    place = row.reshape(1)
    chunks = rotated_chunks(spectra, flags, poly_index, delay_model, place)
    arrived = lax.all_to_all(chunks, plane, split_axis=0, concat_axis=0, tiled=True)
    rows = correlated(partner_order, arrived)
    owned = lax.all_to_all(rows, everyone, split_axis=0, concat_axis=0, tiled=True)
    return fringed(owned)


def solution(mesh):
    finer = Mesh(
        mesh.devices.reshape(STN, QUARTERS, UNITS), ("stn", "quarter", "unit")
    )
    time = ("quarter", "unit")
    return jax.shard_map(
        per_device,
        mesh=finer,
        in_specs=(
            P("stn", None, time, None, None),
            P("stn", None, time, None),
            P("stn", None, time),
            P(),
            P(),
        ),
        out_specs=P(None, ("stn", "quarter", "unit"), None, None),
        check_vma=False,
    )
```

```python
import math

import jax
import jax.numpy as jnp
import ml_dtypes
import numpy as np
from jax import lax
from jax.experimental import pallas as pl
from jax.experimental.pallas import tpu as pltpu
from jax.sharding import Mesh
from jax.sharding import PartitionSpec as P

S = 16
C = 4096
PERIODS = 8
LAGS = 256
SPP = 128
CB = 32
STN = 8
QUARTERS = 4
UNITS = 8
ITEMS = 4
K = 4
NPOLY = 64
SPECTRA = 2 * K
TILES = ITEMS * SPECTRA + 1
LANES = 128
HALF = LAGS // 2
HIGHEST = lax.Precision.HIGHEST
WIDE = LANES // ITEMS
TERMS = WIDE - 1
COSINE = [(-1) ** n * (2 * math.pi) ** (2 * n) / math.factorial(2 * n) for n in range(10)]
SINE = [(-1) ** n * (2 * math.pi) ** (2 * n + 1) / math.factorial(2 * n + 1) for n in range(10)]


def rows_of(shape):
    return lax.broadcasted_iota(jnp.int32, shape, len(shape) - 2)


def lanes_of(shape):
    return lax.broadcasted_iota(jnp.int32, shape, len(shape) - 1)


def turn(delay, index, whole):
    turns = delay * index.astype(jnp.float32) * (1.0 / whole)
    turns = turns - jnp.round(turns)
    square = turns * turns
    cosine = jnp.full_like(square, COSINE[-1])
    for coefficient in COSINE[-2::-1]:
        cosine = cosine * square + coefficient
    sine = jnp.full_like(square, SINE[-1])
    for coefficient in SINE[-2::-1]:
        sine = sine * square + coefficient
    return cosine, sine * turns


def in_hbm(array):
    return pltpu.with_memory_space_constraint(array, pltpu.HBM)


def rotate_kernel(
    place_ref,
    poly_hbm,
    model_hbm,
    flags_hbm,
    x_hbm,
    out_ref,
    poly_ref,
    model_ref,
    flags_ref,
    x_ref,
    turned_re,
    turned_im,
    sems,
):
    small = [
        pltpu.make_async_copy(source, target, sems.at[number])
        for number, (source, target) in enumerate(
            ((poly_hbm, poly_ref), (model_hbm, model_ref), (flags_hbm, flags_ref))
        )
    ]
    for copy in small:
        copy.start()
    fetch = pltpu.make_async_copy(x_hbm, x_ref, sems.at[3])
    fetch.start()
    for copy in small:
        copy.wait()
    row = rows_of((8, LANES))
    lane = lanes_of((8, LANES))
    across = jnp.zeros((8, LANES), jnp.float32)
    down = []
    for p in range(PERIODS):
        column = jnp.zeros((8, LANES), jnp.float32)
        for s in range(2):
            for k in range(K):
                index = poly_ref[s, k, p]
                time = p * SPP + place_ref[0] % (QUARTERS * UNITS) * K + k
                moment = time.astype(jnp.float32) * (1.0 / (PERIODS * SPP))
                delay = (
                    model_ref[0, index]
                    + model_ref[1, index] * moment
                    + model_ref[2, index] * moment * moment
                )
                column = jnp.where(row == s * K + k, delay, column)
                across = jnp.where(lane == p * SPECTRA + s * K + k, delay, across)
        down.append(column)
    fine_cos, fine_sin = zip(*(turn(column, lane, 2 * C) for column in down))
    weight = 1.0 - flags_ref[...].reshape(2 * PERIODS * K, CB).astype(jnp.float32)
    weight = weight.astype(jnp.bfloat16)
    source = rows_of((2 * PERIODS * K, LANES))
    source_s, source_p, source_k = source // (PERIODS * K), source // K % PERIODS, source % K
    target = lanes_of((2 * PERIODS * K, LANES))

    def spread(chosen):
        return lax.dot_general(
            weight,
            chosen.astype(jnp.bfloat16),
            (((0,), (0,)), ((), ())),
            preferred_element_type=jnp.float32,
        )

    spectrum = source_s * K + source_k
    coarse_weight = spread(
        jnp.where(target == source_p * SPECTRA + spectrum, 1.0, 0.0)
    )
    block = rows_of((CB, LANES))
    cosine, sine = turn(jnp.tile(across, (CB // 8, 1)), block, 2 * CB)
    coarse_cos = coarse_weight * cosine
    coarse_sin = coarse_weight * sine
    held = block % ITEMS == lanes_of((CB, LANES)) // (LANES // ITEMS)
    merge = rows_of((UNITS, CB)) == lanes_of((UNITS, CB)) // ITEMS
    merge = jnp.where(merge, 1.0, 0.0).astype(jnp.bfloat16)
    for p in range(PERIODS):
        mark = jnp.where((source_p == p) & (target % SPECTRA == spectrum), 1.0, 0.0)
        sent = jnp.where(held, spread(mark), 0.0).astype(jnp.bfloat16)
        sent = jnp.dot(merge, sent, preferred_element_type=jnp.float32).astype(jnp.bfloat16)
        if p == 0:
            fetch.wait()
        for s in range(2):
            for k in range(K):
                r = s * K + k
                x = x_ref[s, p, k].astype(jnp.float32)
                re = x[0:1].reshape(CB, LANES)
                im = x[1:2].reshape(CB, LANES)
                at = p * SPECTRA + r
                a_cos = jnp.broadcast_to(coarse_cos[:, at : at + 1], (CB, LANES))
                a_sin = jnp.broadcast_to(coarse_sin[:, at : at + 1], (CB, LANES))
                b_cos = jnp.broadcast_to(fine_cos[p][r : r + 1], (CB, LANES))
                b_sin = jnp.broadcast_to(fine_sin[p][r : r + 1], (CB, LANES))
                cosine = a_cos * b_cos - a_sin * b_sin
                sine = a_sin * b_cos + a_cos * b_sin
                turned_re[p % 2, pl.ds(r, CB, stride=SPECTRA), :] = re * cosine + im * sine
                turned_im[p % 2, pl.ds(r, CB, stride=SPECTRA), :] = im * cosine - re * sine
        for q in range(CB):
            at = slice(q * SPECTRA, (q + 1) * SPECTRA)
            both = jnp.concatenate([turned_re[p % 2, at], turned_im[p % 2, at]])
            tile = q % ITEMS * SPECTRA
            out_ref[p * UNITS + q // ITEMS, tile : tile + SPECTRA] = both.astype(
                jnp.bfloat16
            ).reshape(SPECTRA, 2, LANES)
        out_ref[p * UNITS : (p + 1) * UNITS, TILES - 1] = jnp.broadcast_to(
            sent[:, None, :], (UNITS, 2, LANES)
        )


def rotated_chunks(spectra, flags, poly_index, delay_model, place):
    return pl.pallas_call(
        rotate_kernel,
        in_specs=[pl.BlockSpec(memory_space=pltpu.SMEM)]
        + [pl.BlockSpec(memory_space=pltpu.HBM)] * 4,
        out_specs=pl.BlockSpec(memory_space=pltpu.VMEM),
        out_shape=jax.ShapeDtypeStruct((PERIODS * UNITS, TILES, 2, LANES), jnp.bfloat16),
        scratch_shapes=[
            pltpu.SMEM((2, K, PERIODS), jnp.int32),
            pltpu.SMEM((3, NPOLY), jnp.float32),
            pltpu.VMEM((2, PERIODS, K, CB), jnp.int32),
            pltpu.VMEM((2, PERIODS, K, 2, C), jnp.bfloat16),
            pltpu.VMEM((2, CB * SPECTRA, LANES), jnp.float32),
            pltpu.VMEM((2, CB * SPECTRA, LANES), jnp.float32),
            pltpu.SemaphoreType.DMA((4,)),
        ],
        compiler_params=pltpu.CompilerParams(vmem_limit_bytes=32 * 2**20),
        name="rotate",
    )(
        place,
        in_hbm(poly_index.transpose(0, 2, 1)),
        in_hbm(delay_model.T),
        in_hbm(flags),
        in_hbm(spectra),
    )


def group_sums(values, group):
    row = rows_of((8, LANES))
    stage = list(values)
    distance = group // 2
    while distance:
        first = row % (2 * distance) < distance
        if 2 * distance == 8:
            stage = [
                jnp.where(first, stage[i], stage[i + distance])
                + pltpu.roll(jnp.where(first, stage[i + distance], stage[i]), 4, 0)
                for i in range(distance)
            ]
        else:
            stage = [
                jnp.where(first, stage[i], stage[i + distance])
                + jnp.where(
                    first,
                    pltpu.roll(stage[i], 8 - distance, 0),
                    pltpu.roll(stage[i + distance], distance, 0),
                )
                for i in range(distance)
            ]
        distance //= 2
    return stage[0]


PAIRS = [(n, m) for n in range(STN) for m in range(n, STN)]


def three_passes(values, table):
    high = values.astype(jnp.bfloat16)
    low = (values - high.astype(jnp.float32)).astype(jnp.bfloat16)
    return jnp.dot(
        jnp.concatenate([high, low, high], axis=1),
        table,
        preferred_element_type=jnp.float32,
    )


def correlate_kernel(order_ref, y_ref, terms_ref, out_ref, mine_ref, crossed_ref, tiles, place_ref):
    for j in range(S):
        place_ref[order_ref[j]] = j
    row = rows_of((8, LANES))
    lane = lanes_of((8, LANES))
    zero = jnp.zeros((8, LANES), jnp.float32)

    def finish(n, m, item, sums):
        if n == m:
            values = [sums[0] + sums[1], zero]
        else:
            values = [sums[0] + sums[2], sums[0] - sums[1]]
        values += [sums[-3] + sums[-1], sums[-3] - sums[-2]]
        tile = group_sums(values, 4)
        tiles[item, pl.ds(PAIRS.index((n, m)) * 8, 8)] = tile

    weights = [
        y_ref[n, :, TILES - 1].astype(jnp.float32)[:, 0, :] for n in range(STN)
    ]
    swapped = [pltpu.roll(weight, K, 1) for weight in weights]
    counts = []
    for n, m in PAIRS:
        same, other = weights[n] * weights[m], weights[n] * swapped[m]
        counts.append(group_sums([same, zero, other, zero] * 2, 8))
    counts = jnp.concatenate(counts)
    at = rows_of(counts.shape) % 8 // 4
    counts = jnp.where(lanes_of(counts.shape) % WIDE // K == 4 + at, counts, 0.0)
    i, j = rows_of((LANES, LANES)), lanes_of((LANES, LANES))
    last = jnp.where(j == i // WIDE * WIDE + TERMS, 1.0, 0.0)
    counts = jnp.dot(
        counts.astype(jnp.bfloat16),
        last.astype(jnp.bfloat16),
        preferred_element_type=jnp.float32,
    )

    def one_item(item, carry):
        for n in range(STN):
            for u in range(UNITS):
                x = y_ref[n, u, pl.ds(item * SPECTRA, SPECTRA)].reshape(2 * SPECTRA, LANES)
                x = x.astype(jnp.float32)
                re, im = x[:SPECTRA], x[SPECTRA:]
                for part, value in enumerate((re, im)):
                    mine_ref[n, part, u] = value
                    crossed_ref[n, part, u] = pltpu.roll(value, 4, 0)
        for block_n in range(0, STN, 2):
            for block_m in range(block_n - block_n % 2, STN, 2):
                pairs = [
                    (n, m)
                    for n in range(block_n, block_n + 2)
                    for m in range(block_m, block_m + 2)
                    if n <= m
                ]
                sums = {}
                for u in range(UNITS):
                    mine, theirs = {}, {}
                    for n in range(block_n, block_n + 2):
                        re, im = mine_ref[n, 0, u], mine_ref[n, 1, u]
                        mine[n] = re, im, re + im
                    for m in range(block_m, block_m + 2):
                        for number, ref in enumerate((mine_ref, crossed_ref)):
                            re, im = ref[m, 0, u], ref[m, 1, u]
                            theirs[m, number] = re, re + im, im - re
                    for n, m in pairs:
                        re, im, both = mine[n]
                        terms = []
                        for number in range(2):
                            their_re, their_both, their_gap = theirs[m, number]
                            if n == m and not number:
                                terms += [re * re, im * im]
                            else:
                                terms += [both * their_re, re * their_both, im * their_gap]
                        old = sums.get((n, m))
                        sums[n, m] = (
                            terms if old is None else [x + y for x, y in zip(old, terms)]
                        )
                for n, m in pairs:
                    finish(n, m, item, sums[n, m])
        return carry

    lax.fori_loop(0, ITEMS, one_item, 0)
    conjugate = jnp.where(row % 2 == 0, 1.0, -1.0)
    total = counts + three_passes(
        jnp.concatenate([tiles[item] for item in range(ITEMS)], axis=1), terms_ref[...]
    )
    for number, (n, m) in enumerate(PAIRS):
        value = total[number * 8 : number * 8 + 8]
        if n == m:
            left = value - value.astype(jnp.bfloat16).astype(jnp.float32)
            left = jnp.where(lane % WIDE == TERMS, 1.0, pltpu.roll(left, 1, 0))
            value = jnp.where(row % 4 == 1, left, value)
        other = (value * conjugate).astype(jnp.bfloat16)
        value = value.astype(jnp.bfloat16)
        for pair in range(4):
            h = pair // 2
            a, b = 2 * n + h, 2 * m + (h if pair % 2 == 0 else 1 - h)
            at = slice(2 * pair, 2 * pair + 2)
            out_ref[a * S + place_ref[b]] = value[at]
            if n != m:
                out_ref[b * S + place_ref[a]] = other[at]


def correlated(order, arrived):
    return pl.pallas_call(
        correlate_kernel,
        in_specs=[
            pl.BlockSpec(memory_space=pltpu.SMEM),
            pl.BlockSpec(memory_space=pltpu.VMEM),
            pl.BlockSpec(memory_space=pltpu.VMEM),
        ],
        out_specs=pl.BlockSpec(memory_space=pltpu.VMEM),
        out_shape=jax.ShapeDtypeStruct((S * S, 2, LANES), jnp.bfloat16),
        scratch_shapes=[
            pltpu.VMEM((STN, 2, UNITS, 8, LANES), jnp.float32),
            pltpu.VMEM((STN, 2, UNITS, 8, LANES), jnp.float32),
            pltpu.VMEM((ITEMS, len(PAIRS) * 8, LANES), jnp.float32),
            pltpu.SMEM((S,), jnp.int32),
        ],
        compiler_params=pltpu.CompilerParams(vmem_limit_bytes=32 * 2**20),
        name="correlate",
    )(order, arrived.reshape(STN, UNITS, TILES, 2, LANES), term_tables())


def split_table(table):
    high = table.astype(np.float32).astype(ml_dtypes.bfloat16)
    low = (table - high.astype(np.float64)).astype(np.float32).astype(ml_dtypes.bfloat16)
    return np.concatenate([high, high, low])


CENTRE = (LANES - 1) / 2


def term_tables():
    x = (np.arange(LANES) - CENTRE) / CENTRE
    table = np.cos(np.arccos(x)[:, None] * np.arange(TERMS))
    placed = np.zeros((ITEMS, LANES, LANES))
    for item in range(ITEMS):
        placed[item, :, item * WIDE : item * WIDE + TERMS] = table
    return split_table(placed.reshape(ITEMS * LANES, LANES))


def fringe_tables():
    lag = np.arange(1, HALF + 1)
    z = 2.0 * np.pi * CENTRE * lag / C
    points = 2.0 * np.pi * np.arange(256) / 256
    order = np.arange(TERMS)
    bessel = np.cos(
        order[:, None, None] * points - z[:, None] * np.sin(points)
    ).mean(axis=2)
    series = np.where(order == 0, 1, 2)[:, None] * np.array([1, -1j, -1, 1j])[order % 4][:, None] * bessel
    fine = np.zeros((LANES, HALF), np.complex128)
    for item in range(ITEMS):
        turned = np.exp(-2j * np.pi * ((CENTRE + item * LANES) * lag % C) / C)
        fine[item * WIDE : item * WIDE + TERMS] = series * turned
    unit = 2.0 * np.pi * ((np.arange(UNITS)[:, None] * lag) % UNITS) / UNITS
    period = 2.0 * np.pi * ((np.arange(PERIODS)[:, None] * np.arange(PERIODS)) % PERIODS)
    period = period / PERIODS
    factor = 1.0 / math.sqrt(PERIODS * C)
    return [split_table(np.concatenate([fine.real, -fine.imag], axis=1))] + [
        np.ascontiguousarray(table, np.float32)
        for table in (
            np.stack([np.cos(unit), np.sin(unit)]),
            np.stack([np.cos(period), np.sin(period)]) * factor,
            np.eye(HALF)[::-1],
        )
    ]


def fringe_kernel(z_ref, fine_ref, coarse_ref, period_ref, flip_ref, out_ref):
    sums = [
        sum(z_ref[p, quarter].astype(jnp.float32) for quarter in range(QUARTERS))
        for p in range(PERIODS)
    ]
    real = jnp.concatenate([each[:, 0, :] for each in sums])
    imag = jnp.concatenate([each[:, 1, :] for each in sums])
    i, j = rows_of((LANES, LANES)), lanes_of((LANES, LANES))
    spread = jnp.where(i == j // WIDE * WIDE + TERMS, 1.0, 0.0).astype(jnp.bfloat16)
    marks = jnp.concatenate([real, imag])
    marks = jnp.dot(
        jnp.where(lanes_of(marks.shape) % WIDE == TERMS, marks, 0.0).astype(jnp.bfloat16),
        spread,
        preferred_element_type=jnp.float32,
    )
    counts, alone = marks[: PERIODS * UNITS], marks[PERIODS * UNITS :] > 0.5
    real, imag = jnp.where(alone, real + imag, real), jnp.where(alone, 0.0, imag)
    scale = 1.0 / jnp.sqrt(jnp.maximum(counts, 1.0))
    both = three_passes(
        jnp.concatenate([real * scale, imag * scale]), fine_ref[...]
    )
    re, im = both[: PERIODS * UNITS], both[PERIODS * UNITS :]
    parts = [[], [], [], []]
    for p in range(PERIODS):
        sums = [jnp.zeros((8, LANES), jnp.float32)] * 4
        for g in range(1):
            at = slice(p * UNITS, p * UNITS + UNITS)
            re_cos, re_sin = re[at, :HALF], re[at, HALF:]
            im_cos, im_sin = im[at, :HALF], im[at, HALF:]
            cosine = coarse_ref[0, g * 8 : g * 8 + 8, :]
            sine = coarse_ref[1, g * 8 : g * 8 + 8, :]
            plus_re, plus_im = re_cos + im_sin, im_cos - re_sin
            minus_re, minus_im = re_cos - im_sin, im_cos + re_sin
            terms = (
                cosine * minus_re - sine * minus_im,
                cosine * minus_im + sine * minus_re,
                cosine * plus_re + sine * plus_im,
                cosine * plus_im - sine * plus_re,
            )
            sums = [total + term for total, term in zip(sums, terms)]
        for part, total in zip(parts, sums):
            part.append(total)
    minus_re, minus_im, plus_re, plus_im = (group_sums(part, 8) for part in parts)
    reversed_ = jnp.dot(
        jnp.concatenate([minus_re, minus_im]),
        flip_ref[...],
        precision=HIGHEST,
        preferred_element_type=jnp.float32,
    )
    real = jnp.concatenate([reversed_[:8], plus_re], axis=1)
    imag = jnp.concatenate([reversed_[8:], plus_im], axis=1)
    cosine, sine = period_ref[0], period_ref[1]

    def turn(a, b):
        return jnp.dot(a, b, precision=HIGHEST, preferred_element_type=jnp.float32)

    out_ref[0, 0] = turn(cosine, real) + turn(sine, imag)
    out_ref[1, 0] = turn(cosine, imag) - turn(sine, real)


def fringed(owned):
    return pl.pallas_call(
        fringe_kernel,
        in_specs=[pl.BlockSpec(memory_space=pltpu.VMEM)] * 5,
        out_specs=pl.BlockSpec(memory_space=pltpu.VMEM),
        out_shape=jax.ShapeDtypeStruct((2, 1, PERIODS, LAGS), jnp.float32),
        compiler_params=pltpu.CompilerParams(vmem_limit_bytes=32 * 2**20),
        name="fringe",
    )(
        owned.reshape(PERIODS, QUARTERS, UNITS, 2, LANES),
        *fringe_tables(),
    )


def per_device(spectra, flags, poly_index, delay_model, partner_order):
    plane = ("stn", "unit")
    everyone = ("stn", "quarter", "unit")
    row = lax.axis_index(everyone).astype(jnp.int32)
    place = row.reshape(1)
    chunks = rotated_chunks(spectra, flags, poly_index, delay_model, place)
    arrived = lax.all_to_all(chunks, plane, split_axis=0, concat_axis=0, tiled=True)
    rows = correlated(partner_order, arrived)
    owned = lax.all_to_all(rows, everyone, split_axis=0, concat_axis=0, tiled=True)
    return fringed(owned)


def solution(mesh):
    finer = Mesh(
        mesh.devices.reshape(STN, QUARTERS, UNITS), ("stn", "quarter", "unit")
    )
    time = ("quarter", "unit")
    return jax.shard_map(
        per_device,
        mesh=finer,
        in_specs=(
            P("stn", None, time, None, None),
            P("stn", None, time, None),
            P("stn", None, time),
            P(),
            P(),
        ),
        out_specs=P(None, ("stn", "quarter", "unit"), None, None),
        check_vma=False,
    )
```
